256 devices in a mesh: shot: 4 (over x_hi, core), dom: 64 (over x_lo, z, y).
Axes of the slice: x: 4 (x_hi: 2, x_lo: 2; x = x_hi * 2 + x_lo), y: 4, z: 8, core: 2. Of those that a mesh axis runs over, the one named last changes fastest.
Arguments:
- parked: bfloat16 [4, 4096, 4096], P('shot', 'dom'), may hold values from -6 to 6
- parked_slot: int32 [4, 64, 64], P('shot', 'dom'), may hold values from 0 to 63, as said below
- holder_list: int32 [4, 64, 64], P('shot', 'dom'), may hold values from 0 to 63, as said below
- speed_sq: float32 [512, 128, 128], P('dom'), may hold values from 0.04 to 0.18
- adjoint_next: float32 [4, 512, 128, 128], P('shot', 'dom'), may hold values from -6 to 6
- adjoint_now: float32 [4, 512, 128, 128], P('shot', 'dom'), may hold values from -6 to 6
- wavelet: float32 [4, 3], P('shot'), may hold values from -9 to 9
- src_depth: int32 [4], P('shot'), may hold values from 0 to 511
- src_row: int32 [4], P('shot'), may hold values from 0 to 16383
- rec_depth: int32 [1024], replicated, may hold values from 0 to 511
- rec_row: int32 [1024], replicated, may hold values from 0 to 16383
- residuals: float32 [4, 4, 1024], P('shot'), may hold values from -6 to 6
Outputs:
- gradient: float32 [512, 128, 128], P('dom', 'shot')
- adjoint_late: float32 [4, 512, 128, 128], P('shot', 'dom')
- adjoint_early: float32 [4, 512, 128, 128], P('shot', 'dom')
The draws below stay inside these ranges and needn't reach their ends.
Inputs may be any that keep to these rules, and one draw needn't show every extreme that they name: Each row of parked_slot names every slot of its holder once. Each row of holder_list names every holder slab once.
All inputs are finite; a program needn't handle non-finite values.
Results may differ from the reference program's by a relative error of at most 0.0005.
Values may be sent and summed in bfloat16 or wider, within the bound.
No kernel may reach another device: no remote copies, remote signals or barrier semaphores. Data moves between devices by JAX's collectives and lax.ppermute only.
A program may use at most 64 MiB of HBM per device.

```python
import math
import jax
import jax.numpy as jnp
import numpy as np
from jax import lax

DZ = 8
NX = 128
NY = 128
NREC = 1024
STEPS = 4
SHOTS = 4
NZ = 512
PIECE = 4096
N_DOM = 64


two_pi = 2.0 * math.pi


def shuffle_row(row_key):
    return jax.random.permutation(row_key, N_DOM).astype(jnp.int32)


def owner_layout(key):
    slot_keys = jax.random.split(jax.random.fold_in(key, 101), SHOTS * N_DOM)
    holder_keys = jax.random.split(jax.random.fold_in(key, 102), SHOTS * N_DOM)
    slot_table = jax.vmap(shuffle_row)(slot_keys).reshape(SHOTS, N_DOM, N_DOM)
    holder_table = jax.vmap(shuffle_row)(holder_keys).reshape(SHOTS, N_DOM, N_DOM)
    return (slot_table, holder_table)


def draw_parked_slot(key, part):
    return owner_layout(key)[0]


def draw_holder_list(key, part):
    return owner_layout(key)[1]


def per_shot(values, rank_of):
    return values.reshape((SHOTS,) + (1,) * (rank_of - 1))


def wave_factor(position, period, offset_by):
    phase_idx = jnp.remainder(position + offset_by, period).astype(jnp.float32)
    return jnp.cos(phase_idx * (two_pi / period.astype(jnp.float32)))


def smooth_part(wave_key, depth_at, lateral_x, lateral_y, level_lo, level_hi):
    rank_of = depth_at.ndim
    periods = jax.random.randint(jax.random.fold_in(wave_key, 1), (3, 3, SHOTS), 8, 17).astype(jnp.int32)
    offsets = jax.random.randint(jax.random.fold_in(wave_key, 2), (3, 3, SHOTS), 0, 64).astype(jnp.int32)
    amplitudes = jax.random.uniform(jax.random.fold_in(wave_key, 3), (3, SHOTS), jnp.float32, -0.6, 0.6)
    mean_level = jax.random.uniform(jax.random.fold_in(wave_key, 4), (SHOTS,), jnp.float32, level_lo, level_hi)
    summed = per_shot(mean_level, rank_of)
    for wave_num in range(3):
        factor = per_shot(amplitudes[wave_num], rank_of)
        factor = factor * wave_factor(depth_at, per_shot(periods[wave_num, 0], rank_of), per_shot(offsets[wave_num, 0], rank_of))
        factor = factor * wave_factor(lateral_x, per_shot(periods[wave_num, 1], rank_of), per_shot(offsets[wave_num, 1], rank_of))
        factor = factor * wave_factor(lateral_y, per_shot(periods[wave_num, 2], rank_of), per_shot(offsets[wave_num, 2], rank_of))
        summed = summed + factor
    return summed


def rough_part(rough_key, shape_of, flat_law):
    if flat_law:
        return jax.random.uniform(rough_key, shape_of, jnp.float32, -0.85, 0.85)
    else:
        return 0.5 * jax.random.truncated_normal(rough_key, -3.0, 3.0, shape_of, jnp.float32)


def adjoint_field(key, rough_num, level_lo, level_hi, flat_law):
    depth_at = jnp.arange(NZ, dtype=jnp.int32).reshape(1, NZ, 1, 1)
    lateral_x = jnp.arange(NX, dtype=jnp.int32).reshape(1, 1, NX, 1)
    lateral_y = jnp.arange(NY, dtype=jnp.int32).reshape(1, 1, 1, NY)
    smooth = smooth_part(jax.random.fold_in(key, 41), depth_at, lateral_x, lateral_y, level_lo, level_hi)
    rough = rough_part(jax.random.fold_in(key, rough_num), (SHOTS, NZ, NX, NY), flat_law)
    return (smooth + rough).astype(jnp.float32)


def draw_adjoint_next(key, part):
    return adjoint_field(key, 51, 1.0, 2.0, False)


def draw_adjoint_now(key, part):
    return adjoint_field(key, 52, 1.0, 2.0, False)


def take_rows(field_rows, source_row):
    return jnp.take(field_rows, source_row, axis=0)


def parked_field(key, level_lo, level_hi, flat_law):
    planes = jnp.arange(N_DOM, dtype=jnp.int32)[:, None] * DZ + jnp.arange(DZ, dtype=jnp.int32)[None, :]
    depth_at = planes.reshape(1, N_DOM, 1, DZ, 1, 1)
    lateral_x = jnp.arange(NX, dtype=jnp.int32).reshape(1, 1, 1, 1, NX, 1)
    lateral_y = jnp.arange(NY, dtype=jnp.int32).reshape(1, 1, 1, 1, 1, NY)
    smooth = smooth_part(jax.random.fold_in(key, 42), depth_at, lateral_x, lateral_y, level_lo, level_hi)
    field = smooth + rough_part(jax.random.fold_in(key, 53), (SHOTS, N_DOM, 2, DZ, NX, NY), flat_law)
    field_rows = field.reshape(SHOTS, N_DOM * N_DOM, PIECE)
    slot_table, holder_table = owner_layout(key)
    owner_of_row = jnp.argsort(slot_table, axis=-1).astype(jnp.int32).reshape(SHOTS, N_DOM * N_DOM)
    piece_table = jnp.argsort(holder_table, axis=-1).astype(jnp.int32).reshape(SHOTS, N_DOM * N_DOM)
    holder_of_row = (jnp.arange(N_DOM * N_DOM, dtype=jnp.int32) // N_DOM)[None, :]
    piece_of_row = jnp.take_along_axis(piece_table, owner_of_row * N_DOM + holder_of_row, axis=1)
    source_row = (owner_of_row * N_DOM + piece_of_row).astype(jnp.int32)
    parked_rows = jax.vmap(take_rows)(field_rows, source_row)
    return parked_rows.astype(jnp.bfloat16)


def draw_parked(key, part):
    return parked_field(key, 1.0, 2.0, False)


def place_ends(array, stream_key, low, top_value):
    dims = array.shape
    spot = [jax.random.randint(jax.random.fold_in(stream_key, axis), (), 0, dims[axis]) for axis in range(len(dims))]
    array = array.at[tuple(spot)].set(low)
    longest = dims.index(max(dims))
    spot[longest] = (spot[longest] + 1) % dims[longest]
    return array.at[tuple(spot)].set(top_value)


def steps_of(own_key, dims, cuts, least, high):
    def one(dim, blocks):
        heights = jax.random.uniform(jax.random.fold_in(jax.random.fold_in(own_key, 6), dim), (blocks,), jnp.float32, least / len(cuts), high / len(cuts))
        return jnp.repeat(jnp.exp(heights), dims[dim] // blocks).reshape((-1,) + (1,) * (len(dims) - dim - 1))

    loudness = one(*cuts[0])
    for cut in cuts[1:]:
        loudness = loudness * one(*cut)
    return loudness


def rank_table(count, lean):
    portions = [(1 << 20) // math.isqrt(grade ** lean) + 1 for grade in range(1, count + 1)]
    spread = 1 + sum(portions) // (1 << 30)
    return np.cumsum(np.array([max(1, weight // spread) for weight in portions]))


def ranked_ids(stream_key, extent, count, skew):
    table = rank_table(count, skew)
    pick = jax.random.randint(jax.random.fold_in(stream_key, 1), extent, 0, int(table[count - 1]))
    rank = jnp.searchsorted(jnp.asarray(table, jnp.int32), pick, side="right")
    return jax.random.permutation(jax.random.fold_in(stream_key, 2), count)[rank].astype(jnp.int32)


def scatter_about(rng, shape, spread, reach, shards=(), held_as=jnp.bfloat16):
    loudness = steps_of(rng, shape, shards, -0.22, 0.18) if shards else 1.0
    values = jax.random.normal(rng, shape, jnp.float32) * spread * loudness
    return jnp.minimum(jnp.maximum(values, -reach), reach).astype(held_as)


def setup_inputs(seed: int = 0) -> dict:
    key_list = jax.random.split(jax.random.key(seed), 13)
    return {
        "parked": draw_parked(jax.random.fold_in(key_list[12], 71), 0),
        "parked_slot": draw_parked_slot(jax.random.fold_in(key_list[12], 71), 0),
        "holder_list": draw_holder_list(jax.random.fold_in(key_list[12], 71), 0),
        "speed_sq": jnp.clip(jnp.exp(math.log(0.18) - 1.50407746 * jax.random.uniform(key_list[3], (NZ, NX, NY), jnp.float32) ** steps_of(key_list[3], (NZ, NX, NY), ((0, 64),), -0.2, 0.2)), 0.04, 0.18),
        "adjoint_next": draw_adjoint_next(jax.random.fold_in(key_list[12], 71), 0),
        "adjoint_now": draw_adjoint_now(jax.random.fold_in(key_list[12], 71), 0),
        "wavelet": scatter_about(key_list[6], (SHOTS, STEPS - 1), 3.0, 9.0, ((0, 4),), jnp.float32),
        "src_depth": place_ends(jax.random.randint(key_list[7], (SHOTS,), 0, NZ), jax.random.fold_in(key_list[7], 1), 0, NZ - 1).astype(jnp.int32),
        "src_row": place_ends(jax.random.randint(key_list[8], (SHOTS,), 0, NX * NY), jax.random.fold_in(key_list[8], 1), 0, (NX * NY) - 1).astype(jnp.int32),
        "rec_depth": place_ends(ranked_ids(key_list[9], (NREC,), NZ, 2), jax.random.fold_in(key_list[9], 3), 0, NZ - 1).astype(jnp.int32),
        "rec_row": place_ends(jax.random.randint(key_list[10], (NREC,), 0, NX * NY), jax.random.fold_in(key_list[10], 1), 0, (NX * NY) - 1).astype(jnp.int32),
        "residuals": scatter_about(key_list[11], (SHOTS, STEPS, NREC), 1.0, 6.0, ((0, 4),), jnp.float32),
    }


stencil_coef = (-205.0 / 72.0, 8.0 / 5.0, -1.0 / 5.0, 8.0 / 315.0, -1.0 / 560.0)
grad_scale = 0.0625


def shifted(field, offset, axis_num):
    widths = [(0, 0), (0, 0), (0, 0)]
    widths[axis_num] = (4, 4)
    padded = jnp.pad(field, widths)
    return lax.slice_in_dim(padded, 4 + offset, 4 + offset + field.shape[axis_num], axis=axis_num)


def laplace(field):
    summed = 3.0 * stencil_coef[0] * field
    for offset in range(1, 5):
        neighbours = shifted(field, offset, 0) + shifted(field, -offset, 0)
        neighbours = neighbours + shifted(field, offset, 1) + shifted(field, -offset, 1)
        neighbours = neighbours + shifted(field, offset, 2) + shifted(field, -offset, 2)
        summed = summed + stencil_coef[offset] * neighbours
    return summed


def inject(field, depth_at, row_at, amount):
    flat_index = depth_at * (NX * NY) + row_at
    updated = field.reshape(-1).at[flat_index].add(amount)
    return updated.reshape(field.shape)


def reference(parked, parked_slot, holder_list, speed_sq, adjoint_next, adjoint_now, wavelet, src_depth, src_row, rec_depth, rec_row, residuals):
    owners = jnp.arange(N_DOM, dtype=jnp.int32)
    gradient = jnp.zeros((NZ, NX, NY), jnp.float32)
    late_list = []
    early_list = []
    for shot_index in range(SHOTS):
        holders = holder_list[shot_index]
        slot_ids = parked_slot[shot_index][holders, owners[:, None]]
        row_ids = (holders * N_DOM + slot_ids).astype(jnp.int32)
        pieces = parked[shot_index][row_ids]
        stored = pieces.reshape(N_DOM, 2, DZ, NX, NY).astype(jnp.float32)
        previous = stored[:, 0].reshape(NZ, NX, NY)
        current = stored[:, 1].reshape(NZ, NX, NY)
        forward_laps = []
        for step_num in range(STEPS):
            laplacian = laplace(current)
            forward_laps.append(laplacian)
            if step_num + 1 < STEPS:
                advanced = 2.0 * current - previous + speed_sq * laplacian
                advanced = inject(advanced, src_depth[shot_index:shot_index + 1], src_row[shot_index:shot_index + 1], wavelet[shot_index, step_num:step_num + 1])
                previous, current = current, advanced
        adj_later = adjoint_next[shot_index]
        present = adjoint_now[shot_index]
        summed = jnp.zeros((NZ, NX, NY), jnp.float32)
        for step_num in range(STEPS):
            summed = summed + present * forward_laps[STEPS - 1 - step_num]
            laplacian = laplace(speed_sq * present)
            advanced = 2.0 * present - adj_later + laplacian
            advanced = inject(advanced, rec_depth, rec_row, residuals[shot_index, step_num])
            adj_later, present = present, advanced
        gradient = gradient + grad_scale * summed
        late_list.append(adj_later)
        early_list.append(present)
    return gradient, jnp.stack(late_list), jnp.stack(early_list)
```

```python
import functools

import jax
import jax.numpy as jnp
from jax import lax
from jax.experimental import pallas as pl
from jax.experimental.pallas import tpu as pltpu
from jax.sharding import PartitionSpec as P

stencil_coef = (-205.0 / 72.0, 8.0 / 5.0, -1.0 / 5.0, 8.0 / 315.0, -1.0 / 560.0)
grad_scale = 0.0625

DEPTH = 8
HALF = 4
EXT = DEPTH + 2 * HALF
WIDE = DEPTH + 4 * HALF
NX = 128
NY = 128
PAD = 8
CHUNK = 32
bf16 = jnp.bfloat16
f32 = jnp.float32

VM = pl.BlockSpec(memory_space=pltpu.VMEM)
SM = pl.BlockSpec(memory_space=pltpu.SMEM)


def call(kernel, name, ins, outs, scratch, args, flops=0, nbytes=0, limit=40 << 20):
    return pl.pallas_call(
        kernel,
        name=name,
        out_shape=[jax.ShapeDtypeStruct(s, d) for s, d in outs],
        in_specs=ins,
        out_specs=[VM] * len(outs),
        scratch_shapes=scratch,
        compiler_params=pltpu.CompilerParams(vmem_limit_bytes=limit),
        cost_estimate=pl.CostEstimate(flops=flops, bytes_accessed=nbytes, transcendentals=0),
    )(*args)


def buffer():
    return pltpu.VMEM((WIDE, NX + 2 * PAD, NY), f32)


def edge_weights():
    lane = lax.broadcasted_iota(jnp.int32, (CHUNK, NY), 1)
    left = [jnp.where(lane >= k, stencil_coef[k], 0.0) for k in range(1, HALF + 1)]
    right = [jnp.where(lane < NY - k, stencil_coef[k], 0.0) for k in range(1, HALF + 1)]
    return left, right


def zero_pads(buf):
    zeros = jnp.zeros((WIDE, PAD, NY), f32)
    buf[:, 0:PAD, :] = zeros
    buf[:, PAD + NX : PAD + NX + PAD, :] = zeros


def zero_far(buf):
    zeros = jnp.zeros((HALF, NX, NY), f32)
    buf[0:HALF, PAD : PAD + NX, :] = zeros
    buf[WIDE - HALF : WIDE, PAD : PAD + NX, :] = zeros


def lap_chunk(buf, plane, row, weights):
    left, right = weights
    base = PAD + row
    centre = buf[plane, base : base + CHUNK, :]
    total = (3.0 * stencil_coef[0]) * centre
    for k in range(1, HALF + 1):
        near = buf[plane + k, base : base + CHUNK, :] + buf[plane - k, base : base + CHUNK, :]
        near = near + buf[plane, base + k : base + k + CHUNK, :]
        near = near + buf[plane, base - k : base - k + CHUNK, :]
        total = total + stencil_coef[k] * near
        total = total + pltpu.roll(centre, k, 1) * left[k - 1]
        total = total + pltpu.roll(centre, NY - k, 1) * right[k - 1]
    return total


def sweep(buf, first, count, body):
    weights = edge_weights()

    @pl.loop(first, first + count)
    def _(e):
        for row in range(0, NX, CHUNK):
            body(e, row, lap_chunk(buf, e + HALF, row, weights))


def rows(row):
    return slice(row, row + CHUNK)


def padded(row):
    return slice(PAD + row, PAD + row + CHUNK)


def add_cell(ref, plane, row, column, amount):
    lane = lax.broadcasted_iota(jnp.int32, (1, NY), 1)
    old = ref[plane, pl.ds(row, 1), :]
    ref[plane, pl.ds(row, 1), :] = old + jnp.where(lane == column, amount, 0.0)


def parity():
    return lax.rem(lax.axis_index("dom"), 2)


def by_side(par, first, second, body):
    @pl.when(par == 0)
    def _():
        body(second, first)

    @pl.when(par == 1)
    def _():
        body(first, second)


def gather_kernel(slot_ref, parked_ref, out_ref, held):
    pieces = parked_ref.shape[0]
    row = lax.broadcasted_iota(jnp.int32, (pieces, pieces), 0)
    pick = jnp.where(row == slot_ref[...], 1.0, 0.0).astype(bf16)
    for col in range(32):
        part = lax.dot_general(
            pick,
            parked_ref[:, col * NY : (col + 1) * NY],
            (((0,), (0,)), ((), ())),
            preferred_element_type=f32,
        )
        held[pl.ds(col, pieces, stride=32), :] = part
    out_ref[...] = held[...].reshape(pieces, 32, NY).astype(bf16)


def split(value):
    head = value.astype(bf16)
    return head, (value - head.astype(f32)).astype(bf16)


def adjoint_pack_kernel(now_ref, next_ref, speed_ref, first_ref, second_ref):
    par = parity()
    for out_ref, near in ((first_ref, HALF * (1 - par)), (second_ref, HALF * par)):
        far = HALF - near
        close = near + near // 2
        for n, ref in enumerate((now_ref, next_ref, speed_ref)):
            out_ref[pl.ds(HALF * n, HALF)] = ref[pl.ds(near, HALF)].astype(bf16)
            out_ref[pl.ds(4 * HALF + 2 * n, 2)] = split(ref[pl.ds(close, 2)])[1]
        out_ref[pl.ds(3 * HALF, HALF)] = (now_ref[pl.ds(far, HALF)] * speed_ref[pl.ds(far, HALF)]).astype(bf16)


def inject_kernel(depth_ref, row_ref, amount_ref, out_ref, table):
    top = lax.axis_index("dom") * DEPTH - HALF
    count = depth_ref.shape[1]
    steps = amount_ref.shape[0]
    local = depth_ref[...] - top
    place = row_ref[...]
    across = lax.rem(place, NY)
    key = jnp.where((local >= 0) & (local < EXT), local * NX + place // NY, -1)
    lane_id = lax.broadcasted_iota(jnp.int32, (NY, count), 0)
    hit = lane_id == across
    for k in range(steps):
        amount = amount_ref[k : k + 1, :]
        head = amount.astype(bf16).astype(f32)
        table[0, k * NY : (k + 1) * NY, :] = jnp.where(hit, head, 0.0).astype(bf16)
        table[1, k * NY : (k + 1) * NY, :] = jnp.where(hit, amount - head, 0.0).astype(bf16)
    planes = 2
    cell = lax.broadcasted_iota(jnp.int32, (planes * NX, count), 0)

    @pl.loop(0, EXT // planes)
    def _(group):
        pick = jnp.where(cell + group * (planes * NX) == key, 1.0, 0.0).astype(bf16)
        field = lax.dot_general(
            pick, table[0], (((1,), (1,)), ((), ())), preferred_element_type=f32
        ) + lax.dot_general(pick, table[1], (((1,), (1,)), ((), ())), preferred_element_type=f32)
        for k in range(steps):
            for j in range(planes):
                out_ref[k, group * planes + j] = field[j * NX : (j + 1) * NX, k * NY : (k + 1) * NY]


def correction(buf, near_up, scale):
    for p in range(DEPTH):
        for row in range(0, NX, CHUNK):
            total = None
            for k in range(1, HALF + 1):
                q = p - k if p >= HALF else p + k
                if (p >= HALF) == (q >= HALF):
                    continue
                term = stencil_coef[k] * buf[q + 2 * HALF, padded(row), :]
                total = term if total is None else total + term
            if scale is not None:
                total = total * scale[p + HALF, rows(row), :]
            near_up[p, rows(row), :] = total.astype(bf16)


def send_second(par, near, far, first_ref, second_ref):
    for out_ref, at in ((first_ref, HALF * (1 - par)), (second_ref, HALF * par)):
        out_ref[pl.ds(0, HALF)] = near[pl.ds(at, HALF)]
        out_ref[pl.ds(HALF, HALF)] = far[pl.ds(HALF - at, HALF)]


def adjoint_first_kernel(
    now_ref, next_ref, speed_ref, got_a, got_b, inject_ref,
    first_ref, second_ref, lam3_ref, lam2_ref, speed_ext,
    buf4, buf3, now_ext, next_ext, near, far,
):
    par = parity()
    zero_pads(buf4)
    zero_pads(buf3)
    zero_far(buf3)
    own = slice(HALF, HALF + DEPTH)
    now_ext[own] = now_ref[...]
    next_ext[own] = next_ref[...]
    speed_ext[own] = speed_ref[...]
    buf4[2 * HALF : 2 * HALF + DEPTH, PAD : PAD + NX, :] = now_ref[...] * speed_ref[...]

    def halo(lower, upper):
        for ref, at, close, far_at in (
            (lower, 0, 2, 0),
            (upper, HALF + DEPTH, 0, WIDE - HALF),
        ):
            for n, ext in enumerate((now_ext, next_ext, speed_ext)):
                ext[at : at + HALF] = ref[HALF * n : HALF * n + HALF].astype(f32)
                ext[at + close : at + close + 2] = ext[at + close : at + close + 2] + ref[
                    4 * HALF + 2 * n : 4 * HALF + 2 * n + 2
                ].astype(f32)
            buf4[far_at : far_at + HALF, PAD : PAD + NX, :] = ref[3 * HALF : 4 * HALF].astype(f32)
            buf4[at + HALF : at + 2 * HALF, PAD : PAD + NX, :] = (
                now_ext[at : at + HALF] * speed_ext[at : at + HALF]
            )

    by_side(par, got_a, got_b, halo)

    def to_lam3(e, row, lap):
        lam = 2.0 * now_ext[e, rows(row), :] - next_ext[e, rows(row), :] + lap
        lam = lam + inject_ref[0, e, rows(row), :]
        lam3_ref[e, rows(row), :] = lam
        buf3[e + HALF, padded(row), :] = lam * speed_ext[e, rows(row), :]

    sweep(buf4, 0, EXT, to_lam3)

    def to_lam2(e, row, lap):
        lam = 2.0 * lam3_ref[e, rows(row), :] - now_ext[e, rows(row), :] + lap
        lam2_ref[e, rows(row), :] = lam + inject_ref[1, e, rows(row), :]

    sweep(buf3, 0, EXT, to_lam2)
    correction(buf3, near, None)
    far[...] = (lam2_ref[own] * speed_ext[own]).astype(bf16)
    send_second(par, near, far, first_ref, second_ref)


def second_halo(par, got_a, got_b, field, buf, scale):
    def halo(lower, upper):
        for ref, at, far_at in ((lower, 0, 0), (upper, HALF + DEPTH, WIDE - HALF)):
            field[at : at + HALF] = field[at : at + HALF] + ref[0:HALF].astype(f32)
            buf[far_at : far_at + HALF, PAD : PAD + NX, :] = ref[HALF : 2 * HALF].astype(f32)

    by_side(par, got_a, got_b, halo)
    for e in range(EXT):
        value = field[e]
        buf[e + HALF, PAD : PAD + NX, :] = value if scale is None else value * scale[e]


def adjoint_second_kernel(
    lam3_ref, lam2_ref, speed_ext, got_a, got_b, inject_ref, late_ref, early_ref, buf2, buf1, lam2, lam1
):
    par = parity()
    zero_pads(buf2)
    zero_pads(buf1)
    lam2[...] = lam2_ref[...]
    second_halo(par, got_a, got_b, lam2, buf2, speed_ext)

    def to_lam1(e, row, lap):
        lam = 2.0 * lam2[e, rows(row), :] - lam3_ref[e, rows(row), :] + lap
        lam = lam + inject_ref[2, e, rows(row), :]
        lam1[e, rows(row), :] = lam
        buf1[e + HALF, padded(row), :] = lam * speed_ext[e, rows(row), :]

    sweep(buf2, 0, EXT, to_lam1)
    late_ref[...] = lam1[HALF : HALF + DEPTH]

    def to_lam0(e, row, lap):
        lam = 2.0 * lam1[e, rows(row), :] - lam2[e, rows(row), :] + lap
        early_ref[e - HALF, rows(row), :] = lam + inject_ref[3, e, rows(row), :]

    sweep(buf1, HALF, DEPTH, to_lam0)


def forward_pack_kernel(holder_ref, pieces_ref, first_ref, second_ref):
    par = parity()
    per_plane = NX // 32
    for p in range(DEPTH):
        for j in range(per_plane):
            piece = pieces_ref[holder_ref[0, 0, (DEPTH + p) * per_plane + j]]
            first_ref[HALF + p, 32 * j : 32 * j + 32, :] = piece
            second_ref[HALF + p, 32 * j : 32 * j + 32, :] = piece
    at = HALF * (1 - par)
    for p in range(HALF):
        for j in range(per_plane):
            first_ref[p, 32 * j : 32 * j + 32, :] = pieces_ref[holder_ref[0, 0, (at + p) * per_plane + j]]
            second_ref[p, 32 * j : 32 * j + 32, :] = pieces_ref[
                holder_ref[0, 0, (HALF - at + p) * per_plane + j]
            ]


def source_place(depth_ref, row_ref):
    local = depth_ref[0] - (lax.axis_index("dom") * DEPTH - HALF)
    return local, row_ref[0] // NY, lax.rem(row_ref[0], NY)


def forward_first_kernel(
    depth_ref, row_ref, wave_ref, mine_a, mine_b, got_a, got_b, speed_ext, late_ref, lam2_ref,
    first_ref, second_ref, u1_ref, u2_ref, grad_ref,
    buf0, buf1, prev_ext, near, far,
):
    par = parity()
    zero_pads(buf0)
    zero_pads(buf1)
    zero_far(buf1)
    low = HALF + HALF * (1 - par)
    prev_ext[pl.ds(low, HALF)] = mine_a[0:HALF].astype(f32)
    prev_ext[pl.ds(HALF + HALF * par, HALF)] = mine_b[0:HALF].astype(f32)
    buf0[2 * HALF : 2 * HALF + DEPTH, PAD : PAD + NX, :] = mine_a[HALF : HALF + DEPTH].astype(f32)

    def halo(lower, upper):
        for ref, at, wide_at in ((lower, 0, 0), (upper, HALF + DEPTH, 2 * HALF + DEPTH)):
            prev_ext[at : at + HALF] = ref[0:HALF].astype(f32)
            buf0[wide_at : wide_at + DEPTH, PAD : PAD + NX, :] = ref[HALF : HALF + DEPTH].astype(f32)

    by_side(par, got_a, got_b, halo)

    def to_u1(e, row, lap):
        value = 2.0 * buf0[e + HALF, padded(row), :] - prev_ext[e, rows(row), :]
        value = value + speed_ext[e, rows(row), :] * lap
        u1_ref[e, rows(row), :] = value
        buf1[e + HALF, padded(row), :] = value

        @pl.when((e >= HALF) & (e < HALF + DEPTH))
        def _():
            grad_ref[e - HALF, rows(row), :] = lap * late_ref[e - HALF, rows(row), :]

    sweep(buf0, 0, EXT, to_u1)
    local, across, along = source_place(depth_ref, row_ref)
    inside = (local >= 0) & (local < EXT)

    @pl.when(inside)
    def _():
        add_cell(u1_ref, local, across, along, wave_ref[0, 0])
        add_cell(buf1, local + HALF, across + PAD, along, wave_ref[0, 0])

    def to_u2(e, row, lap):
        value = 2.0 * u1_ref[e, rows(row), :] - buf0[e + HALF, padded(row), :]
        u2_ref[e, rows(row), :] = value + speed_ext[e, rows(row), :] * lap

        @pl.when((e >= HALF) & (e < HALF + DEPTH))
        def _():
            grad_ref[e - HALF, rows(row), :] = (
                grad_ref[e - HALF, rows(row), :] + lap * lam2_ref[e, rows(row), :]
            )

    sweep(buf1, 0, EXT, to_u2)

    @pl.when(inside)
    def _():
        add_cell(u2_ref, local, across, along, wave_ref[0, 1])

    correction(buf1, near, speed_ext)
    far[...] = u2_ref[HALF : HALF + DEPTH].astype(bf16)
    send_second(par, near, far, first_ref, second_ref)


def forward_second_kernel(
    depth_ref, row_ref, wave_ref, got_a, got_b, u1_ref, u2_ref, speed_ext, lam3_ref, lam4_ref, grad_ref,
    keep_ref, send_ref, buf2, buf3, u2, total,
):
    par = parity()
    zero_pads(buf2)
    zero_pads(buf3)
    u2[...] = u2_ref[...]
    second_halo(par, got_a, got_b, u2, buf2, None)

    def to_u3(e, row, lap):
        value = 2.0 * u2[e, rows(row), :] - u1_ref[e, rows(row), :]
        buf3[e + HALF, padded(row), :] = value + speed_ext[e, rows(row), :] * lap

        @pl.when((e >= HALF) & (e < HALF + DEPTH))
        def _():
            total[e - HALF, rows(row), :] = (
                grad_ref[e - HALF, rows(row), :] + lap * lam3_ref[e, rows(row), :]
            )

    sweep(buf2, 0, EXT, to_u3)
    local, across, along = source_place(depth_ref, row_ref)

    @pl.when((local >= 0) & (local < EXT))
    def _():
        add_cell(buf3, local + HALF, across + PAD, along, wave_ref[0, 2])

    def to_gradient(e, row, lap):
        value = total[e - HALF, rows(row), :] + lap * lam4_ref[e - HALF, rows(row), :]
        total[e - HALF, rows(row), :] = grad_scale * value

    sweep(buf3, HALF, DEPTH, to_gradient)
    shot = lax.axis_index("shot")
    pair, core = shot // 2, lax.rem(shot, 2)
    for n, half in enumerate((pair, 1 - pair)):
        keep_at = pl.multiple_of((half * 2 + core) * 32, 32)
        send_at = pl.multiple_of((half * 2 + 1 - core) * 32, 32)
        keep_ref[n] = total[:, pl.ds(keep_at, 32), :]
        send_ref[n] = total[:, pl.ds(send_at, 32), :]


def per_device(
    parked, parked_slot, holder_list, speed_sq, adjoint_next, adjoint_now,
    wavelet, src_depth, src_row, rec_depth, rec_row, residuals,
):
    peers = lax.axis_size("dom")
    even = [(i, i ^ 1) for i in range(peers)]
    odd = [(i, ((i + 1) ^ 1) - 1) for i in range(1, peers - 1)]
    swap = lambda a, b: (lax.ppermute(a, "dom", even), lax.ppermute(b, "dom", odd))
    lam4, lam5 = adjoint_now[0], adjoint_next[0]
    ext = ((EXT, NX, NY), f32)
    slab = ((DEPTH, NX, NY), f32)

    def planes(count):
        return ((count, NX, NY), bf16)

    lap_flops = 60 * EXT * NX * NY

    send_a, send_b = call(
        adjoint_pack_kernel, "adjoint_pack", [VM] * 3, [planes(22)] * 2, [], (lam4, lam5, speed_sq),
        nbytes=3 << 20,
    )
    got_a, got_b = swap(send_a, send_b)
    (outgoing,) = call(
        gather_kernel, "gather", [VM, VM], [((64, 32, NY), bf16)], [pltpu.VMEM((64 * 32, NY), f32)],
        (parked_slot[0], parked[0]), nbytes=1 << 20,
    )
    incoming = lax.all_to_all(outgoing, "dom", split_axis=0, concat_axis=0, tiled=True)
    count = rec_depth.shape[0]
    (inject,) = call(
        inject_kernel, "inject", [VM] * 3, [((4, EXT, NX, NY), f32)],
        [pltpu.VMEM((2, 4 * NY, count), bf16)],
        (rec_depth.reshape(1, count), rec_row.reshape(1, count), residuals[0]),
        flops=4 * EXT * NX * count * 4 * NY, nbytes=4 << 20,
    )
    send_a, send_b, lam3, lam2, speed_ext = call(
        adjoint_first_kernel, "adjoint_first", [VM] * 6, [planes(8)] * 2 + [ext] * 3,
        [buffer(), buffer(), pltpu.VMEM(*ext), pltpu.VMEM(*ext), pltpu.VMEM(*planes(8)), pltpu.VMEM(*planes(8))],
        (lam4, lam5, speed_sq, got_a, got_b, inject), flops=2 * lap_flops, nbytes=10 << 20,
    )
    got_a, got_b = swap(send_a, send_b)
    late, early = call(
        adjoint_second_kernel, "adjoint_second", [VM] * 6, [slab] * 2,
        [buffer(), buffer(), pltpu.VMEM(*ext), pltpu.VMEM(*ext)],
        (lam3, lam2, speed_ext, got_a, got_b, inject), flops=2 * lap_flops, nbytes=10 << 20,
    )

    mine_a, mine_b = call(
        forward_pack_kernel, "forward_pack", [SM, VM], [planes(12)] * 2, [], (holder_list, incoming), nbytes=1 << 20
    )
    got_a, got_b = swap(mine_a, mine_b)
    send_a, send_b, u1, u2, grad = call(
        forward_first_kernel, "forward_first", [SM] * 3 + [VM] * 7, [planes(8)] * 2 + [ext] * 2 + [slab],
        [buffer(), buffer(), pltpu.VMEM(*ext), pltpu.VMEM(*planes(8)), pltpu.VMEM(*planes(8))],
        (src_depth, src_row, wavelet, mine_a, mine_b, got_a, got_b, speed_ext, late, lam2),
        flops=2 * lap_flops, nbytes=8 << 20,
    )
    got_a, got_b = swap(send_a, send_b)
    quarter = ((2, DEPTH, NX // 4, NY), f32)
    keep, send = call(
        forward_second_kernel, "forward_second", [SM] * 3 + [VM] * 8, [quarter] * 2,
        [buffer(), buffer(), pltpu.VMEM(*ext), pltpu.VMEM(*slab)],
        (src_depth, src_row, wavelet, got_a, got_b, u1, u2, speed_ext, lam3, lam4, grad),
        flops=2 * lap_flops, nbytes=6 << 20,
    )
    got = lax.ppermute(send, "shot", [(0, 1), (1, 0), (2, 3), (3, 2)])
    other = lax.ppermute(keep[1] + got[1], "shot", [(0, 2), (2, 0), (1, 3), (3, 1)])
    gradient = keep[0] + got[0] + other
    return (gradient, late[None], early[None])


def solution(mesh):
    in_specs = (
        P("shot", "dom", None),
        P("shot", "dom", None),
        P("shot", "dom", None),
        P("dom", None, None),
        P("shot", "dom", None, None),
        P("shot", "dom", None, None),
        P("shot", None),
        P("shot"),
        P("shot"),
        P(),
        P(),
        P("shot", None, None),
    )
    out_specs = (P("dom", "shot", None), P("shot", "dom", None, None), P("shot", "dom", None, None))
    return jax.shard_map(
        per_device, mesh=mesh, in_specs=in_specs, out_specs=out_specs, check_vma=False
    )
```

```python
import functools

import jax
import jax.numpy as jnp
from jax import lax
from jax.experimental import pallas as pl
from jax.experimental.pallas import tpu as pltpu
from jax.sharding import PartitionSpec as P

stencil_coef = (-205.0 / 72.0, 8.0 / 5.0, -1.0 / 5.0, 8.0 / 315.0, -1.0 / 560.0)
grad_scale = 0.0625

DEPTH = 8
HALF = 4
EXT = DEPTH + 2 * HALF
WIDE = DEPTH + 4 * HALF
NX = 128
NY = 128
PAD = 8
ROWS = NX + 2 * PAD
CHUNK = 32
GROUP = 4
bf16 = jnp.bfloat16
f32 = jnp.float32

VM = pl.BlockSpec(memory_space=pltpu.VMEM)
HB = pl.BlockSpec(memory_space=pltpu.HBM)
SM = pl.BlockSpec(memory_space=pltpu.SMEM)


def call(kernel, name, ins, outs, scratch, args, flops=0, nbytes=0, limit=40 << 20):
    return pl.pallas_call(
        kernel,
        name=name,
        out_shape=[jax.ShapeDtypeStruct(s, d) for s, d in outs],
        in_specs=ins,
        out_specs=[VM] * len(outs),
        scratch_shapes=scratch,
        compiler_params=pltpu.CompilerParams(vmem_limit_bytes=limit),
        cost_estimate=pl.CostEstimate(flops=flops, bytes_accessed=nbytes, transcendentals=0),
    )(*args)


def buffer(planes):
    return pltpu.VMEM((planes, ROWS, NY), f32)


def zero_pads(buf):
    zeros = jnp.zeros((buf.shape[0], PAD, NY), f32)
    buf[:, 0:PAD, :] = zeros
    buf[:, PAD + NX : ROWS, :] = zeros


def band():
    apart = jnp.abs(
        lax.broadcasted_iota(jnp.int32, (NY, NY), 0) - lax.broadcasted_iota(jnp.int32, (NY, NY), 1)
    )
    weights = jnp.zeros((NY, NY), f32)
    for k in range(1, HALF + 1):
        weights = jnp.where(apart == k, 5.0 * stencil_coef[k], weights)
    head = weights.astype(bf16)
    rest = (weights - head.astype(f32)).astype(bf16)
    both = jnp.concatenate([head, rest], axis=1)
    return jnp.concatenate([both, both], axis=0), head


def along(plane, weights):
    both, head = weights
    first = plane.astype(bf16)
    left = plane - first.astype(f32)
    second = left.astype(bf16)
    third = (left - second.astype(f32)).astype(bf16)
    pair = jnp.dot(jnp.concatenate([first, second], axis=1), both, preferred_element_type=f32)
    return 0.2 * (pair[:, :NY] + pair[:, NY:] + jnp.dot(third, head, preferred_element_type=f32))


def rows(row):
    return slice(row, row + CHUNK)


def padded(row):
    return slice(PAD + row, PAD + row + CHUNK)


def group_laps(buf, first, weights, body):
    static = isinstance(first, int)
    parts = [along(buf[first + j, PAD : PAD + NX, :], weights) for j in range(GROUP)]
    for j in range(GROUP):
        at = first + j
        for row in range(0, NX, CHUNK):
            base = PAD + row
            lap = (3.0 * stencil_coef[0]) * buf[at, padded(row), :] + parts[j][row : row + CHUNK]
            for k in range(1, HALF + 1):
                near = buf[at, base + k : base + k + CHUNK, :] + buf[at, base - k : base - k + CHUNK, :]
                for q in (at + k, at - k):
                    if not static or 0 <= q < buf.shape[0]:
                        near = near + buf[q, padded(row), :]
                lap = lap + stencil_coef[k] * near
            body(j, row, lap)


def sweep_own(buf, shift, weights, body):
    @pl.loop(0, DEPTH // GROUP)
    def _(g):
        group_laps(buf, g * GROUP + shift, weights, lambda j, row, lap: body(g * GROUP + j, row, lap))


def sweep_halo(buf, weights, body):
    @pl.loop(0, 2)
    def _(g):
        group_laps(
            buf, HALF + g * (HALF + DEPTH), weights, lambda j, row, lap: body(g * GROUP + j, row, lap)
        )


def sweep_halo_alone(buf, weights, body):
    for g in range(2):
        group_laps(
            buf, g * (HALF + DEPTH), weights, lambda j, row, lap, g=g: body(g * GROUP + j, row, lap)
        )


def ext_of_halo(h):
    return h + DEPTH * (h // HALF) if isinstance(h, int) else jnp.where(h < HALF, h, h + DEPTH)


def add_cell(ref, plane, row, column, amount):
    lane = lax.broadcasted_iota(jnp.int32, (1, NY), 1)
    old = ref[plane, pl.ds(row, 1), :]
    ref[plane, pl.ds(row, 1), :] = old + jnp.where(lane == column, amount, 0.0)


def parity():
    return lax.rem(lax.axis_index("dom"), 2)


def by_side(par, first, second, body):
    @pl.when(par == 0)
    def _():
        body(second, first)

    @pl.when(par == 1)
    def _():
        body(first, second)


def gather_kernel(slot_hbm, parked_hbm, out_ref, held, slot_ref, parked_ref, sems):
    copies = [
        pltpu.make_async_copy(slot_hbm, slot_ref, sems.at[0]),
        pltpu.make_async_copy(parked_hbm, parked_ref, sems.at[1]),
    ]
    for copy in copies:
        copy.start()
    for copy in copies:
        copy.wait()
    pieces = parked_ref.shape[0]
    row = lax.broadcasted_iota(jnp.int32, (pieces, pieces), 0)
    pick = jnp.where(row == slot_ref[...], 1.0, 0.0).astype(bf16)
    for col in range(32):
        part = lax.dot_general(
            pick,
            parked_ref[:, col * NY : (col + 1) * NY],
            (((0,), (0,)), ((), ())),
            preferred_element_type=f32,
        )
        held[pl.ds(col, pieces, stride=32), :] = part
    out_ref[...] = held[...].reshape(pieces, 32, NY).astype(bf16)


def adjoint_pack_kernel(now_hbm, next_hbm, speed_hbm, first_ref, second_ref, now_ref, next_ref, speed_ref, sems):
    fields = (now_ref, next_ref, speed_ref)
    copies = [
        pltpu.make_async_copy(src, dst, sems.at[n])
        for n, (src, dst) in enumerate(zip((now_hbm, next_hbm, speed_hbm), fields))
    ]
    for copy in copies:
        copy.start()
    for copy in copies:
        copy.wait()
    par = parity()
    for out_ref, near in ((first_ref, HALF * (1 - par)), (second_ref, HALF * par)):
        far = HALF - near
        close = near + near // 2
        for n, ref in enumerate(fields):
            out_ref[pl.ds(HALF * n, HALF)] = ref[pl.ds(near, HALF)].astype(bf16)
            value = ref[pl.ds(close, 2)]
            out_ref[pl.ds(4 * HALF + 2 * n, 2)] = (value - value.astype(bf16).astype(f32)).astype(bf16)
        out_ref[pl.ds(3 * HALF, HALF)] = (now_ref[pl.ds(far, HALF)] * speed_ref[pl.ds(far, HALF)]).astype(bf16)


def inject_kernel(depth_ref, row_ref, amount_ref, out_ref, table):
    top = lax.axis_index("dom") * DEPTH - HALF
    count = depth_ref.shape[1]
    steps = amount_ref.shape[0]
    local = depth_ref[...] - top
    place = row_ref[...]
    across = lax.rem(place, NY)
    key = jnp.where((local >= 0) & (local < EXT), local * NX + place // NY, -1)
    lane_id = lax.broadcasted_iota(jnp.int32, (NY, count), 0)
    hit = lane_id == across
    for k in range(steps):
        amount = amount_ref[k : k + 1, :]
        head = amount.astype(bf16).astype(f32)
        table[0, k * NY : (k + 1) * NY, :] = jnp.where(hit, head, 0.0).astype(bf16)
        table[1, k * NY : (k + 1) * NY, :] = jnp.where(hit, amount - head, 0.0).astype(bf16)
    planes = 2
    cell = lax.broadcasted_iota(jnp.int32, (planes * NX, count), 0)

    @pl.loop(0, EXT // planes)
    def _(group):
        pick = jnp.where(cell + group * (planes * NX) == key, 1.0, 0.0).astype(bf16)
        field = lax.dot_general(
            pick, table[0], (((1,), (1,)), ((), ())), preferred_element_type=f32
        ) + lax.dot_general(pick, table[1], (((1,), (1,)), ((), ())), preferred_element_type=f32)
        for k in range(steps):
            for j in range(planes):
                out_ref[k, group * planes + j] = field[j * NX : (j + 1) * NX, k * NY : (k + 1) * NY]


def ordered(kernel):
    def with_mark(depth_ref, row_ref, amount_ref, out_ref, mark_ref, table):
        kernel(depth_ref, row_ref, amount_ref, out_ref, table)
        mark_ref[...] = jnp.zeros(mark_ref.shape, f32)

    return with_mark


def send_second(par, buf, far_ref, speed_ext, scale_far, first_ref, second_ref):
    for p in range(DEPTH):
        out_at = p % HALF
        for row in range(0, NX, CHUNK):
            total = None
            for k in range(1, HALF + 1):
                q = p - k if p >= HALF else p + k
                if (p >= HALF) == (q >= HALF):
                    continue
                term = stencil_coef[k] * buf[q + HALF, padded(row), :]
                total = term if total is None else total + term
            if not scale_far:
                total = total * speed_ext[p + HALF, rows(row), :]
            fresh = far_ref[p, rows(row), :]
            if scale_far:
                fresh = fresh * speed_ext[p + HALF, rows(row), :]
            total = total.astype(bf16)
            fresh = fresh.astype(bf16)
            near_first = par == (0 if p >= HALF else 1)

            @pl.when(near_first)
            def _():
                first_ref[out_at, rows(row), :] = total
                second_ref[HALF + out_at, rows(row), :] = fresh

            @pl.when(jnp.logical_not(near_first))
            def _():
                second_ref[out_at, rows(row), :] = total
                first_ref[HALF + out_at, rows(row), :] = fresh


def adjoint_first_kernel(
    now_ref, next_ref, speed_ref, got_a, got_b, inject_ref,
    first_ref, second_ref, lam3_ref, q3_ref, lam2_ref, base_ref, speed_ext,
    buf4, now_halo, next_halo,
):
    par = parity()
    zero_pads(buf4)
    zero_pads(q3_ref)
    weights = band()
    own = slice(HALF, HALF + DEPTH)
    inner = slice(PAD, PAD + NX)
    speed_ext[own] = speed_ref[...]
    buf4[2 * HALF : 2 * HALF + DEPTH, inner, :] = now_ref[...] * speed_ref[...]

    def halo(lower, upper):
        for ref, at, close, far_at in ((lower, 0, 2, 0), (upper, HALF, 0, WIDE - HALF)):
            ext_at = ext_of_halo(at)
            for n, (held, to) in enumerate(((now_halo, at), (next_halo, at), (speed_ext, ext_at))):
                held[to : to + HALF] = ref[HALF * n : HALF * n + HALF].astype(f32)
                held[to + close : to + close + 2] = held[to + close : to + close + 2] + ref[
                    4 * HALF + 2 * n : 4 * HALF + 2 * n + 2
                ].astype(f32)
            buf4[far_at : far_at + HALF, inner, :] = ref[3 * HALF : 4 * HALF].astype(f32)
            buf4[ext_at + HALF : ext_at + 2 * HALF, inner, :] = (
                now_halo[at : at + HALF] * speed_ext[ext_at : ext_at + HALF]
            )

    by_side(par, got_a, got_b, halo)

    def halo_lam3(h, row, lap):
        e = ext_of_halo(h)
        now = now_halo[h, rows(row), :]
        lam = 2.0 * now - next_halo[h, rows(row), :] + lap + inject_ref[0, e, rows(row), :]
        lam3_ref[e, rows(row), :] = lam
        base_ref[h, rows(row), :] = 2.0 * lam - now + inject_ref[1, e, rows(row), :]
        q3_ref[e, padded(row), :] = lam * speed_ext[e, rows(row), :]

    sweep_halo(buf4, weights, halo_lam3)

    def own_lam3(p, row, lap):
        lam = 2.0 * now_ref[p, rows(row), :] - next_ref[p, rows(row), :] + lap
        lam = lam + inject_ref[0, p + HALF, rows(row), :]
        lam3_ref[p + HALF, rows(row), :] = lam
        q3_ref[p + HALF, padded(row), :] = lam * speed_ext[p + HALF, rows(row), :]

    sweep_own(buf4, 2 * HALF, weights, own_lam3)

    def own_lam2(p, row, lap):
        lam = 2.0 * lam3_ref[p + HALF, rows(row), :] - now_ref[p, rows(row), :] + lap
        lam2_ref[p, rows(row), :] = lam + inject_ref[1, p + HALF, rows(row), :]

    sweep_own(q3_ref, HALF, weights, own_lam2)
    send_second(par, q3_ref, lam2_ref, speed_ext, True, first_ref, second_ref)


def forward_pack_kernel(holder_ref, pieces_ref, order_ref, first_ref, second_ref):
    par = parity()
    per_plane = NX // 32
    for p in range(DEPTH):
        for j in range(per_plane):
            piece = pieces_ref[holder_ref[(DEPTH + p) * per_plane + j]]
            first_ref[HALF + p, 32 * j : 32 * j + 32, :] = piece
            second_ref[HALF + p, 32 * j : 32 * j + 32, :] = piece
    at = HALF * (1 - par)
    for p in range(HALF):
        for j in range(per_plane):
            first_ref[p, 32 * j : 32 * j + 32, :] = pieces_ref[holder_ref[(at + p) * per_plane + j]]
            second_ref[p, 32 * j : 32 * j + 32, :] = pieces_ref[holder_ref[(HALF - at + p) * per_plane + j]]


def source_place(depth_ref, row_ref):
    local = depth_ref[0] - (lax.axis_index("dom") * DEPTH - HALF)
    return local, row_ref[0] // NY, lax.rem(row_ref[0], NY)


def forward_first_kernel(
    depth_ref, row_ref, wave_ref, mine_a, mine_b, got_a, got_b, speed_ext,
    first_ref, second_ref, u1_ref, u2_ref, base_ref, lap0_ref, lap1_ref,
    buf0, prev_ext,
):
    par = parity()
    zero_pads(buf0)
    zero_pads(u1_ref)
    weights = band()
    inner = slice(PAD, PAD + NX)
    prev_ext[pl.ds(HALF + HALF * (1 - par), HALF)] = mine_a[0:HALF].astype(f32)
    prev_ext[pl.ds(HALF + HALF * par, HALF)] = mine_b[0:HALF].astype(f32)
    buf0[2 * HALF : 2 * HALF + DEPTH, inner, :] = mine_a[HALF : HALF + DEPTH].astype(f32)

    def halo(lower, upper):
        for ref, at, wide_at in ((lower, 0, 0), (upper, HALF + DEPTH, 2 * HALF + DEPTH)):
            prev_ext[at : at + HALF] = ref[0:HALF].astype(f32)
            buf0[wide_at : wide_at + DEPTH, inner, :] = ref[HALF : HALF + DEPTH].astype(f32)

    by_side(par, got_a, got_b, halo)

    def step(e, row, lap):
        now = buf0[e + HALF, padded(row), :]
        value = 2.0 * now - prev_ext[e, rows(row), :] + speed_ext[e, rows(row), :] * lap
        u1_ref[e, padded(row), :] = value
        return now

    sweep_halo(buf0, weights, lambda h, row, lap: step(ext_of_halo(h), row, lap))

    def own_u1(p, row, lap):
        step(p + HALF, row, lap)
        lap0_ref[p, rows(row), :] = lap

    sweep_own(buf0, 2 * HALF, weights, own_u1)
    local, across, along_y = source_place(depth_ref, row_ref)

    @pl.when((local >= 0) & (local < EXT))
    def _():
        add_cell(u1_ref, local, across + PAD, along_y, wave_ref[0, 0])

    def own_u2(p, row, lap):
        value = 2.0 * u1_ref[p + HALF, padded(row), :] - buf0[p + 2 * HALF, padded(row), :]
        u2_ref[p, rows(row), :] = value + speed_ext[p + HALF, rows(row), :] * lap
        lap1_ref[p, rows(row), :] = lap

    sweep_own(u1_ref, HALF, weights, own_u2)

    @pl.when((local >= HALF) & (local < HALF + DEPTH))
    def _():
        add_cell(u2_ref, local - HALF, across, along_y, wave_ref[0, 1])

    send_second(par, u1_ref, u2_ref, speed_ext, False, first_ref, second_ref)
    for h in range(2 * HALF):
        e = ext_of_halo(h)
        base_ref[h] = 2.0 * u1_ref[e, inner, :] - buf0[e + HALF, inner, :]


def middle_kernel(
    depth_ref, row_ref, wave_ref, got_a, got_b, inject_ref, lam3_ref, q3_ref, lam2_ref, base_lam_ref, speed_ext,
    u1_ref, base_u_ref, lap0_ref, lap1_ref,
    late_ref, early_ref, u2_ref, grad_ref,
    lam2_halo, lam1, buf2, buf1,
):
    par = parity()
    zero_pads(buf2)
    zero_pads(buf1)
    weights = band()
    inner = slice(PAD, PAD + NX)

    def alone(h, row, lap):
        lam2_halo[h, rows(row), :] = base_lam_ref[h, rows(row), :] + lap

    sweep_halo_alone(q3_ref, weights, alone)

    def halo(lower, upper):
        for ref, at, far_at in ((lower, 0, 0), (upper, HALF, WIDE - HALF)):
            ext_at = ext_of_halo(at)
            value = lam2_halo[at : at + HALF] + ref[0:HALF].astype(f32)
            lam2_halo[at : at + HALF] = value
            buf2[ext_at + HALF : ext_at + 2 * HALF, inner, :] = value * speed_ext[ext_at : ext_at + HALF]
            buf2[far_at : far_at + HALF, inner, :] = ref[HALF : 2 * HALF].astype(f32)

    by_side(par, got_a, got_b, halo)
    buf2[2 * HALF : 2 * HALF + DEPTH, inner, :] = lam2_ref[...] * speed_ext[HALF : HALF + DEPTH]

    def halo_lam1(h, row, lap):
        e = ext_of_halo(h)
        lam = 2.0 * lam2_halo[h, rows(row), :] - lam3_ref[e, rows(row), :] + lap
        lam = lam + inject_ref[2, e, rows(row), :]
        buf1[e, padded(row), :] = lam * speed_ext[e, rows(row), :]

    sweep_halo(buf2, weights, halo_lam1)

    def own_lam1(p, row, lap):
        lam2 = lam2_ref[p, rows(row), :]
        lam = 2.0 * lam2 - lam3_ref[p + HALF, rows(row), :] + lap
        lam = lam + inject_ref[2, p + HALF, rows(row), :]
        late_ref[p, rows(row), :] = lam
        buf1[p + HALF, padded(row), :] = lam * speed_ext[p + HALF, rows(row), :]
        grad_ref[p, rows(row), :] = lam * lap0_ref[p, rows(row), :] + lam2 * lap1_ref[p, rows(row), :]

    sweep_own(buf2, 2 * HALF, weights, own_lam1)

    def own_lam0(p, row, lap):
        lam = 2.0 * late_ref[p, rows(row), :] - lam2_ref[p, rows(row), :] + lap
        early_ref[p, rows(row), :] = lam + inject_ref[3, p + HALF, rows(row), :]

    sweep_own(buf1, HALF, weights, own_lam0)

    def halo_u2(h, row, lap):
        e = ext_of_halo(h)
        u2_ref[h, rows(row), :] = base_u_ref[h, rows(row), :] + speed_ext[e, rows(row), :] * lap

    sweep_halo_alone(u1_ref, weights, halo_u2)
    local, across, along_y = source_place(depth_ref, row_ref)

    @pl.when(((local >= 0) & (local < HALF)) | ((local >= HALF + DEPTH) & (local < EXT)))
    def _():
        add_cell(u2_ref, jnp.where(local < HALF, local, local - DEPTH), across, along_y, wave_ref[0, 1])


def forward_second_kernel(
    depth_ref, row_ref, wave_ref, got_a, got_b, u1_ref, u2_ref, u2_halo_ref, speed_ext, lam3_ref, lam4_ref, grad_ref,
    keep_ref, send_ref, buf2, buf3, total,
):
    par = parity()
    zero_pads(buf2)
    zero_pads(buf3)
    weights = band()
    inner = slice(PAD, PAD + NX)

    def halo(lower, upper):
        for ref, at, far_at in ((lower, 0, 0), (upper, HALF, WIDE - HALF)):
            ext_at = ext_of_halo(at)
            buf2[ext_at + HALF : ext_at + 2 * HALF, inner, :] = u2_halo_ref[at : at + HALF] + ref[0:HALF].astype(f32)
            buf2[far_at : far_at + HALF, inner, :] = ref[HALF : 2 * HALF].astype(f32)

    by_side(par, got_a, got_b, halo)
    buf2[2 * HALF : 2 * HALF + DEPTH, inner, :] = u2_ref[...]

    def step(e, row, lap):
        value = 2.0 * buf2[e + HALF, padded(row), :] - u1_ref[e, padded(row), :]
        buf3[e, padded(row), :] = value + speed_ext[e, rows(row), :] * lap

    sweep_halo(buf2, weights, lambda h, row, lap: step(ext_of_halo(h), row, lap))

    def own_u3(p, row, lap):
        step(p + HALF, row, lap)
        total[p, rows(row), :] = grad_ref[p, rows(row), :] + lap * lam3_ref[p + HALF, rows(row), :]

    sweep_own(buf2, 2 * HALF, weights, own_u3)
    local, across, along_y = source_place(depth_ref, row_ref)

    @pl.when((local >= 0) & (local < EXT))
    def _():
        add_cell(buf3, local, across + PAD, along_y, wave_ref[0, 2])

    def to_gradient(p, row, lap):
        value = total[p, rows(row), :] + lap * lam4_ref[p, rows(row), :]
        total[p, rows(row), :] = grad_scale * value

    sweep_own(buf3, HALF, weights, to_gradient)
    shot = lax.axis_index("shot")
    pair, core = shot // 2, lax.rem(shot, 2)
    for n, half in enumerate((pair, 1 - pair)):
        keep_at = pl.multiple_of((half * 2 + core) * 32, 32)
        send_at = pl.multiple_of((half * 2 + 1 - core) * 32, 32)
        keep_ref[n] = total[:, pl.ds(keep_at, 32), :]
        send_ref[n] = total[:, pl.ds(send_at, 32), :]


def per_device(
    parked, parked_slot, holder_list, speed_sq, adjoint_next, adjoint_now,
    wavelet, src_depth, src_row, rec_depth, rec_row, residuals,
):
    peers = lax.axis_size("dom")
    even = [(i, i ^ 1) for i in range(peers)]
    odd = [(i, ((i + 1) ^ 1) - 1) for i in range(1, peers - 1)]
    swap = lambda a, b: (lax.ppermute(a, "dom", even), lax.ppermute(b, "dom", odd))
    lam4, lam5 = adjoint_now[0], adjoint_next[0]
    ext = ((EXT, NX, NY), f32)
    slab = ((DEPTH, NX, NY), f32)
    wide = ((EXT, ROWS, NY), f32)

    def planes(count):
        return ((count, NX, NY), bf16)

    lap_flops = 60 * EXT * NX * NY

    (outgoing,) = call(
        gather_kernel, "gather", [HB, HB], [((64, 32, NY), bf16)],
        [
            pltpu.VMEM((64 * 32, NY), f32), pltpu.VMEM((1, 64), jnp.int32), pltpu.VMEM((64, 4096), bf16),
            pltpu.SemaphoreType.DMA((2,)),
        ],
        (parked_slot[0], parked[0]), nbytes=1 << 20,
    )
    incoming = lax.all_to_all(outgoing, "dom", split_axis=0, concat_axis=0, tiled=True)
    send_a, send_b = call(
        adjoint_pack_kernel, "adjoint_pack", [HB] * 3, [planes(22)] * 2,
        [pltpu.VMEM(*slab)] * 3 + [pltpu.SemaphoreType.DMA((3,))], (lam4, lam5, speed_sq), nbytes=3 << 20,
    )
    got_a, got_b = swap(send_a, send_b)
    count = rec_depth.shape[0]
    inject, order = call(
        ordered(inject_kernel), "inject", [VM] * 3, [((4, EXT, NX, NY), f32), ((8, NY), f32)],
        [pltpu.VMEM((2, 4 * NY, count), bf16)],
        (rec_depth.reshape(1, count), rec_row.reshape(1, count), residuals[0]),
        flops=4 * EXT * NX * count * 4 * NY, nbytes=4 << 20,
    )
    send_a, send_b, lam3, q3, lam2, base_lam, speed_ext = call(
        adjoint_first_kernel, "adjoint_first", [VM] * 6, [planes(8)] * 2 + [ext, wide, slab, slab, ext],
        [buffer(WIDE), pltpu.VMEM(*slab), pltpu.VMEM(*slab)],
        (lam4, lam5, speed_sq, got_a, got_b, inject), flops=2 * lap_flops, nbytes=10 << 20,
    )
    back_a, back_b = swap(send_a, send_b)

    mine_a, mine_b = call(
        forward_pack_kernel, "forward_pack", [SM, VM, VM], [planes(12)] * 2, [],
        (holder_list.reshape(64), incoming, order), nbytes=1 << 20,
    )
    got_a, got_b = swap(mine_a, mine_b)
    send_a, send_b, u1, u2, base_u, lap0, lap1 = call(
        forward_first_kernel, "forward_first", [SM] * 3 + [VM] * 5,
        [planes(8)] * 2 + [wide, slab, slab, slab, slab],
        [buffer(WIDE), pltpu.VMEM(*ext)],
        (src_depth, src_row, wavelet, mine_a, mine_b, got_a, got_b, speed_ext),
        flops=2 * lap_flops, nbytes=8 << 20,
    )
    got_a, got_b = swap(send_a, send_b)
    late, early, u2_halo, grad = call(
        middle_kernel, "middle", [SM] * 3 + [VM] * 12, [slab] * 4,
        [pltpu.VMEM(*slab), pltpu.VMEM(*slab), buffer(WIDE), buffer(EXT)],
        (
            src_depth, src_row, wavelet, back_a, back_b, inject, lam3, q3, lam2, base_lam, speed_ext,
            u1, base_u, lap0, lap1,
        ),
        flops=3 * lap_flops, nbytes=10 << 20,
    )
    quarter = ((2, DEPTH, NX // 4, NY), f32)
    keep, send = call(
        forward_second_kernel, "forward_second", [SM] * 3 + [VM] * 9, [quarter] * 2,
        [buffer(WIDE), buffer(EXT), pltpu.VMEM(*slab)],
        (src_depth, src_row, wavelet, got_a, got_b, u1, u2, u2_halo, speed_ext, lam3, lam4, grad),
        flops=2 * lap_flops, nbytes=6 << 20,
    )
    got = lax.ppermute(send, "shot", [(0, 1), (1, 0), (2, 3), (3, 2)])
    other = lax.ppermute(keep[1] + got[1], "shot", [(0, 2), (2, 0), (1, 3), (3, 1)])
    gradient = keep[0] + got[0] + other
    return (gradient, late[None], early[None])


def solution(mesh):
    in_specs = (
        P("shot", "dom", None),
        P("shot", "dom", None),
        P("shot", "dom", None),
        P("dom", None, None),
        P("shot", "dom", None, None),
        P("shot", "dom", None, None),
        P("shot", None),
        P("shot"),
        P("shot"),
        P(),
        P(),
        P("shot", None, None),
    )
    out_specs = (P("dom", "shot", None), P("shot", "dom", None, None), P("shot", "dom", None, None))
    return jax.shard_map(
        per_device, mesh=mesh, in_specs=in_specs, out_specs=out_specs, check_vma=False
    )
```

```python
import functools

import jax
import jax.numpy as jnp
from jax import lax
from jax.experimental import pallas as pl
from jax.experimental.pallas import tpu as pltpu
from jax.sharding import PartitionSpec as P

stencil_coef = (-205.0 / 72.0, 8.0 / 5.0, -1.0 / 5.0, 8.0 / 315.0, -1.0 / 560.0)
grad_scale = 0.0625

DEPTH = 8
HALF = 4
EXT = DEPTH + 2 * HALF
WIDE = DEPTH + 4 * HALF
NX = 128
NY = 128
PAD = 8
ROWS = NX + 2 * PAD
CHUNK = 32
GROUP = 4
bf16 = jnp.bfloat16
f32 = jnp.float32

VM = pl.BlockSpec(memory_space=pltpu.VMEM)
SM = pl.BlockSpec(memory_space=pltpu.SMEM)
HB = pl.BlockSpec(memory_space=pltpu.HBM)


def in_hbm(*arrays):
    return tuple(pltpu.with_memory_space_constraint(a, pltpu.HBM) for a in arrays)


def fetch(sources, targets, sems):
    copies = [pltpu.make_async_copy(src, dst, sems.at[n]) for n, (src, dst) in enumerate(zip(sources, targets))]
    for copy in copies:
        copy.start()
    return copies


def call(kernel, name, ins, outs, scratch, args, us=0, limit=20 << 20):
    return pl.pallas_call(
        kernel,
        name=name,
        out_shape=[jax.ShapeDtypeStruct(s, d) for s, d in outs],
        in_specs=ins,
        out_specs=[VM] * len(outs),
        scratch_shapes=scratch,
        compiler_params=pltpu.CompilerParams(vmem_limit_bytes=limit),
        cost_estimate=pl.CostEstimate(flops=us * 10**9, bytes_accessed=us * 3_600_000, transcendentals=0),
    )(*args)


def buffer(planes):
    return pltpu.VMEM((planes, ROWS, NY), f32)


def zero_pads(buf):
    zeros = jnp.zeros((buf.shape[0], PAD, NY), f32)
    buf[:, 0:PAD, :] = zeros
    buf[:, PAD + NX : ROWS, :] = zeros


def band():
    apart = jnp.abs(
        lax.broadcasted_iota(jnp.int32, (NY, NY), 0) - lax.broadcasted_iota(jnp.int32, (NY, NY), 1)
    )
    weights = jnp.zeros((NY, NY), f32)
    for k in range(1, HALF + 1):
        weights = jnp.where(apart == k, 5.0 * stencil_coef[k], weights)
    head = weights.astype(bf16)
    rest = (weights - head.astype(f32)).astype(bf16)
    both = jnp.concatenate([head, rest], axis=1)
    return jnp.concatenate([both, both], axis=0), head


def along(plane, weights):
    both, head = weights
    first = plane.astype(bf16)
    left = plane - first.astype(f32)
    second = left.astype(bf16)
    third = (left - second.astype(f32)).astype(bf16)
    pair = jnp.dot(jnp.concatenate([first, second], axis=1), both, preferred_element_type=f32)
    return 0.2 * (pair[:, :NY] + pair[:, NY:] + jnp.dot(third, head, preferred_element_type=f32))


def rows(row):
    return slice(row, row + CHUNK)


def padded(row):
    return slice(PAD + row, PAD + row + CHUNK)


def group_laps(buf, first, weights, body):
    static = isinstance(first, int)
    parts = [along(buf[first + j, PAD : PAD + NX, :], weights) for j in range(GROUP)]
    for j in range(GROUP):
        at = first + j
        for row in range(0, NX, CHUNK):
            base = PAD + row
            lap = (3.0 * stencil_coef[0]) * buf[at, padded(row), :] + parts[j][row : row + CHUNK]
            for k in range(1, HALF + 1):
                near = buf[at, base + k : base + k + CHUNK, :] + buf[at, base - k : base - k + CHUNK, :]
                for q in (at + k, at - k):
                    if not static or 0 <= q < buf.shape[0]:
                        near = near + buf[q, padded(row), :]
                lap = lap + stencil_coef[k] * near
            body(j, row, lap)


def sweep_own(buf, shift, weights, body):
    @pl.loop(0, DEPTH // GROUP)
    def _(g):
        group_laps(buf, g * GROUP + shift, weights, lambda j, row, lap: body(g * GROUP + j, row, lap))


def sweep_halo(buf, weights, body):
    @pl.loop(0, 2)
    def _(g):
        group_laps(
            buf, HALF + g * (HALF + DEPTH), weights, lambda j, row, lap: body(g * GROUP + j, row, lap)
        )


def sweep_halo_alone(buf, weights, body):
    for g in range(2):
        group_laps(
            buf, g * (HALF + DEPTH), weights, lambda j, row, lap, g=g: body(g * GROUP + j, row, lap)
        )


def ext_of_halo(h):
    return h + DEPTH * (h // HALF) if isinstance(h, int) else jnp.where(h < HALF, h, h + DEPTH)


def add_cell(ref, plane, row, column, amount):
    lane = lax.broadcasted_iota(jnp.int32, (1, NY), 1)
    old = ref[plane, pl.ds(row, 1), :]
    ref[plane, pl.ds(row, 1), :] = old + jnp.where(lane == column, amount, 0.0)


def parity():
    return lax.rem(lax.axis_index("dom"), 2)


def by_side(par, first, second, body):
    @pl.when(par == 0)
    def _():
        body(second, first)

    @pl.when(par == 1)
    def _():
        body(first, second)


def gather_kernel(slot_ref, parked_ref, order_ref, out_ref, held):
    pieces = parked_ref.shape[0]
    row = lax.broadcasted_iota(jnp.int32, (pieces, pieces), 0)
    pick = jnp.where(row == slot_ref[...], 1.0, 0.0).astype(bf16)
    for col in range(32):
        part = lax.dot_general(
            pick,
            parked_ref[:, col * NY : (col + 1) * NY],
            (((0,), (0,)), ((), ())),
            preferred_element_type=f32,
        )
        held[pl.ds(col, pieces, stride=32), :] = part
    out_ref[...] = held[...].reshape(pieces, 32, NY).astype(bf16)


def adjoint_pack_kernel(now_hbm, next_hbm, speed_hbm, first_ref, second_ref, mark_ref, now_ref, next_ref, speed_ref, sems):
    fields = (now_ref, next_ref, speed_ref)
    for copy in fetch((now_hbm, next_hbm, speed_hbm), fields, sems):
        copy.wait()
    mark_ref[...] = jnp.zeros(mark_ref.shape, f32)
    par = parity()
    for out_ref, near in ((first_ref, HALF * (1 - par)), (second_ref, HALF * par)):
        far = HALF - near
        close = near + near // 2
        for n, ref in enumerate(fields):
            out_ref[pl.ds(HALF * n, HALF)] = ref[pl.ds(near, HALF)].astype(bf16)
            value = ref[pl.ds(close, 2)]
            out_ref[pl.ds(4 * HALF + 2 * n, 2)] = (value - value.astype(bf16).astype(f32)).astype(bf16)
        out_ref[pl.ds(3 * HALF, HALF)] = (now_ref[pl.ds(far, HALF)] * speed_ref[pl.ds(far, HALF)]).astype(bf16)


def inject_fields(depth_ref, row_ref, amount_ref, first_step, out_ref, table, last_on_halo):
    top = lax.axis_index("dom") * DEPTH - HALF
    count = depth_ref.shape[1]
    steps = out_ref.shape[0]
    local = depth_ref[...] - top
    place = row_ref[...]
    key = jnp.where((local >= 0) & (local < EXT), local * NX + place // NY, -1)
    hit = lax.broadcasted_iota(jnp.int32, (NY, count), 0) == lax.rem(place, NY)
    for k in range(steps):
        amount = amount_ref[first_step + k : first_step + k + 1, :]
        head = amount.astype(bf16).astype(f32)
        table[0, k * NY : (k + 1) * NY, :] = jnp.where(hit, head, 0.0).astype(bf16)
        table[1, k * NY : (k + 1) * NY, :] = jnp.where(hit, amount - head, 0.0).astype(bf16)
    planes = 2
    cell = lax.broadcasted_iota(jnp.int32, (planes * NX, count), 0)

    def group(g, used):
        pick = jnp.where(cell + g * (planes * NX) == key, 1.0, 0.0).astype(bf16)
        field = jnp.zeros((planes * NX, used * NY), f32)
        for n in range(2):
            field = field + lax.dot_general(
                pick, table[n, : used * NY], (((1,), (1,)), ((), ())), preferred_element_type=f32
            )
        for k in range(used):
            for j in range(planes):
                out_ref[k, g * planes + j] = field[j * NX : (j + 1) * NX, k * NY : (k + 1) * NY]

    if last_on_halo:

        @pl.loop(0, EXT // planes)
        def _(g):
            group(g, steps)
    else:

        @pl.loop(0, DEPTH // planes)
        def _(g):
            group(g + HALF // planes, steps)

        @pl.loop(0, DEPTH // planes)
        def _(h):
            group(jnp.where(h < HALF // planes, h, h + DEPTH // planes), steps - 1)


def send_second(par, buf, far_ref, speed_ext, scale_far, first_ref, second_ref):
    def emit(lower, upper):
        for p in range(DEPTH):
            near_ref, other_ref = (upper, lower) if p >= HALF else (lower, upper)
            for row in range(0, NX, CHUNK):
                total = None
                for k in range(1, HALF + 1):
                    q = p - k if p >= HALF else p + k
                    if (p >= HALF) == (q >= HALF):
                        continue
                    term = stencil_coef[k] * buf[q + HALF, padded(row), :]
                    total = term if total is None else total + term
                fresh = far_ref[p, rows(row), :]
                if scale_far:
                    fresh = fresh * speed_ext[p + HALF, rows(row), :]
                else:
                    total = total * speed_ext[p + HALF, rows(row), :]
                near_ref[p % HALF, rows(row), :] = total.astype(bf16)
                other_ref[HALF + p % HALF, rows(row), :] = fresh.astype(bf16)

    by_side(par, first_ref, second_ref, emit)


def adjoint_first_kernel(
    depth_ref, row_ref, amount_ref, now_hbm, next_hbm, speed_hbm, got_a_hbm, got_b_hbm,
    first_ref, second_ref, lam_ref, speed_ext, mark_ref,
    buf4, q3_ref, now_halo, next_halo, now_ref, next_ref, got_a, got_b, sems, inject_ref, table,
):
    par = parity()
    own = slice(HALF, HALF + DEPTH)
    copies = fetch(
        (now_hbm, next_hbm, speed_hbm, got_a_hbm, got_b_hbm), (now_ref, next_ref, speed_ext.at[own], got_a, got_b), sems
    )
    inject_fields(depth_ref, row_ref, amount_ref, 0, inject_ref, table, True)
    zero_pads(buf4)
    zero_pads(q3_ref)
    weights = band()
    inner = slice(PAD, PAD + NX)
    for copy in copies:
        copy.wait()
    buf4[2 * HALF : 2 * HALF + DEPTH, inner, :] = now_ref[...] * speed_ext[own]

    def halo(lower, upper):
        for ref, at, close, far_at in ((lower, 0, 2, 0), (upper, HALF, 0, WIDE - HALF)):
            ext_at = ext_of_halo(at)
            for n, (held, to) in enumerate(((now_halo, at), (next_halo, at), (speed_ext, ext_at))):
                held[to : to + HALF] = ref[HALF * n : HALF * n + HALF].astype(f32)
                held[to + close : to + close + 2] = held[to + close : to + close + 2] + ref[
                    4 * HALF + 2 * n : 4 * HALF + 2 * n + 2
                ].astype(f32)
            buf4[far_at : far_at + HALF, inner, :] = ref[3 * HALF : 4 * HALF].astype(f32)
            buf4[ext_at + HALF : ext_at + 2 * HALF, inner, :] = (
                now_halo[at : at + HALF] * speed_ext[ext_at : ext_at + HALF]
            )

    by_side(par, got_a, got_b, halo)

    def halo_lam3(h, row, lap):
        e = ext_of_halo(h)
        now = now_halo[h, rows(row), :]
        lam = 2.0 * now - next_halo[h, rows(row), :] + lap + inject_ref[0, e, rows(row), :]
        lam_ref[e, rows(row), :] = lam
        lam_ref[EXT + DEPTH + h, rows(row), :] = 2.0 * lam - now + inject_ref[1, e, rows(row), :]
        q3_ref[e, padded(row), :] = lam * speed_ext[e, rows(row), :]

    sweep_halo(buf4, weights, halo_lam3)

    def own_lam3(p, row, lap):
        lam = 2.0 * now_ref[p, rows(row), :] - next_ref[p, rows(row), :] + lap
        lam = lam + inject_ref[0, p + HALF, rows(row), :]
        lam_ref[p + HALF, rows(row), :] = lam
        q3_ref[p + HALF, padded(row), :] = lam * speed_ext[p + HALF, rows(row), :]

    sweep_own(buf4, 2 * HALF, weights, own_lam3)

    def own_lam2(p, row, lap):
        lam = 2.0 * lam_ref[p + HALF, rows(row), :] - now_ref[p, rows(row), :] + lap
        lam_ref[EXT + p, rows(row), :] = lam + inject_ref[1, p + HALF, rows(row), :]

    sweep_own(q3_ref, HALF, weights, own_lam2)
    send_second(par, q3_ref, lam_ref.at[EXT : EXT + DEPTH], speed_ext, True, first_ref, second_ref)
    mark_ref[...] = jnp.zeros(mark_ref.shape, f32)


def forward_pack_kernel(holder_ref, pieces_ref, order_ref, first_ref, second_ref, mark_ref):
    par = parity()
    mark_ref[...] = jnp.zeros(mark_ref.shape, f32)
    per_plane = NX // 32
    for p in range(DEPTH):
        for j in range(per_plane):
            piece = pieces_ref[holder_ref[(DEPTH + p) * per_plane + j]]
            first_ref[HALF + p, 32 * j : 32 * j + 32, :] = piece
            second_ref[HALF + p, 32 * j : 32 * j + 32, :] = piece
    at = HALF * (1 - par)
    for p in range(HALF):
        for j in range(per_plane):
            first_ref[p, 32 * j : 32 * j + 32, :] = pieces_ref[holder_ref[(at + p) * per_plane + j]]
            second_ref[p, 32 * j : 32 * j + 32, :] = pieces_ref[holder_ref[(HALF - at + p) * per_plane + j]]


def source_place(depth_ref, row_ref):
    local = depth_ref[0] - (lax.axis_index("dom") * DEPTH - HALF)
    return local, row_ref[0] // NY, lax.rem(row_ref[0], NY)


def forward_first_kernel(
    depth_ref, row_ref, wave_ref, mine_a, mine_b, got_a, got_b, speed_ext, order_ref,
    first_ref, second_ref, u1_ref, u2_ref, base_ref, lap0_ref, lap1_ref,
    buf0, prev_ext,
):
    par = parity()
    zero_pads(buf0)
    zero_pads(u1_ref)
    weights = band()
    inner = slice(PAD, PAD + NX)
    prev_ext[pl.ds(HALF + HALF * (1 - par), HALF)] = mine_a[0:HALF].astype(f32)
    prev_ext[pl.ds(HALF + HALF * par, HALF)] = mine_b[0:HALF].astype(f32)
    buf0[2 * HALF : 2 * HALF + DEPTH, inner, :] = mine_a[HALF : HALF + DEPTH].astype(f32)

    def halo(lower, upper):
        for ref, at, wide_at in ((lower, 0, 0), (upper, HALF + DEPTH, 2 * HALF + DEPTH)):
            prev_ext[at : at + HALF] = ref[0:HALF].astype(f32)
            buf0[wide_at : wide_at + DEPTH, inner, :] = ref[HALF : HALF + DEPTH].astype(f32)

    by_side(par, got_a, got_b, halo)

    def step(e, row, lap):
        now = buf0[e + HALF, padded(row), :]
        value = 2.0 * now - prev_ext[e, rows(row), :] + speed_ext[e, rows(row), :] * lap
        u1_ref[e, padded(row), :] = value
        return now

    sweep_halo(buf0, weights, lambda h, row, lap: step(ext_of_halo(h), row, lap))

    def own_u1(p, row, lap):
        step(p + HALF, row, lap)
        lap0_ref[p, rows(row), :] = lap

    sweep_own(buf0, 2 * HALF, weights, own_u1)
    local, across, along_y = source_place(depth_ref, row_ref)

    @pl.when((local >= 0) & (local < EXT))
    def _():
        add_cell(u1_ref, local, across + PAD, along_y, wave_ref[0, 0])

    def own_u2(p, row, lap):
        value = 2.0 * u1_ref[p + HALF, padded(row), :] - buf0[p + 2 * HALF, padded(row), :]
        u2_ref[p, rows(row), :] = value + speed_ext[p + HALF, rows(row), :] * lap
        lap1_ref[p, rows(row), :] = lap

    sweep_own(u1_ref, HALF, weights, own_u2)

    @pl.when((local >= HALF) & (local < HALF + DEPTH))
    def _():
        add_cell(u2_ref, local - HALF, across, along_y, wave_ref[0, 1])

    send_second(par, u1_ref, u2_ref, speed_ext, False, first_ref, second_ref)
    for h in range(2 * HALF):
        e = ext_of_halo(h)
        base_ref[h] = 2.0 * u1_ref[e, inner, :] - buf0[e + HALF, inner, :]


def adjoint_second_kernel(
    depth_ref, row_ref, amount_ref, got_a, got_b, lam_ref, speed_ext, order_ref,
    late_ref, early_ref, mark_ref,
    lam2_halo, buf2, buf1, inject_ref, table,
):
    par = parity()
    mark_ref[...] = jnp.zeros(mark_ref.shape, f32)
    inject_fields(depth_ref, row_ref, amount_ref, 2, inject_ref, table, False)
    zero_pads(buf2)
    zero_pads(buf1)
    weights = band()
    inner = slice(PAD, PAD + NX)
    buf1[:, inner, :] = lam_ref[0:EXT] * speed_ext[...]

    def alone(h, row, lap):
        lam2_halo[h, rows(row), :] = lam_ref[EXT + DEPTH + h, rows(row), :] + lap

    sweep_halo_alone(buf1, weights, alone)

    def halo(lower, upper):
        for ref, at, far_at in ((lower, 0, 0), (upper, HALF, WIDE - HALF)):
            ext_at = ext_of_halo(at)
            value = lam2_halo[at : at + HALF] + ref[0:HALF].astype(f32)
            lam2_halo[at : at + HALF] = value
            buf2[ext_at + HALF : ext_at + 2 * HALF, inner, :] = value * speed_ext[ext_at : ext_at + HALF]
            buf2[far_at : far_at + HALF, inner, :] = ref[HALF : 2 * HALF].astype(f32)

    by_side(par, got_a, got_b, halo)
    buf2[2 * HALF : 2 * HALF + DEPTH, inner, :] = lam_ref[EXT : EXT + DEPTH] * speed_ext[HALF : HALF + DEPTH]

    def halo_lam1(h, row, lap):
        e = ext_of_halo(h)
        lam = 2.0 * lam2_halo[h, rows(row), :] - lam_ref[e, rows(row), :] + lap
        lam = lam + inject_ref[0, e, rows(row), :]
        buf1[e, padded(row), :] = lam * speed_ext[e, rows(row), :]

    sweep_halo(buf2, weights, halo_lam1)

    def own_lam1(p, row, lap):
        lam = 2.0 * lam_ref[EXT + p, rows(row), :] - lam_ref[p + HALF, rows(row), :] + lap
        lam = lam + inject_ref[0, p + HALF, rows(row), :]
        late_ref[p, rows(row), :] = lam
        buf1[p + HALF, padded(row), :] = lam * speed_ext[p + HALF, rows(row), :]

    sweep_own(buf2, 2 * HALF, weights, own_lam1)

    def own_lam0(p, row, lap):
        lam = 2.0 * late_ref[p, rows(row), :] - lam_ref[EXT + p, rows(row), :] + lap
        early_ref[p, rows(row), :] = lam + inject_ref[1, p + HALF, rows(row), :]

    sweep_own(buf1, HALF, weights, own_lam0)


def middle_kernel(
    depth_ref, row_ref, wave_ref, lam_ref, late_ref, speed_ext, u1_ref, base_ref, lap0_ref, lap1_ref,
    u2_ref, grad_ref,
):
    weights = band()
    grad_ref[...] = late_ref[...] * lap0_ref[...] + lam_ref[EXT : EXT + DEPTH] * lap1_ref[...]

    def halo_u2(h, row, lap):
        e = ext_of_halo(h)
        u2_ref[h, rows(row), :] = base_ref[h, rows(row), :] + speed_ext[e, rows(row), :] * lap

    sweep_halo_alone(u1_ref, weights, halo_u2)
    local, across, along_y = source_place(depth_ref, row_ref)

    @pl.when(((local >= 0) & (local < HALF)) | ((local >= HALF + DEPTH) & (local < EXT)))
    def _():
        add_cell(u2_ref, jnp.where(local < HALF, local, local - DEPTH), across, along_y, wave_ref[0, 1])


def forward_second_kernel(
    depth_ref, row_ref, wave_ref, got_a, got_b, u1_ref, u2_ref, u2_halo_ref, speed_ext, lam3_ref, lam4_ref, grad_ref,
    keep_ref, send_ref, buf2, buf3, total,
):
    par = parity()
    zero_pads(buf2)
    zero_pads(buf3)
    weights = band()
    inner = slice(PAD, PAD + NX)

    def halo(lower, upper):
        for ref, at, far_at in ((lower, 0, 0), (upper, HALF, WIDE - HALF)):
            ext_at = ext_of_halo(at)
            buf2[ext_at + HALF : ext_at + 2 * HALF, inner, :] = u2_halo_ref[at : at + HALF] + ref[0:HALF].astype(f32)
            buf2[far_at : far_at + HALF, inner, :] = ref[HALF : 2 * HALF].astype(f32)

    by_side(par, got_a, got_b, halo)
    buf2[2 * HALF : 2 * HALF + DEPTH, inner, :] = u2_ref[...]

    def step(e, row, lap):
        value = 2.0 * buf2[e + HALF, padded(row), :] - u1_ref[e, padded(row), :]
        buf3[e, padded(row), :] = value + speed_ext[e, rows(row), :] * lap

    sweep_halo(buf2, weights, lambda h, row, lap: step(ext_of_halo(h), row, lap))

    def own_u3(p, row, lap):
        step(p + HALF, row, lap)
        total[p, rows(row), :] = grad_ref[p, rows(row), :] + lap * lam3_ref[p + HALF, rows(row), :]

    sweep_own(buf2, 2 * HALF, weights, own_u3)
    local, across, along_y = source_place(depth_ref, row_ref)

    @pl.when((local >= 0) & (local < EXT))
    def _():
        add_cell(buf3, local, across + PAD, along_y, wave_ref[0, 2])

    def to_gradient(p, row, lap):
        value = total[p, rows(row), :] + lap * lam4_ref[p, rows(row), :]
        total[p, rows(row), :] = grad_scale * value

    sweep_own(buf3, HALF, weights, to_gradient)
    shot = lax.axis_index("shot")
    pair, core = shot // 2, lax.rem(shot, 2)
    for n, half in enumerate((pair, 1 - pair)):
        keep_at = pl.multiple_of((half * 2 + core) * 32, 32)
        send_at = pl.multiple_of((half * 2 + 1 - core) * 32, 32)
        keep_ref[n] = total[:, pl.ds(keep_at, 32), :]
        send_ref[n] = total[:, pl.ds(send_at, 32), :]


def per_device(
    parked, parked_slot, holder_list, speed_sq, adjoint_next, adjoint_now,
    wavelet, src_depth, src_row, rec_depth, rec_row, residuals,
):
    peers = lax.axis_size("dom")
    even = [(i, i ^ 1) for i in range(peers)]
    odd = [(i, ((i + 1) ^ 1) - 1) for i in range(1, peers - 1)]
    swap = lambda a, b: (lax.ppermute(a, "dom", even), lax.ppermute(b, "dom", odd))
    lam4, lam5 = adjoint_now[0], adjoint_next[0]
    ext = ((EXT, NX, NY), f32)
    slab = ((DEPTH, NX, NY), f32)
    wide = ((EXT, ROWS, NY), f32)

    def planes(count):
        return ((count, NX, NY), bf16)

    mark = ((8, NY), f32)
    lam23_shape = (EXT + 2 * DEPTH, NX, NY)
    send_a, send_b, order = call(
        adjoint_pack_kernel, "adjoint_pack", [HB] * 3, [planes(22)] * 2 + [mark],
        [pltpu.VMEM(*slab)] * 3 + [pltpu.SemaphoreType.DMA((3,))], in_hbm(lam4, lam5, speed_sq),
    )
    got_a, got_b = swap(send_a, send_b)
    (outgoing,) = call(
        gather_kernel, "gather", [VM] * 3, [((64, 32, NY), bf16)], [pltpu.VMEM((64 * 32, NY), f32)],
        (parked_slot[0], parked[0], order),
    )
    incoming = lax.all_to_all(outgoing, "dom", split_axis=0, concat_axis=0, tiled=True)
    count = rec_depth.shape[0]
    receivers = (rec_depth.reshape(1, count), rec_row.reshape(1, count), residuals[0])
    fields = [pltpu.VMEM((2, EXT, NX, NY), f32), pltpu.VMEM((2, 2 * NY, count), bf16)]
    send_a, send_b, lam23, speed_ext, order = call(
        adjoint_first_kernel, "adjoint_first", [VM] * 3 + [HB] * 5, [planes(8)] * 2 + [(lam23_shape, f32), ext, mark],
        [buffer(WIDE), buffer(EXT)] + [pltpu.VMEM(*slab)] * 4 + [pltpu.VMEM(*planes(22))] * 2
        + [pltpu.SemaphoreType.DMA((5,))] + fields,
        receivers + in_hbm(lam4, lam5, speed_sq, got_a, got_b), us=4,
    )
    back_a, back_b = swap(send_a, send_b)

    mine_a, mine_b, order = call(
        forward_pack_kernel, "forward_pack", [SM, VM, VM], [planes(12)] * 2 + [mark], [],
        (holder_list.reshape(64), incoming, order), us=4,
    )
    got_a, got_b = swap(mine_a, mine_b)
    late, early, order = call(
        adjoint_second_kernel, "adjoint_second", [VM] * 8, [slab] * 2 + [mark],
        [pltpu.VMEM(*slab), buffer(WIDE), buffer(EXT)] + fields,
        receivers + (back_a, back_b, lam23, speed_ext, order), us=4,
    )
    send_a, send_b, u1, u2, base_u, lap0, lap1 = call(
        forward_first_kernel, "forward_first", [SM] * 3 + [VM] * 6,
        [planes(8)] * 2 + [wide, slab, slab, slab, slab],
        [buffer(WIDE), pltpu.VMEM(*ext)],
        (src_depth, src_row, wavelet, mine_a, mine_b, got_a, got_b, speed_ext, order),
        us=4,
    )
    got_a, got_b = swap(send_a, send_b)
    u2_halo, grad = call(
        middle_kernel, "middle", [SM] * 3 + [VM] * 7, [slab] * 2, [],
        (src_depth, src_row, wavelet, lam23, late, speed_ext, u1, base_u, lap0, lap1),
        us=0,
    )
    quarter = ((2, DEPTH, NX // 4, NY), f32)
    keep, send = call(
        forward_second_kernel, "forward_second", [SM] * 3 + [VM] * 9, [quarter] * 2,
        [buffer(WIDE), buffer(EXT), pltpu.VMEM(*slab)],
        (src_depth, src_row, wavelet, got_a, got_b, u1, u2, u2_halo, speed_ext, lam23, lam4, grad),
        us=0,
    )
    got = lax.ppermute(send, "shot", [(0, 1), (1, 0), (2, 3), (3, 2)])
    other = lax.ppermute(keep[1] + got[1], "shot", [(0, 2), (2, 0), (1, 3), (3, 1)])
    gradient = keep[0] + got[0] + other
    return (gradient, late[None], early[None])


def solution(mesh):
    in_specs = (
        P("shot", "dom", None),
        P("shot", "dom", None),
        P("shot", "dom", None),
        P("dom", None, None),
        P("shot", "dom", None, None),
        P("shot", "dom", None, None),
        P("shot", None),
        P("shot"),
        P("shot"),
        P(),
        P(),
        P("shot", None, None),
    )
    out_specs = (P("dom", "shot", None), P("shot", "dom", None, None), P("shot", "dom", None, None))
    return jax.shard_map(
        per_device, mesh=mesh, in_specs=in_specs, out_specs=out_specs, check_vma=False
    )
```

```python
import functools

import jax
import jax.numpy as jnp
from jax import lax
from jax.experimental import pallas as pl
from jax.experimental.pallas import tpu as pltpu
from jax.sharding import PartitionSpec as P

stencil_coef = (-205.0 / 72.0, 8.0 / 5.0, -1.0 / 5.0, 8.0 / 315.0, -1.0 / 560.0)
grad_scale = 0.0625

DEPTH = 8
HALF = 4
EXT = DEPTH + 2 * HALF
WIDE = DEPTH + 4 * HALF
NX = 128
NY = 128
PAD = 8
ROWS = NX + 2 * PAD
CHUNK = 32
GROUP = 4
bf16 = jnp.bfloat16
f32 = jnp.float32

VM = pl.BlockSpec(memory_space=pltpu.VMEM)
SM = pl.BlockSpec(memory_space=pltpu.SMEM)
HB = pl.BlockSpec(memory_space=pltpu.HBM)


def in_hbm(*arrays):
    return tuple(pltpu.with_memory_space_constraint(a, pltpu.HBM) for a in arrays)


def fetch(sources, targets, sems):
    copies = [pltpu.make_async_copy(src, dst, sems.at[n]) for n, (src, dst) in enumerate(zip(sources, targets))]
    for copy in copies:
        copy.start()
    return copies


def call(kernel, name, ins, outs, scratch, args, us=2, limit=20 << 20):
    return pl.pallas_call(
        kernel,
        name=name,
        out_shape=[pltpu.HBM(*o) if name == "inject" else jax.ShapeDtypeStruct(*o) for o in outs],
        in_specs=ins,
        out_specs=[HB if name == "inject" else VM] * len(outs),
        scratch_shapes=scratch,
        compiler_params=pltpu.CompilerParams(vmem_limit_bytes=limit),
        cost_estimate=pl.CostEstimate(flops=us * 10**9, bytes_accessed=us * 3_600_000, transcendentals=0),
    )(*args)


def buffer(planes):
    return pltpu.VMEM((planes, ROWS, NY), f32)


def zero_pads(buf):
    zeros = jnp.zeros((buf.shape[0], PAD, NY), f32)
    buf[:, 0:PAD, :] = zeros
    buf[:, PAD + NX : ROWS, :] = zeros


def band():
    apart = jnp.abs(
        lax.broadcasted_iota(jnp.int32, (NY, NY), 0) - lax.broadcasted_iota(jnp.int32, (NY, NY), 1)
    )
    weights = jnp.zeros((NY, NY), f32)
    for k in range(1, HALF + 1):
        weights = jnp.where(apart == k, 5.0 * stencil_coef[k], weights)
    head = weights.astype(bf16)
    rest = (weights - head.astype(f32)).astype(bf16)
    both = jnp.concatenate([head, rest], axis=1)
    return jnp.concatenate([both, both], axis=0), head


def along(plane, weights):
    both, head = weights
    first = plane.astype(bf16)
    left = plane - first.astype(f32)
    second = left.astype(bf16)
    third = (left - second.astype(f32)).astype(bf16)
    pair = jnp.dot(jnp.concatenate([first, second], axis=1), both, preferred_element_type=f32)
    return 0.2 * (pair[:, :NY] + pair[:, NY:] + jnp.dot(third, head, preferred_element_type=f32))


def rows(row):
    return slice(row, row + CHUNK)


def padded(row):
    return slice(PAD + row, PAD + row + CHUNK)


def group_laps(buf, first, weights, body):
    static = isinstance(first, int)
    parts = [along(buf[first + j, PAD : PAD + NX, :], weights) for j in range(GROUP)]
    for j in range(GROUP):
        at = first + j
        for row in range(0, NX, CHUNK):
            base = PAD + row
            lap = (3.0 * stencil_coef[0]) * buf[at, padded(row), :] + parts[j][row : row + CHUNK]
            for k in range(1, HALF + 1):
                near = buf[at, base + k : base + k + CHUNK, :] + buf[at, base - k : base - k + CHUNK, :]
                for q in (at + k, at - k):
                    if not static or 0 <= q < buf.shape[0]:
                        near = near + buf[q, padded(row), :]
                lap = lap + stencil_coef[k] * near
            body(j, row, lap)


def sweep_own(buf, shift, weights, body):
    @pl.loop(0, DEPTH // GROUP)
    def _(g):
        group_laps(buf, g * GROUP + shift, weights, lambda j, row, lap: body(g * GROUP + j, row, lap))


def sweep_halo(buf, weights, body):
    @pl.loop(0, 2)
    def _(g):
        group_laps(
            buf, HALF + g * (HALF + DEPTH), weights, lambda j, row, lap: body(g * GROUP + j, row, lap)
        )


def sweep_halo_alone(buf, weights, body):
    for g in range(2):
        group_laps(
            buf, g * (HALF + DEPTH), weights, lambda j, row, lap, g=g: body(g * GROUP + j, row, lap)
        )


def ext_of_halo(h):
    return h + DEPTH * (h // HALF) if isinstance(h, int) else jnp.where(h < HALF, h, h + DEPTH)


def add_cell(ref, plane, row, column, amount):
    lane = lax.broadcasted_iota(jnp.int32, (1, NY), 1)
    old = ref[plane, pl.ds(row, 1), :]
    ref[plane, pl.ds(row, 1), :] = old + jnp.where(lane == column, amount, 0.0)


def parity():
    return lax.rem(lax.axis_index("dom"), 2)


def by_side(par, first, second, body):
    @pl.when(par == 0)
    def _():
        body(second, first)

    @pl.when(par == 1)
    def _():
        body(first, second)


def gather_kernel(slot_hbm, parked_hbm, out_ref, held, slot_ref, parked_ref, sems):
    for copy in fetch((slot_hbm, parked_hbm), (slot_ref, parked_ref), sems):
        copy.wait()
    pieces = parked_ref.shape[0]
    row = lax.broadcasted_iota(jnp.int32, (pieces, pieces), 0)
    pick = jnp.where(row == slot_ref[...], 1.0, 0.0).astype(bf16)
    for col in range(32):
        part = lax.dot_general(
            pick,
            parked_ref[:, col * NY : (col + 1) * NY],
            (((0,), (0,)), ((), ())),
            preferred_element_type=f32,
        )
        held[pl.ds(col, pieces, stride=32), :] = part
    out_ref[...] = held[...].reshape(pieces, 32, NY).astype(bf16)


def adjoint_pack_kernel(now_hbm, next_hbm, speed_hbm, first_ref, second_ref, now_ref, next_ref, speed_ref, sems):
    fields = (now_ref, next_ref, speed_ref)
    for copy in fetch((now_hbm, next_hbm, speed_hbm), fields, sems):
        copy.wait()
    par = parity()
    for out_ref, near in ((first_ref, HALF * (1 - par)), (second_ref, HALF * par)):
        far = HALF - near
        close = near + 3 * (near // HALF)
        for n, ref in enumerate(fields):
            out_ref[pl.ds(HALF * n, HALF)] = ref[pl.ds(near, HALF)].astype(bf16)
            value = ref[pl.ds(close, 1)]
            out_ref[pl.ds(4 * HALF + n, 1)] = (value - value.astype(bf16).astype(f32)).astype(bf16)
        out_ref[pl.ds(3 * HALF, HALF)] = (now_ref[pl.ds(far, HALF)] * speed_ref[pl.ds(far, HALF)]).astype(bf16)


def inject_kernel(depth_ref, row_ref, amount_ref, out_hbm, mark_hbm, table, fields, sems):
    top = lax.axis_index("dom") * DEPTH - HALF
    count = depth_ref.shape[1]
    steps = amount_ref.shape[0]
    local = depth_ref[...] - top
    place = row_ref[...]
    key = jnp.where((local >= 0) & (local < EXT), local * NX + place // NY, -1)
    hit = lax.broadcasted_iota(jnp.int32, (NY, count), 0) == lax.rem(place, NY)
    for k in range(steps):
        amount = amount_ref[k : k + 1, :]
        head = amount.astype(bf16).astype(f32)
        table[0, k * NY : (k + 1) * NY, :] = jnp.where(hit, head, 0.0).astype(bf16)
        table[1, k * NY : (k + 1) * NY, :] = jnp.where(hit, amount - head, 0.0).astype(bf16)
    planes = 2
    cell = lax.broadcasted_iota(jnp.int32, (planes * NX, count), 0)

    def store(g):
        at = pl.ds(g * planes, planes)
        return pltpu.make_async_copy(fields.at[at], out_hbm.at[at], sems.at[g])

    @pl.loop(0, EXT // planes)
    def _(g):
        pick = jnp.where(cell + g * (planes * NX) == key, 1.0, 0.0).astype(bf16)
        field = lax.dot_general(
            pick, table[0], (((1,), (1,)), ((), ())), preferred_element_type=f32
        ) + lax.dot_general(pick, table[1], (((1,), (1,)), ((), ())), preferred_element_type=f32)
        for k in range(steps):
            for j in range(planes):
                fields[g * planes + j, k] = field[j * NX : (j + 1) * NX, k * NY : (k + 1) * NY]
        store(g).start()

    mark = pltpu.make_async_copy(fields.at[0, 0, 0:8], mark_hbm, sems.at[EXT // planes])
    mark.start()
    for g in range(EXT // planes):
        store(g).wait()
    mark.wait()


def send_second(par, buf, far_ref, speed_ext, scale_far, first_ref, second_ref):
    def emit(lower, upper):
        for p in range(DEPTH):
            near_ref, other_ref = (upper, lower) if p >= HALF else (lower, upper)
            for row in range(0, NX, CHUNK):
                total = None
                for k in range(1, HALF + 1):
                    q = p - k if p >= HALF else p + k
                    if (p >= HALF) == (q >= HALF):
                        continue
                    term = stencil_coef[k] * buf[q + HALF, padded(row), :]
                    total = term if total is None else total + term
                fresh = far_ref[p, rows(row), :]
                if scale_far:
                    fresh = fresh * speed_ext[p + HALF, rows(row), :]
                else:
                    total = total * speed_ext[p + HALF, rows(row), :]
                near_ref[p % HALF, rows(row), :] = total.astype(bf16)
                other_ref[HALF + p % HALF, rows(row), :] = fresh.astype(bf16)

    by_side(par, first_ref, second_ref, emit)


def adjoint_first_kernel(
    now_hbm, next_hbm, speed_hbm, inject_hbm, got_a, got_b,
    first_ref, second_ref, lam_ref, speed_ext,
    buf4, q3_ref, now_halo, next_halo, now_ref, next_ref, inject_ref, sems,
):
    par = parity()
    own = slice(HALF, HALF + DEPTH)
    copies = fetch(
        (speed_hbm, now_hbm, next_hbm, inject_hbm.at[:, 0:2]), (speed_ext.at[own], now_ref, next_ref, inject_ref), sems
    )
    zero_pads(buf4)
    zero_pads(q3_ref)
    weights = band()
    inner = slice(PAD, PAD + NX)
    for copy in copies[:2]:
        copy.wait()
    buf4[2 * HALF : 2 * HALF + DEPTH, inner, :] = now_ref[...] * speed_ext[own]

    def halo(lower, upper):
        for ref, at, close, far_at in ((lower, 0, 3, 0), (upper, HALF, 0, WIDE - HALF)):
            ext_at = ext_of_halo(at)
            for n, (held, to) in enumerate(((now_halo, at), (next_halo, at), (speed_ext, ext_at))):
                held[to : to + HALF] = ref[HALF * n : HALF * n + HALF].astype(f32)
                held[to + close] = held[to + close] + ref[4 * HALF + n].astype(f32)
            buf4[far_at : far_at + HALF, inner, :] = ref[3 * HALF : 4 * HALF].astype(f32)
            buf4[ext_at + HALF : ext_at + 2 * HALF, inner, :] = (
                now_halo[at : at + HALF] * speed_ext[ext_at : ext_at + HALF]
            )

    by_side(par, got_a, got_b, halo)
    for copy in copies[2:]:
        copy.wait()

    def halo_lam3(h, row, lap):
        e = ext_of_halo(h)
        now = now_halo[h, rows(row), :]
        lam = 2.0 * now - next_halo[h, rows(row), :] + lap + inject_ref[e, 0, rows(row), :]
        lam_ref[e, rows(row), :] = lam
        lam_ref[EXT + DEPTH + h, rows(row), :] = 2.0 * lam - now + inject_ref[e, 1, rows(row), :]
        q3_ref[e, padded(row), :] = lam * speed_ext[e, rows(row), :]

    sweep_halo(buf4, weights, halo_lam3)

    def own_lam3(p, row, lap):
        lam = 2.0 * now_ref[p, rows(row), :] - next_ref[p, rows(row), :] + lap
        lam = lam + inject_ref[p + HALF, 0, rows(row), :]
        lam_ref[p + HALF, rows(row), :] = lam
        q3_ref[p + HALF, padded(row), :] = lam * speed_ext[p + HALF, rows(row), :]

    sweep_own(buf4, 2 * HALF, weights, own_lam3)

    def own_lam2(p, row, lap):
        lam = 2.0 * lam_ref[p + HALF, rows(row), :] - now_ref[p, rows(row), :] + lap
        lam_ref[EXT + p, rows(row), :] = lam + inject_ref[p + HALF, 1, rows(row), :]

    sweep_own(q3_ref, HALF, weights, own_lam2)
    send_second(par, q3_ref, lam_ref.at[EXT : EXT + DEPTH], speed_ext, True, first_ref, second_ref)


def forward_pack_kernel(holder_ref, pieces_ref, order_ref, first_ref, second_ref):
    par = parity()
    per_plane = NX // 32
    for p in range(DEPTH):
        for j in range(per_plane):
            piece = pieces_ref[holder_ref[(DEPTH + p) * per_plane + j]]
            first_ref[HALF + p, 32 * j : 32 * j + 32, :] = piece
            second_ref[HALF + p, 32 * j : 32 * j + 32, :] = piece
    at = HALF * (1 - par)
    for p in range(HALF):
        for j in range(per_plane):
            first_ref[p, 32 * j : 32 * j + 32, :] = pieces_ref[holder_ref[(at + p) * per_plane + j]]
            second_ref[p, 32 * j : 32 * j + 32, :] = pieces_ref[holder_ref[(HALF - at + p) * per_plane + j]]


def source_place(depth_ref, row_ref):
    local = depth_ref[0] - (lax.axis_index("dom") * DEPTH - HALF)
    return local, row_ref[0] // NY, lax.rem(row_ref[0], NY)


def forward_first_kernel(
    depth_ref, row_ref, wave_ref, mine_a, mine_b, got_a, got_b, speed_ext,
    first_ref, second_ref, u1_ref, u2_ref, base_ref, lap0_ref, lap1_ref,
    buf0, prev_ext,
):
    par = parity()
    zero_pads(buf0)
    zero_pads(u1_ref)
    weights = band()
    inner = slice(PAD, PAD + NX)
    prev_ext[pl.ds(HALF + HALF * (1 - par), HALF)] = mine_a[0:HALF].astype(f32)
    prev_ext[pl.ds(HALF + HALF * par, HALF)] = mine_b[0:HALF].astype(f32)
    buf0[2 * HALF : 2 * HALF + DEPTH, inner, :] = mine_a[HALF : HALF + DEPTH].astype(f32)

    def halo(lower, upper):
        for ref, at, wide_at in ((lower, 0, 0), (upper, HALF + DEPTH, 2 * HALF + DEPTH)):
            prev_ext[at : at + HALF] = ref[0:HALF].astype(f32)
            buf0[wide_at : wide_at + DEPTH, inner, :] = ref[HALF : HALF + DEPTH].astype(f32)

    by_side(par, got_a, got_b, halo)

    def step(e, row, lap):
        now = buf0[e + HALF, padded(row), :]
        value = 2.0 * now - prev_ext[e, rows(row), :] + speed_ext[e, rows(row), :] * lap
        u1_ref[e, padded(row), :] = value
        return now

    sweep_halo(buf0, weights, lambda h, row, lap: step(ext_of_halo(h), row, lap))

    def own_u1(p, row, lap):
        step(p + HALF, row, lap)
        lap0_ref[p, rows(row), :] = lap

    sweep_own(buf0, 2 * HALF, weights, own_u1)
    local, across, along_y = source_place(depth_ref, row_ref)

    @pl.when((local >= 0) & (local < EXT))
    def _():
        add_cell(u1_ref, local, across + PAD, along_y, wave_ref[0, 0])

    def own_u2(p, row, lap):
        value = 2.0 * u1_ref[p + HALF, padded(row), :] - buf0[p + 2 * HALF, padded(row), :]
        u2_ref[p, rows(row), :] = value + speed_ext[p + HALF, rows(row), :] * lap
        lap1_ref[p, rows(row), :] = lap

    sweep_own(u1_ref, HALF, weights, own_u2)

    @pl.when((local >= HALF) & (local < HALF + DEPTH))
    def _():
        add_cell(u2_ref, local - HALF, across, along_y, wave_ref[0, 1])

    send_second(par, u1_ref, u2_ref, speed_ext, False, first_ref, second_ref)
    for h in range(2 * HALF):
        e = ext_of_halo(h)
        base_ref[h] = 2.0 * u1_ref[e, inner, :] - buf0[e + HALF, inner, :]


def middle_kernel(
    depth_ref, row_ref, wave_ref, inject_hbm, got_a, got_b, lam_ref, speed_ext, u1_ref, base_ref, lap0_ref, lap1_ref,
    late_ref, early_ref, u2_ref, grad_ref,
    lam2_halo, buf2, buf1, inject_ref, sems,
):
    par = parity()
    (copy,) = fetch((inject_hbm.at[:, 2:4],), (inject_ref,), sems)
    zero_pads(buf2)
    zero_pads(buf1)
    weights = band()
    inner = slice(PAD, PAD + NX)
    buf1[:, inner, :] = lam_ref[0:EXT] * speed_ext[...]

    def alone(h, row, lap):
        lam2_halo[h, rows(row), :] = lam_ref[EXT + DEPTH + h, rows(row), :] + lap

    sweep_halo_alone(buf1, weights, alone)
    copy.wait()

    def halo(lower, upper):
        for ref, at, far_at in ((lower, 0, 0), (upper, HALF, WIDE - HALF)):
            ext_at = ext_of_halo(at)
            value = lam2_halo[at : at + HALF] + ref[0:HALF].astype(f32)
            lam2_halo[at : at + HALF] = value
            buf2[ext_at + HALF : ext_at + 2 * HALF, inner, :] = value * speed_ext[ext_at : ext_at + HALF]
            buf2[far_at : far_at + HALF, inner, :] = ref[HALF : 2 * HALF].astype(f32)

    by_side(par, got_a, got_b, halo)
    buf2[2 * HALF : 2 * HALF + DEPTH, inner, :] = lam_ref[EXT : EXT + DEPTH] * speed_ext[HALF : HALF + DEPTH]

    def halo_lam1(h, row, lap):
        e = ext_of_halo(h)
        lam = 2.0 * lam2_halo[h, rows(row), :] - lam_ref[e, rows(row), :] + lap
        lam = lam + inject_ref[e, 0, rows(row), :]
        buf1[e, padded(row), :] = lam * speed_ext[e, rows(row), :]

    sweep_halo(buf2, weights, halo_lam1)

    def own_lam1(p, row, lap):
        lam = 2.0 * lam_ref[EXT + p, rows(row), :] - lam_ref[p + HALF, rows(row), :] + lap
        lam = lam + inject_ref[p + HALF, 0, rows(row), :]
        late_ref[p, rows(row), :] = lam
        grad_ref[p, rows(row), :] = (
            lam * lap0_ref[p, rows(row), :] + lam_ref[EXT + p, rows(row), :] * lap1_ref[p, rows(row), :]
        )
        buf1[p + HALF, padded(row), :] = lam * speed_ext[p + HALF, rows(row), :]

    sweep_own(buf2, 2 * HALF, weights, own_lam1)

    def own_lam0(p, row, lap):
        lam = 2.0 * late_ref[p, rows(row), :] - lam_ref[EXT + p, rows(row), :] + lap
        early_ref[p, rows(row), :] = lam + inject_ref[p + HALF, 1, rows(row), :]

    sweep_own(buf1, HALF, weights, own_lam0)

    def halo_u2(h, row, lap):
        e = ext_of_halo(h)
        u2_ref[h, rows(row), :] = base_ref[h, rows(row), :] + speed_ext[e, rows(row), :] * lap

    sweep_halo_alone(u1_ref, weights, halo_u2)
    local, across, along_y = source_place(depth_ref, row_ref)

    @pl.when(((local >= 0) & (local < HALF)) | ((local >= HALF + DEPTH) & (local < EXT)))
    def _():
        add_cell(u2_ref, jnp.where(local < HALF, local, local - DEPTH), across, along_y, wave_ref[0, 1])


def forward_second_kernel(
    depth_ref, row_ref, wave_ref, got_a, got_b, u1_ref, u2_ref, u2_halo_ref, speed_ext, lam3_ref, lam4_ref, grad_ref,
    keep_ref, send_ref, buf2, buf3, total,
):
    par = parity()
    zero_pads(buf2)
    zero_pads(buf3)
    weights = band()
    inner = slice(PAD, PAD + NX)

    def halo(lower, upper):
        for ref, at, far_at in ((lower, 0, 0), (upper, HALF, WIDE - HALF)):
            ext_at = ext_of_halo(at)
            buf2[ext_at + HALF : ext_at + 2 * HALF, inner, :] = u2_halo_ref[at : at + HALF] + ref[0:HALF].astype(f32)
            buf2[far_at : far_at + HALF, inner, :] = ref[HALF : 2 * HALF].astype(f32)

    by_side(par, got_a, got_b, halo)
    buf2[2 * HALF : 2 * HALF + DEPTH, inner, :] = u2_ref[...]

    def step(e, row, lap):
        value = 2.0 * buf2[e + HALF, padded(row), :] - u1_ref[e, padded(row), :]
        buf3[e, padded(row), :] = value + speed_ext[e, rows(row), :] * lap

    sweep_halo(buf2, weights, lambda h, row, lap: step(ext_of_halo(h), row, lap))

    def own_u3(p, row, lap):
        step(p + HALF, row, lap)
        total[p, rows(row), :] = grad_ref[p, rows(row), :] + lap * lam3_ref[p + HALF, rows(row), :]

    sweep_own(buf2, 2 * HALF, weights, own_u3)
    local, across, along_y = source_place(depth_ref, row_ref)

    @pl.when((local >= 0) & (local < EXT))
    def _():
        add_cell(buf3, local, across + PAD, along_y, wave_ref[0, 2])

    def to_gradient(p, row, lap):
        value = total[p, rows(row), :] + lap * lam4_ref[p, rows(row), :]
        total[p, rows(row), :] = grad_scale * value

    sweep_own(buf3, HALF, weights, to_gradient)
    shot = lax.axis_index("shot")
    pair, core = shot // 2, lax.rem(shot, 2)
    for n, half in enumerate((pair, 1 - pair)):
        keep_at = pl.multiple_of((half * 2 + core) * 32, 32)
        send_at = pl.multiple_of((half * 2 + 1 - core) * 32, 32)
        keep_ref[n] = total[:, pl.ds(keep_at, 32), :]
        send_ref[n] = total[:, pl.ds(send_at, 32), :]


def per_device(
    parked, parked_slot, holder_list, speed_sq, adjoint_next, adjoint_now,
    wavelet, src_depth, src_row, rec_depth, rec_row, residuals,
):
    peers = lax.axis_size("dom")
    even = [(i, i ^ 1) for i in range(peers)]
    odd = [(i, ((i + 1) ^ 1) - 1) for i in range(1, peers - 1)]
    swap = lambda a, b: (lax.ppermute(a, "dom", even), lax.ppermute(b, "dom", odd))
    lam4, lam5 = adjoint_now[0], adjoint_next[0]
    ext = ((EXT, NX, NY), f32)
    slab = ((DEPTH, NX, NY), f32)
    wide = ((EXT, ROWS, NY), f32)

    def planes(count):
        return ((count, NX, NY), bf16)

    mark = ((8, NY), f32)
    (outgoing,) = call(
        gather_kernel, "gather", [HB] * 2, [((64, 32, NY), bf16)],
        [
            pltpu.VMEM((64 * 32, NY), f32), pltpu.VMEM((1, 64), jnp.int32), pltpu.VMEM((64, 4096), bf16),
            pltpu.SemaphoreType.DMA((2,)),
        ],
        in_hbm(parked_slot[0], parked[0]),
    )
    incoming = lax.all_to_all(outgoing, "dom", split_axis=0, concat_axis=0, tiled=True)
    send_a, send_b = call(
        adjoint_pack_kernel, "adjoint_pack", [HB] * 3, [planes(19)] * 2,
        [pltpu.VMEM(*slab)] * 3 + [pltpu.SemaphoreType.DMA((3,))], in_hbm(lam4, lam5, speed_sq),
    )
    got_a, got_b = swap(send_a, send_b)
    count = rec_depth.shape[0]
    steps = residuals.shape[1]
    inject, order = call(
        inject_kernel, "inject", [VM] * 3, [((EXT, steps, NX, NY), f32), mark],
        [
            pltpu.VMEM((2, steps * NY, count), bf16), pltpu.VMEM((EXT, steps, NX, NY), f32),
            pltpu.SemaphoreType.DMA((EXT // 2 + 1,)),
        ],
        (rec_depth.reshape(1, count), rec_row.reshape(1, count), residuals[0]), us=4,
    )
    fields = pltpu.VMEM((EXT, 2, NX, NY), f32)
    send_a, send_b, lam23, speed_ext = call(
        adjoint_first_kernel, "adjoint_first", [HB] * 4 + [VM] * 2,
        [planes(8)] * 2 + [((EXT + 2 * DEPTH, NX, NY), f32), ext],
        [buffer(WIDE), buffer(EXT)] + [pltpu.VMEM(*slab)] * 4 + [fields, pltpu.SemaphoreType.DMA((4,))],
        in_hbm(lam4, lam5, speed_sq, inject) + (got_a, got_b),
    )
    back_a, back_b = swap(send_a, send_b)

    mine_a, mine_b = call(
        forward_pack_kernel, "forward_pack", [SM, VM, HB], [planes(12)] * 2, [],
        (holder_list.reshape(64), incoming) + in_hbm(order),
    )
    got_a, got_b = swap(mine_a, mine_b)
    send_a, send_b, u1, u2, base_u, lap0, lap1 = call(
        forward_first_kernel, "forward_first", [SM] * 3 + [VM] * 5,
        [planes(8)] * 2 + [wide, slab, slab, slab, slab],
        [buffer(WIDE), pltpu.VMEM(*ext)],
        (src_depth, src_row, wavelet, mine_a, mine_b, got_a, got_b, speed_ext),
    )
    got_a, got_b = swap(send_a, send_b)
    late, early, u2_halo, grad = call(
        middle_kernel, "middle", [SM] * 3 + [HB] + [VM] * 8, [slab] * 4,
        [pltpu.VMEM(*slab), buffer(WIDE), buffer(EXT), fields, pltpu.SemaphoreType.DMA((1,))],
        (src_depth, src_row, wavelet) + in_hbm(inject)
        + (back_a, back_b, lam23, speed_ext, u1, base_u, lap0, lap1),
    )
    quarter = ((2, DEPTH, NX // 4, NY), f32)
    keep, send = call(
        forward_second_kernel, "forward_second", [SM] * 3 + [VM] * 9, [quarter] * 2,
        [buffer(WIDE), buffer(EXT), pltpu.VMEM(*slab)],
        (src_depth, src_row, wavelet, got_a, got_b, u1, u2, u2_halo, speed_ext, lam23, lam4, grad),
    )
    got = lax.ppermute(send, "shot", [(0, 1), (1, 0), (2, 3), (3, 2)])
    other = lax.ppermute(keep[1] + got[1], "shot", [(0, 2), (2, 0), (1, 3), (3, 1)])
    gradient = keep[0] + got[0] + other
    return (gradient, late[None], early[None])


def solution(mesh):
    in_specs = (
        P("shot", "dom", None),
        P("shot", "dom", None),
        P("shot", "dom", None),
        P("dom", None, None),
        P("shot", "dom", None, None),
        P("shot", "dom", None, None),
        P("shot", None),
        P("shot"),
        P("shot"),
        P(),
        P(),
        P("shot", None, None),
    )
    out_specs = (P("dom", "shot", None), P("shot", "dom", None, None), P("shot", "dom", None, None))
    return jax.shard_map(
        per_device, mesh=mesh, in_specs=in_specs, out_specs=out_specs, check_vma=False
    )
```

```python
import functools

import jax
import jax.numpy as jnp
from jax import lax
from jax.experimental import pallas as pl
from jax.experimental.pallas import tpu as pltpu
from jax.sharding import PartitionSpec as P

stencil_coef = (-205.0 / 72.0, 8.0 / 5.0, -1.0 / 5.0, 8.0 / 315.0, -1.0 / 560.0)
grad_scale = 0.0625

DEPTH = 8
HALF = 4
EXT = DEPTH + 2 * HALF
WIDE = DEPTH + 4 * HALF
NX = 128
NY = 128
PAD = 8
ROWS = NX + 2 * PAD
CHUNK = 32
GROUP = 4
bf16 = jnp.bfloat16
f32 = jnp.float32

VM = pl.BlockSpec(memory_space=pltpu.VMEM)
SM = pl.BlockSpec(memory_space=pltpu.SMEM)
HB = pl.BlockSpec(memory_space=pltpu.HBM)


def in_hbm(*arrays):
    return tuple(pltpu.with_memory_space_constraint(a, pltpu.HBM) for a in arrays)


def fetch(sources, targets, sems):
    copies = [pltpu.make_async_copy(src, dst, sems.at[n]) for n, (src, dst) in enumerate(zip(sources, targets))]
    for copy in copies:
        copy.start()
    return copies


def call(kernel, name, ins, outs, scratch, args, us=2, limit=20 << 20):
    return pl.pallas_call(
        kernel,
        name=name,
        out_shape=[pltpu.HBM(*o) if name == "inject" else jax.ShapeDtypeStruct(*o) for o in outs],
        in_specs=ins,
        out_specs=[HB if name == "inject" else VM] * len(outs),
        scratch_shapes=scratch,
        compiler_params=pltpu.CompilerParams(vmem_limit_bytes=limit),
        cost_estimate=pl.CostEstimate(flops=us * 10**9, bytes_accessed=us * 3_600_000, transcendentals=0),
    )(*args)


def buffer(planes):
    return pltpu.VMEM((planes, ROWS, NY), f32)


def zero_pads(buf):
    zeros = jnp.zeros((buf.shape[0], PAD, NY), f32)
    buf[:, 0:PAD, :] = zeros
    buf[:, PAD + NX : ROWS, :] = zeros


def band():
    apart = jnp.abs(
        lax.broadcasted_iota(jnp.int32, (NY, NY), 0) - lax.broadcasted_iota(jnp.int32, (NY, NY), 1)
    )
    weights = jnp.zeros((NY, NY), f32)
    for k in range(1, HALF + 1):
        weights = jnp.where(apart == k, 5.0 * stencil_coef[k], weights)
    head = weights.astype(bf16)
    rest = (weights - head.astype(f32)).astype(bf16)
    both = jnp.concatenate([head, rest], axis=1)
    return jnp.concatenate([both, both], axis=0), head


def along(plane, weights):
    both, head = weights
    first = plane.astype(bf16)
    left = plane - first.astype(f32)
    second = left.astype(bf16)
    third = (left - second.astype(f32)).astype(bf16)
    pair = jnp.dot(jnp.concatenate([first, second], axis=1), both, preferred_element_type=f32)
    return 0.2 * (pair[:, :NY] + pair[:, NY:] + jnp.dot(third, head, preferred_element_type=f32))


def rows(row):
    return slice(row, row + CHUNK)


def padded(row):
    return slice(PAD + row, PAD + row + CHUNK)


def group_laps(buf, first, weights, body):
    static = isinstance(first, int)
    parts = [along(buf[first + j, PAD : PAD + NX, :], weights) for j in range(GROUP)]
    for j in range(GROUP):
        at = first + j
        for row in range(0, NX, CHUNK):
            base = PAD + row
            lap = (3.0 * stencil_coef[0]) * buf[at, padded(row), :] + parts[j][row : row + CHUNK]
            for k in range(1, HALF + 1):
                near = buf[at, base + k : base + k + CHUNK, :] + buf[at, base - k : base - k + CHUNK, :]
                for q in (at + k, at - k):
                    if not static or 0 <= q < buf.shape[0]:
                        near = near + buf[q, padded(row), :]
                lap = lap + stencil_coef[k] * near
            body(j, row, lap)


def sweep_own(buf, shift, weights, body):
    @pl.loop(0, DEPTH // GROUP)
    def _(g):
        group_laps(buf, g * GROUP + shift, weights, lambda j, row, lap: body(g * GROUP + j, row, lap))


def sweep_halo(buf, weights, body):
    @pl.loop(0, 2)
    def _(g):
        group_laps(
            buf, HALF + g * (HALF + DEPTH), weights, lambda j, row, lap: body(g * GROUP + j, row, lap)
        )


def sweep_halo_alone(buf, weights, body):
    for g in range(2):
        group_laps(
            buf, g * (HALF + DEPTH), weights, lambda j, row, lap, g=g: body(g * GROUP + j, row, lap)
        )


def ext_of_halo(h):
    return h + DEPTH * (h // HALF) if isinstance(h, int) else jnp.where(h < HALF, h, h + DEPTH)


def add_cell(ref, plane, row, column, amount):
    lane = lax.broadcasted_iota(jnp.int32, (1, NY), 1)
    old = ref[plane, pl.ds(row, 1), :]
    ref[plane, pl.ds(row, 1), :] = old + jnp.where(lane == column, amount, 0.0)


def parity():
    return lax.rem(lax.axis_index("dom"), 2)


def by_side(par, first, second, body):
    @pl.when(par == 0)
    def _():
        body(second, first)

    @pl.when(par == 1)
    def _():
        body(first, second)


def gather_kernel(slot_hbm, parked_hbm, out_ref, held, slot_ref, parked_ref, sems):
    width = parked_ref.shape[1] // 4
    parts = [pl.ds(width * n, width) for n in range(4)]
    slots, *copies = fetch(
        [slot_hbm] + [parked_hbm.at[:, part] for part in parts], [slot_ref] + [parked_ref.at[:, part] for part in parts], sems
    )
    slots.wait()
    pieces = parked_ref.shape[0]
    row = lax.broadcasted_iota(jnp.int32, (pieces, pieces), 0)
    pick = jnp.where(row == slot_ref[...], 1.0, 0.0).astype(bf16)
    for col in range(32):
        if col % 8 == 0:
            copies[col // 8].wait()
        part = lax.dot_general(
            pick,
            parked_ref[:, col * NY : (col + 1) * NY],
            (((0,), (0,)), ((), ())),
            preferred_element_type=f32,
        )
        held[pl.ds(col, pieces, stride=32), :] = part
    out_ref[...] = held[...].reshape(pieces, 32, NY).astype(bf16)


def adjoint_pack_kernel(now_hbm, next_hbm, speed_hbm, first_ref, second_ref, now_ref, next_ref, speed_ref, sems):
    fields = (now_ref, next_ref, speed_ref)
    for copy in fetch((now_hbm, next_hbm, speed_hbm), fields, sems):
        copy.wait()
    par = parity()
    for out_ref, near in ((first_ref, HALF * (1 - par)), (second_ref, HALF * par)):
        far = HALF - near
        close = near + 3 * (near // HALF)
        for n, ref in enumerate(fields):
            out_ref[pl.ds(HALF * n, HALF)] = ref[pl.ds(near, HALF)].astype(bf16)
            value = ref[pl.ds(close, 1)]
            out_ref[pl.ds(4 * HALF + n, 1)] = (value - value.astype(bf16).astype(f32)).astype(bf16)
        out_ref[pl.ds(3 * HALF, HALF)] = (now_ref[pl.ds(far, HALF)] * speed_ref[pl.ds(far, HALF)]).astype(bf16)


def inject_kernel(depth_ref, row_ref, amount_ref, out_hbm, mark_hbm, table, fields, sems):
    top = lax.axis_index("dom") * DEPTH - HALF
    count = depth_ref.shape[1]
    steps = amount_ref.shape[0]
    local = depth_ref[...] - top
    place = row_ref[...]
    key = jnp.where((local >= 0) & (local < EXT), local * NX + place // NY, -1)
    hit = lax.broadcasted_iota(jnp.int32, (NY, count), 0) == lax.rem(place, NY)
    for k in range(steps):
        amount = amount_ref[k : k + 1, :]
        head = amount.astype(bf16).astype(f32)
        table[0, k * NY : (k + 1) * NY, :] = jnp.where(hit, head, 0.0).astype(bf16)
        table[1, k * NY : (k + 1) * NY, :] = jnp.where(hit, amount - head, 0.0).astype(bf16)
    planes = 2
    cell = lax.broadcasted_iota(jnp.int32, (planes * NX, count), 0)

    def store(g):
        at = pl.ds(g * planes, planes)
        return pltpu.make_async_copy(fields.at[at], out_hbm.at[at], sems.at[g])

    @pl.loop(0, EXT // planes)
    def _(g):
        pick = jnp.where(cell + g * (planes * NX) == key, 1.0, 0.0).astype(bf16)
        field = lax.dot_general(
            pick, table[0], (((1,), (1,)), ((), ())), preferred_element_type=f32
        ) + lax.dot_general(pick, table[1], (((1,), (1,)), ((), ())), preferred_element_type=f32)
        for k in range(steps):
            for j in range(planes):
                fields[g * planes + j, k] = field[j * NX : (j + 1) * NX, k * NY : (k + 1) * NY]
        store(g).start()

    mark = pltpu.make_async_copy(fields.at[0, 0, 0:8], mark_hbm, sems.at[EXT // planes])
    mark.start()
    for g in range(EXT // planes):
        store(g).wait()
    mark.wait()


def send_second(par, buf, far_ref, speed_ext, scale_far, first_ref, second_ref):
    def emit(lower, upper):
        for p in range(DEPTH):
            near_ref, other_ref = (upper, lower) if p >= HALF else (lower, upper)
            for row in range(0, NX, CHUNK):
                total = None
                for k in range(1, HALF + 1):
                    q = p - k if p >= HALF else p + k
                    if (p >= HALF) == (q >= HALF):
                        continue
                    term = stencil_coef[k] * buf[q + HALF, padded(row), :]
                    total = term if total is None else total + term
                fresh = far_ref[p, rows(row), :]
                if scale_far:
                    fresh = fresh * speed_ext[p + HALF, rows(row), :]
                else:
                    total = total * speed_ext[p + HALF, rows(row), :]
                near_ref[p % HALF, rows(row), :] = total.astype(bf16)
                other_ref[HALF + p % HALF, rows(row), :] = fresh.astype(bf16)

    by_side(par, first_ref, second_ref, emit)


def adjoint_first_kernel(
    now_ref, next_ref, speed_ref, inject_hbm, got_a, got_b,
    first_ref, second_ref, lam_ref, speed_ext, q3_ref,
    buf4, now_halo, next_halo, inject_ref, sems,
):
    par = parity()
    own = slice(HALF, HALF + DEPTH)
    (copy,) = fetch((inject_hbm.at[:, 0:2],), (inject_ref,), sems)
    zero_pads(buf4)
    zero_pads(q3_ref)
    weights = band()
    inner = slice(PAD, PAD + NX)
    speed_ext[own] = speed_ref[...]
    buf4[2 * HALF : 2 * HALF + DEPTH, inner, :] = now_ref[...] * speed_ext[own]

    def halo(lower, upper):
        for ref, at, close, far_at in ((lower, 0, 3, 0), (upper, HALF, 0, WIDE - HALF)):
            ext_at = ext_of_halo(at)
            for n, (held, to) in enumerate(((now_halo, at), (next_halo, at), (speed_ext, ext_at))):
                held[to : to + HALF] = ref[HALF * n : HALF * n + HALF].astype(f32)
                held[to + close] = held[to + close] + ref[4 * HALF + n].astype(f32)
            buf4[far_at : far_at + HALF, inner, :] = ref[3 * HALF : 4 * HALF].astype(f32)
            buf4[ext_at + HALF : ext_at + 2 * HALF, inner, :] = (
                now_halo[at : at + HALF] * speed_ext[ext_at : ext_at + HALF]
            )

    by_side(par, got_a, got_b, halo)
    copy.wait()

    def halo_lam3(h, row, lap):
        e = ext_of_halo(h)
        now = now_halo[h, rows(row), :]
        lam = 2.0 * now - next_halo[h, rows(row), :] + lap + inject_ref[e, 0, rows(row), :]
        lam_ref[e, rows(row), :] = lam
        lam_ref[EXT + DEPTH + h, rows(row), :] = 2.0 * lam - now + inject_ref[e, 1, rows(row), :]
        q3_ref[e, padded(row), :] = lam * speed_ext[e, rows(row), :]

    sweep_halo(buf4, weights, halo_lam3)

    def own_lam3(p, row, lap):
        lam = 2.0 * now_ref[p, rows(row), :] - next_ref[p, rows(row), :] + lap
        lam = lam + inject_ref[p + HALF, 0, rows(row), :]
        lam_ref[p + HALF, rows(row), :] = lam
        q3_ref[p + HALF, padded(row), :] = lam * speed_ext[p + HALF, rows(row), :]

    sweep_own(buf4, 2 * HALF, weights, own_lam3)

    def own_lam2(p, row, lap):
        lam = 2.0 * lam_ref[p + HALF, rows(row), :] - now_ref[p, rows(row), :] + lap
        lam_ref[EXT + p, rows(row), :] = lam + inject_ref[p + HALF, 1, rows(row), :]

    sweep_own(q3_ref, HALF, weights, own_lam2)
    send_second(par, q3_ref, lam_ref.at[EXT : EXT + DEPTH], speed_ext, True, first_ref, second_ref)


def forward_pack_kernel(holder_ref, pieces_ref, order_ref, first_ref, second_ref):
    par = parity()
    per_plane = NX // 32
    for p in range(DEPTH):
        for j in range(per_plane):
            piece = pieces_ref[holder_ref[(DEPTH + p) * per_plane + j]]
            first_ref[HALF + p, 32 * j : 32 * j + 32, :] = piece
            second_ref[HALF + p, 32 * j : 32 * j + 32, :] = piece
    at = HALF * (1 - par)
    for p in range(HALF):
        for j in range(per_plane):
            first_ref[p, 32 * j : 32 * j + 32, :] = pieces_ref[holder_ref[(at + p) * per_plane + j]]
            second_ref[p, 32 * j : 32 * j + 32, :] = pieces_ref[holder_ref[(HALF - at + p) * per_plane + j]]


def source_place(depth_ref, row_ref):
    local = depth_ref[0] - (lax.axis_index("dom") * DEPTH - HALF)
    return local, row_ref[0] // NY, lax.rem(row_ref[0], NY)


def forward_first_kernel(
    depth_ref, row_ref, wave_ref, mine_a, mine_b, got_a, got_b, speed_ext,
    first_ref, second_ref, u1_ref, u2_ref, base_ref, lap0_ref, lap1_ref,
    buf0, prev_ext,
):
    par = parity()
    zero_pads(buf0)
    zero_pads(u1_ref)
    weights = band()
    inner = slice(PAD, PAD + NX)
    prev_ext[pl.ds(HALF + HALF * (1 - par), HALF)] = mine_a[0:HALF].astype(f32)
    prev_ext[pl.ds(HALF + HALF * par, HALF)] = mine_b[0:HALF].astype(f32)
    buf0[2 * HALF : 2 * HALF + DEPTH, inner, :] = mine_a[HALF : HALF + DEPTH].astype(f32)

    def halo(lower, upper):
        for ref, at, wide_at in ((lower, 0, 0), (upper, HALF + DEPTH, 2 * HALF + DEPTH)):
            prev_ext[at : at + HALF] = ref[0:HALF].astype(f32)
            buf0[wide_at : wide_at + DEPTH, inner, :] = ref[HALF : HALF + DEPTH].astype(f32)

    by_side(par, got_a, got_b, halo)

    def step(e, row, lap):
        now = buf0[e + HALF, padded(row), :]
        value = 2.0 * now - prev_ext[e, rows(row), :] + speed_ext[e, rows(row), :] * lap
        u1_ref[e, padded(row), :] = value
        return now

    sweep_halo(buf0, weights, lambda h, row, lap: step(ext_of_halo(h), row, lap))

    def own_u1(p, row, lap):
        step(p + HALF, row, lap)
        lap0_ref[p, rows(row), :] = lap

    sweep_own(buf0, 2 * HALF, weights, own_u1)
    local, across, along_y = source_place(depth_ref, row_ref)

    @pl.when((local >= 0) & (local < EXT))
    def _():
        add_cell(u1_ref, local, across + PAD, along_y, wave_ref[0, 0])

    def own_u2(p, row, lap):
        value = 2.0 * u1_ref[p + HALF, padded(row), :] - buf0[p + 2 * HALF, padded(row), :]
        u2_ref[p, rows(row), :] = value + speed_ext[p + HALF, rows(row), :] * lap
        lap1_ref[p, rows(row), :] = lap

    sweep_own(u1_ref, HALF, weights, own_u2)

    @pl.when((local >= HALF) & (local < HALF + DEPTH))
    def _():
        add_cell(u2_ref, local - HALF, across, along_y, wave_ref[0, 1])

    send_second(par, u1_ref, u2_ref, speed_ext, False, first_ref, second_ref)
    for h in range(2 * HALF):
        e = ext_of_halo(h)
        base_ref[h] = 2.0 * u1_ref[e, inner, :] - buf0[e + HALF, inner, :]


def middle_kernel(
    depth_ref, row_ref, wave_ref, inject_hbm, got_a, got_b, lam_ref, q3_ref, speed_ext, u1_ref, base_ref, lap0_ref, lap1_ref,
    late_ref, u2_ref, grad_ref, lam2_halo, buf2,
    inject_ref, sems,
):
    par = parity()
    (copy,) = fetch((inject_hbm.at[HALF : HALF + DEPTH, 2],), (inject_ref,), sems)
    zero_pads(buf2)
    weights = band()
    inner = slice(PAD, PAD + NX)

    def alone(h, row, lap):
        lam2_halo[h, rows(row), :] = lam_ref[EXT + DEPTH + h, rows(row), :] + lap

    sweep_halo_alone(q3_ref, weights, alone)
    copy.wait()

    def halo(lower, upper):
        for ref, at, far_at in ((lower, 0, 0), (upper, HALF, WIDE - HALF)):
            ext_at = ext_of_halo(at)
            value = lam2_halo[at : at + HALF] + ref[0:HALF].astype(f32)
            lam2_halo[at : at + HALF] = value
            buf2[ext_at + HALF : ext_at + 2 * HALF, inner, :] = value * speed_ext[ext_at : ext_at + HALF]
            buf2[far_at : far_at + HALF, inner, :] = ref[HALF : 2 * HALF].astype(f32)

    by_side(par, got_a, got_b, halo)
    buf2[2 * HALF : 2 * HALF + DEPTH, inner, :] = lam_ref[EXT : EXT + DEPTH] * speed_ext[HALF : HALF + DEPTH]

    def own_lam1(p, row, lap):
        lam = 2.0 * lam_ref[EXT + p, rows(row), :] - lam_ref[p + HALF, rows(row), :] + lap
        lam = lam + inject_ref[p, rows(row), :]
        late_ref[p, rows(row), :] = lam
        grad_ref[p, rows(row), :] = (
            lam * lap0_ref[p, rows(row), :] + lam_ref[EXT + p, rows(row), :] * lap1_ref[p, rows(row), :]
        )

    sweep_own(buf2, 2 * HALF, weights, own_lam1)

    def halo_u2(h, row, lap):
        e = ext_of_halo(h)
        u2_ref[h, rows(row), :] = base_ref[h, rows(row), :] + speed_ext[e, rows(row), :] * lap

    sweep_halo_alone(u1_ref, weights, halo_u2)
    local, across, along_y = source_place(depth_ref, row_ref)

    @pl.when(((local >= 0) & (local < HALF)) | ((local >= HALF + DEPTH) & (local < EXT)))
    def _():
        add_cell(u2_ref, jnp.where(local < HALF, local, local - DEPTH), across, along_y, wave_ref[0, 1])


def adjoint_last_kernel(
    inject_hbm, late_ref, lam_ref, lam2_halo, buf2, speed_ext, order_hbm, early_ref, buf1, inject_ref, sems
):
    (copy,) = fetch((inject_hbm.at[:, 2:4],), (inject_ref,), sems)
    zero_pads(buf1)
    weights = band()
    buf1[HALF : HALF + DEPTH, PAD : PAD + NX, :] = late_ref[...] * speed_ext[HALF : HALF + DEPTH]
    copy.wait()

    def halo_lam1(h, row, lap):
        e = ext_of_halo(h)
        lam = 2.0 * lam2_halo[h, rows(row), :] - lam_ref[e, rows(row), :] + lap
        lam = lam + inject_ref[e, 0, rows(row), :]
        buf1[e, padded(row), :] = lam * speed_ext[e, rows(row), :]

    sweep_halo(buf2, weights, halo_lam1)

    def own_lam0(p, row, lap):
        lam = 2.0 * late_ref[p, rows(row), :] - lam_ref[EXT + p, rows(row), :] + lap
        early_ref[p, rows(row), :] = lam + inject_ref[p + HALF, 1, rows(row), :]

    sweep_own(buf1, HALF, weights, own_lam0)


def forward_second_kernel(
    depth_ref, row_ref, wave_ref, got_a, got_b, u1_ref, u2_ref, u2_halo_ref, speed_ext, lam3_ref, lam4_ref, grad_ref,
    keep_ref, send_ref, buf2, buf3, total,
):
    par = parity()
    zero_pads(buf2)
    zero_pads(buf3)
    weights = band()
    inner = slice(PAD, PAD + NX)

    def halo(lower, upper):
        for ref, at, far_at in ((lower, 0, 0), (upper, HALF, WIDE - HALF)):
            ext_at = ext_of_halo(at)
            buf2[ext_at + HALF : ext_at + 2 * HALF, inner, :] = u2_halo_ref[at : at + HALF] + ref[0:HALF].astype(f32)
            buf2[far_at : far_at + HALF, inner, :] = ref[HALF : 2 * HALF].astype(f32)

    by_side(par, got_a, got_b, halo)
    buf2[2 * HALF : 2 * HALF + DEPTH, inner, :] = u2_ref[...]

    def step(e, row, lap):
        value = 2.0 * buf2[e + HALF, padded(row), :] - u1_ref[e, padded(row), :]
        buf3[e, padded(row), :] = value + speed_ext[e, rows(row), :] * lap

    sweep_halo(buf2, weights, lambda h, row, lap: step(ext_of_halo(h), row, lap))

    def own_u3(p, row, lap):
        step(p + HALF, row, lap)
        total[p, rows(row), :] = grad_ref[p, rows(row), :] + lap * lam3_ref[p + HALF, rows(row), :]

    sweep_own(buf2, 2 * HALF, weights, own_u3)
    local, across, along_y = source_place(depth_ref, row_ref)

    @pl.when((local >= 0) & (local < EXT))
    def _():
        add_cell(buf3, local, across + PAD, along_y, wave_ref[0, 2])

    def to_gradient(p, row, lap):
        value = total[p, rows(row), :] + lap * lam4_ref[p, rows(row), :]
        total[p, rows(row), :] = grad_scale * value

    sweep_own(buf3, HALF, weights, to_gradient)
    shot = lax.axis_index("shot")
    pair, core = shot // 2, lax.rem(shot, 2)
    for n, half in enumerate((pair, 1 - pair)):
        keep_at = pl.multiple_of((half * 2 + core) * 32, 32)
        send_at = pl.multiple_of((half * 2 + 1 - core) * 32, 32)
        keep_ref[n] = total[:, pl.ds(keep_at, 32), :]
        send_ref[n] = total[:, pl.ds(send_at, 32), :]


def per_device(
    parked, parked_slot, holder_list, speed_sq, adjoint_next, adjoint_now,
    wavelet, src_depth, src_row, rec_depth, rec_row, residuals,
):
    peers = lax.axis_size("dom")
    even = [(i, i ^ 1) for i in range(peers)]
    odd = [(i, ((i + 1) ^ 1) - 1) for i in range(1, peers - 1)]

    def swap(a, b):
        far = lax.ppermute(b, "dom", odd)
        return lax.ppermute(a, "dom", even), far

    lam4, lam5 = adjoint_now[0], adjoint_next[0]
    ext = ((EXT, NX, NY), f32)
    slab = ((DEPTH, NX, NY), f32)
    wide = ((EXT, ROWS, NY), f32)

    def planes(count):
        return ((count, NX, NY), bf16)

    mark = ((8, NY), f32)
    (outgoing,) = call(
        gather_kernel, "gather", [HB] * 2, [((64, 32, NY), bf16)],
        [
            pltpu.VMEM((64 * 32, NY), f32), pltpu.VMEM((1, 64), jnp.int32), pltpu.VMEM((64, 4096), bf16),
            pltpu.SemaphoreType.DMA((5,)),
        ],
        in_hbm(parked_slot[0], parked[0]),
    )
    incoming = lax.all_to_all(outgoing, "dom", split_axis=0, concat_axis=0, tiled=True)
    send_a, send_b = call(
        adjoint_pack_kernel, "adjoint_pack", [HB] * 3, [planes(19)] * 2,
        [pltpu.VMEM(*slab)] * 3 + [pltpu.SemaphoreType.DMA((3,))], in_hbm(lam4, lam5, speed_sq),
    )
    got_a, got_b = swap(send_a, send_b)
    count = rec_depth.shape[0]
    steps = residuals.shape[1]
    inject, order = call(
        inject_kernel, "inject", [VM] * 3, [((EXT, steps, NX, NY), f32), mark],
        [
            pltpu.VMEM((2, steps * NY, count), bf16), pltpu.VMEM((EXT, steps, NX, NY), f32),
            pltpu.SemaphoreType.DMA((EXT // 2 + 1,)),
        ],
        (rec_depth.reshape(1, count), rec_row.reshape(1, count), residuals[0]), us=4,
    )
    fields = pltpu.VMEM((EXT, 2, NX, NY), f32)
    send_a, send_b, lam23, speed_ext, q3 = call(
        adjoint_first_kernel, "adjoint_first", [VM] * 3 + [HB] + [VM] * 2,
        [planes(8)] * 2 + [((EXT + 2 * DEPTH, NX, NY), f32), ext, wide],
        [buffer(WIDE), pltpu.VMEM(*slab), pltpu.VMEM(*slab), fields, pltpu.SemaphoreType.DMA((1,))],
        (lam4, lam5, speed_sq) + in_hbm(inject) + (got_a, got_b),
    )
    back_a, back_b = swap(send_a, send_b)

    mine_a, mine_b = call(
        forward_pack_kernel, "forward_pack", [SM, VM, HB], [planes(12)] * 2, [],
        (holder_list.reshape(64), incoming) + in_hbm(order),
    )
    got_a, got_b = swap(mine_a, mine_b)
    send_a, send_b, u1, u2, base_u, lap0, lap1 = call(
        forward_first_kernel, "forward_first", [SM] * 3 + [VM] * 5,
        [planes(8)] * 2 + [wide, slab, slab, slab, slab],
        [buffer(WIDE), pltpu.VMEM(*ext)],
        (src_depth, src_row, wavelet, mine_a, mine_b, got_a, got_b, speed_ext),
    )
    got_a, got_b = swap(send_a, send_b)
    late, u2_halo, grad, lam2_halo, q2 = call(
        middle_kernel, "middle", [SM] * 3 + [HB] + [VM] * 9, [slab] * 4 + [((WIDE, ROWS, NY), f32)],
        [pltpu.VMEM(*slab), pltpu.SemaphoreType.DMA((1,))],
        (src_depth, src_row, wavelet) + in_hbm(inject)
        + (back_a, back_b, lam23, q3, speed_ext, u1, base_u, lap0, lap1),
    )
    quarter = ((2, DEPTH, NX // 4, NY), f32)
    keep, send = call(
        forward_second_kernel, "forward_second", [SM] * 3 + [VM] * 9, [quarter] * 2,
        [buffer(WIDE), buffer(EXT), pltpu.VMEM(*slab)],
        (src_depth, src_row, wavelet, got_a, got_b, u1, u2, u2_halo, speed_ext, lam23, lam4, grad),
    )
    got = lax.ppermute(send, "shot", [(0, 1), (1, 0), (2, 3), (3, 2)])
    part = keep[1] + got[1]
    other = lax.ppermute(part, "shot", [(0, 2), (2, 0), (1, 3), (3, 1)])
    (early,) = call(
        adjoint_last_kernel, "adjoint_last", [HB] + [VM] * 5 + [HB], [slab],
        [buffer(EXT), fields, pltpu.SemaphoreType.DMA((1,))],
        in_hbm(inject) + (late, lam23, lam2_halo, q2, speed_ext) + in_hbm(part),
    )
    gradient = keep[0] + got[0] + other
    return (gradient, late[None], early[None])


def solution(mesh):
    in_specs = (
        P("shot", "dom", None),
        P("shot", "dom", None),
        P("shot", "dom", None),
        P("dom", None, None),
        P("shot", "dom", None, None),
        P("shot", "dom", None, None),
        P("shot", None),
        P("shot"),
        P("shot"),
        P(),
        P(),
        P("shot", None, None),
    )
    out_specs = (P("dom", "shot", None), P("shot", "dom", None, None), P("shot", "dom", None, None))
    return jax.shard_map(
        per_device, mesh=mesh, in_specs=in_specs, out_specs=out_specs, check_vma=False
    )
```

```python
import functools

import jax
import jax.numpy as jnp
from jax import lax
from jax.experimental import pallas as pl
from jax.experimental.pallas import tpu as pltpu
from jax.sharding import PartitionSpec as P

stencil_coef = (-205.0 / 72.0, 8.0 / 5.0, -1.0 / 5.0, 8.0 / 315.0, -1.0 / 560.0)
grad_scale = 0.0625

DEPTH = 8
HALF = 4
EXT = DEPTH + 2 * HALF
WIDE = DEPTH + 4 * HALF
NX = 128
NY = 128
PAD = 8
ROWS = NX + 2 * PAD
CHUNK = 32
GROUP = 4
bf16 = jnp.bfloat16
f32 = jnp.float32

VM = pl.BlockSpec(memory_space=pltpu.VMEM)
SM = pl.BlockSpec(memory_space=pltpu.SMEM)
HB = pl.BlockSpec(memory_space=pltpu.HBM)


def in_hbm(*arrays):
    return tuple(pltpu.with_memory_space_constraint(a, pltpu.HBM) for a in arrays)


def fetch(sources, targets, sems):
    copies = [pltpu.make_async_copy(src, dst, sems.at[n]) for n, (src, dst) in enumerate(zip(sources, targets))]
    for copy in copies:
        copy.start()
    return copies


def call(kernel, name, ins, outs, scratch, args, us=2, limit=20 << 20, out=VM):
    return pl.pallas_call(
        kernel,
        name=name,
        out_shape=[pltpu.HBM(*o) if out is HB else jax.ShapeDtypeStruct(*o) for o in outs],
        in_specs=ins,
        out_specs=[out] * len(outs),
        scratch_shapes=scratch,
        compiler_params=pltpu.CompilerParams(vmem_limit_bytes=limit),
        cost_estimate=pl.CostEstimate(flops=us * 10**9, bytes_accessed=us * 3_600_000, transcendentals=0),
    )(*args)


def buffer(planes):
    return pltpu.VMEM((planes, ROWS, NY), f32)


def zero_pads(buf):
    zeros = jnp.zeros((buf.shape[0], PAD, NY), f32)
    buf[:, 0:PAD, :] = zeros
    buf[:, PAD + NX : ROWS, :] = zeros


def band():
    apart = jnp.abs(
        lax.broadcasted_iota(jnp.int32, (NY, NY), 0) - lax.broadcasted_iota(jnp.int32, (NY, NY), 1)
    )
    weights = jnp.zeros((NY, NY), f32)
    for k in range(1, HALF + 1):
        weights = jnp.where(apart == k, 5.0 * stencil_coef[k], weights)
    head = weights.astype(bf16)
    rest = (weights - head.astype(f32)).astype(bf16)
    both = jnp.concatenate([head, rest], axis=1)
    return jnp.concatenate([both, both], axis=0), head


def along(plane, weights):
    both, head = weights
    first = plane.astype(bf16)
    left = plane - first.astype(f32)
    second = left.astype(bf16)
    third = (left - second.astype(f32)).astype(bf16)
    pair = jnp.dot(jnp.concatenate([first, second], axis=1), both, preferred_element_type=f32)
    return 0.2 * (pair[:, :NY] + pair[:, NY:] + jnp.dot(third, head, preferred_element_type=f32))


def rows(row):
    return slice(row, row + CHUNK)


def padded(row):
    return slice(PAD + row, PAD + row + CHUNK)


def group_laps(buf, first, weights, body):
    static = isinstance(first, int)
    parts = [along(buf[first + j, PAD : PAD + NX, :], weights) for j in range(GROUP)]
    for j in range(GROUP):
        at = first + j
        for row in range(0, NX, CHUNK):
            base = PAD + row
            lap = (3.0 * stencil_coef[0]) * buf[at, padded(row), :] + parts[j][row : row + CHUNK]
            for k in range(1, HALF + 1):
                near = buf[at, base + k : base + k + CHUNK, :] + buf[at, base - k : base - k + CHUNK, :]
                for q in (at + k, at - k):
                    if not static or 0 <= q < buf.shape[0]:
                        near = near + buf[q, padded(row), :]
                lap = lap + stencil_coef[k] * near
            body(j, row, lap)


def sweep_own(buf, shift, weights, body):
    @pl.loop(0, DEPTH // GROUP)
    def _(g):
        group_laps(buf, g * GROUP + shift, weights, lambda j, row, lap: body(g * GROUP + j, row, lap))


def sweep_halo(buf, weights, body):
    @pl.loop(0, 2)
    def _(g):
        group_laps(
            buf, HALF + g * (HALF + DEPTH), weights, lambda j, row, lap: body(g * GROUP + j, row, lap)
        )


def sweep_halo_alone(buf, weights, body):
    for g in range(2):
        group_laps(
            buf, g * (HALF + DEPTH), weights, lambda j, row, lap, g=g: body(g * GROUP + j, row, lap)
        )


def sweep_own_alone(buf, weights, body):
    for g in range(DEPTH // GROUP):
        group_laps(buf, g * GROUP, weights, lambda j, row, lap, g=g: body(g * GROUP + j, row, lap))


def fill_side(buf, upper, near, far, own):
    inner = slice(PAD, PAD + NX)
    for j in range(HALF):
        buf[HALF + j, inner, :] = near(j)
        buf[2 * HALF + j if upper else j, inner, :] = far(j)
        buf[j if upper else 2 * HALF + j, inner, :] = own(HALF + j if upper else j)


def side_terms(buf, upper, p, row):
    total = None
    for k in range(1, HALF + 1):
        q = p - HALF + k if upper else 2 * HALF + p - k
        if HALF <= q < 2 * HALF:
            term = stencil_coef[k] * buf[q, padded(row), :]
            total = term if total is None else total + term
    return total


def side_planes(upper):
    return range(HALF, DEPTH) if upper else range(HALF)


def ext_of_halo(h):
    return h + DEPTH * (h // HALF) if isinstance(h, int) else jnp.where(h < HALF, h, h + DEPTH)


def add_cell(ref, plane, row, column, amount):
    lane = lax.broadcasted_iota(jnp.int32, (1, NY), 1)
    old = ref[plane, pl.ds(row, 1), :]
    ref[plane, pl.ds(row, 1), :] = old + jnp.where(lane == column, amount, 0.0)


def parity():
    return lax.rem(lax.axis_index("dom"), 2)


def by_side(par, first, second, body):
    @pl.when(par == 0)
    def _():
        body(second, first)

    @pl.when(par == 1)
    def _():
        body(first, second)


def gather_kernel(slot_hbm, parked_hbm, out_hbm, held, slot_ref, parked_ref, staged, sems, out_sems):
    count, parts = parked_ref.shape[0], 4
    width, lines = parked_ref.shape[1] // parts, 32 // parts
    columns = [pl.ds(width * n, width) for n in range(parts)]
    slots, *copies = fetch(
        [slot_hbm] + [parked_hbm.at[:, c] for c in columns], [slot_ref] + [parked_ref.at[:, c] for c in columns], sems
    )
    slots.wait()
    row = lax.broadcasted_iota(jnp.int32, (count, count), 0)
    pick = jnp.where(row == slot_ref[...], 1.0, 0.0).astype(bf16)
    stores = []
    for n in range(parts):
        copies[n].wait()
        for line in range(lines):
            at = n * width + line * NY
            held[n, pl.ds(line, count, stride=lines), :] = lax.dot_general(
                pick, parked_ref[:, at : at + NY], (((0,), (0,)), ((), ())), preferred_element_type=f32
            )
        staged[n] = held[n].reshape(count, lines, NY).astype(bf16)
        stores.append(pltpu.make_async_copy(staged.at[n], out_hbm.at[:, pl.ds(n * lines, lines)], out_sems.at[n]))
        stores[-1].start()
    for store in stores:
        store.wait()


def adjoint_pack_kernel(now_hbm, next_hbm, speed_hbm, first_ref, second_ref, now_ref, next_ref, speed_ref, sems):
    fields = (now_ref, next_ref, speed_ref)
    for copy in fetch((now_hbm, next_hbm, speed_hbm), fields, sems):
        copy.wait()
    par = parity()
    for out_ref, near in ((first_ref, HALF * (1 - par)), (second_ref, HALF * par)):
        far = HALF - near
        close = near + 3 * (near // HALF)
        for n, ref in enumerate(fields):
            out_ref[pl.ds(HALF * n, HALF)] = ref[pl.ds(near, HALF)].astype(bf16)
            value = ref[pl.ds(close, 1)]
            out_ref[pl.ds(4 * HALF + n, 1)] = (value - value.astype(bf16).astype(f32)).astype(bf16)
        out_ref[pl.ds(3 * HALF, HALF)] = (now_ref[pl.ds(far, HALF)] * speed_ref[pl.ds(far, HALF)]).astype(bf16)


def inject_kernel(depth_ref, row_ref, amount_ref, out_hbm, mark_hbm, table, fields, sems):
    top = lax.axis_index("dom") * DEPTH - HALF
    count = depth_ref.shape[1]
    steps = amount_ref.shape[0]
    local = depth_ref[...] - top
    place = row_ref[...]
    key = jnp.where((local >= 0) & (local < EXT), local * NX + place // NY, -1)
    hit = lax.broadcasted_iota(jnp.int32, (NY, count), 0) == lax.rem(place, NY)
    for k in range(steps):
        amount = amount_ref[k : k + 1, :]
        head = amount.astype(bf16).astype(f32)
        table[0, k * NY : (k + 1) * NY, :] = jnp.where(hit, head, 0.0).astype(bf16)
        table[1, k * NY : (k + 1) * NY, :] = jnp.where(hit, amount - head, 0.0).astype(bf16)
    planes = 2
    cell = lax.broadcasted_iota(jnp.int32, (planes * NX, count), 0)

    def store(g):
        at = pl.ds(g * planes, planes)
        return pltpu.make_async_copy(fields.at[at], out_hbm.at[at], sems.at[g])

    @pl.loop(0, EXT // planes)
    def _(g):
        pick = jnp.where(cell + g * (planes * NX) == key, 1.0, 0.0).astype(bf16)
        field = lax.dot_general(
            pick, table[0], (((1,), (1,)), ((), ())), preferred_element_type=f32
        ) + lax.dot_general(pick, table[1], (((1,), (1,)), ((), ())), preferred_element_type=f32)
        for k in range(steps):
            for j in range(planes):
                fields[g * planes + j, k] = field[j * NX : (j + 1) * NX, k * NY : (k + 1) * NY]
        store(g).start()

    mark = pltpu.make_async_copy(fields.at[0, 0, 0:8], mark_hbm, sems.at[EXT // planes])
    mark.start()
    for g in range(EXT // planes):
        store(g).wait()
    mark.wait()


def send_second(par, buf, far_ref, speed_ext, scale_far, first_ref, second_ref):
    def emit(lower, upper):
        for p in range(DEPTH):
            near_ref, other_ref = (upper, lower) if p >= HALF else (lower, upper)
            for row in range(0, NX, CHUNK):
                total = None
                for k in range(1, HALF + 1):
                    q = p - k if p >= HALF else p + k
                    if (p >= HALF) == (q >= HALF):
                        continue
                    term = stencil_coef[k] * buf[q + HALF, padded(row), :]
                    total = term if total is None else total + term
                fresh = far_ref[p, rows(row), :]
                if scale_far:
                    fresh = fresh * speed_ext[p + HALF, rows(row), :]
                else:
                    total = total * speed_ext[p + HALF, rows(row), :]
                near_ref[p % HALF, rows(row), :] = total.astype(bf16)
                other_ref[HALF + p % HALF, rows(row), :] = fresh.astype(bf16)

    by_side(par, first_ref, second_ref, emit)


def adjoint_side(ref, upper, now_ref, speed_ref, inject_ref, side, buf, weights, store):
    now, after, speed = side
    close = 0 if upper else HALF - 1
    for n, held in enumerate(side):
        held[...] = ref[HALF * n : HALF * n + HALF].astype(f32)
        held[close] = held[close] + ref[4 * HALF + n].astype(f32)
    fill_side(
        buf,
        upper,
        lambda j: now[j] * speed[j],
        lambda j: ref[3 * HALF + j].astype(f32),
        lambda p: now_ref[p] * speed_ref[p],
    )
    first = HALF + DEPTH if upper else 0

    def body(j, row, lap):
        here = now[j, rows(row), :]
        lam = 2.0 * here - after[j, rows(row), :] + lap + inject_ref[first + j, 0, rows(row), :]
        base = 2.0 * lam - here + inject_ref[first + j, 1, rows(row), :]
        store(j, row, lam, base, speed[j, rows(row), :])

    group_laps(buf, HALF, weights, body)


def adjoint_side_kernel(
    now_ref, next_ref, speed_ref, inject_hbm, got_a, out_ref, part_ref, mark_ref,
    own, buf, now_side, next_side, speed_side, inject_ref, sems,
):
    par = parity()
    (copy,) = fetch((inject_hbm.at[:, 0:2],), (inject_ref,), sems)
    mark_ref[...] = jnp.zeros(mark_ref.shape, f32)
    zero_pads(own)
    zero_pads(buf)
    weights = band()
    own[:, PAD : PAD + NX, :] = now_ref[...] * speed_ref[...]

    def alone(p, row, lap):
        part_ref[p, rows(row), :] = 2.0 * now_ref[p, rows(row), :] - next_ref[p, rows(row), :] + lap

    sweep_own_alone(own, weights, alone)
    copy.wait()
    part_ref[...] = part_ref[...] + inject_ref[HALF : HALF + DEPTH, 0]

    def store(j, row, lam, base, speed):
        for n, value in enumerate((lam, base, speed, lam * speed)):
            out_ref[n * HALF + j, rows(row), :] = value

    def one(upper):
        side = (now_side, next_side, speed_side)
        adjoint_side(got_a, upper, now_ref, speed_ref, inject_ref, side, buf, weights, store)
        for p in side_planes(upper):
            for row in range(0, NX, CHUNK):
                part_ref[p, rows(row), :] = part_ref[p, rows(row), :] + side_terms(buf, upper, p, row)

    by_parity(par, one)


def by_parity(par, one):
    @pl.when(par == 0)
    def _():
        one(True)

    @pl.when(par == 1)
    def _():
        one(False)


def adjoint_first_kernel(
    now_ref, speed_ref, inject_hbm, side_ref, part_ref, got_b, order_ref,
    first_ref, second_ref, lam_ref, speed_ext, q3_ref,
    buf, now_side, next_side, speed_side, inject_ref, sems,
):
    par = parity()
    (copy,) = fetch((inject_hbm.at[:, 0:2],), (inject_ref,), sems)
    zero_pads(buf)
    zero_pads(q3_ref)
    weights = band()
    own = slice(HALF, HALF + DEPTH)
    inner = slice(PAD, PAD + NX)
    speed_ext[own] = speed_ref[...]
    copy.wait()

    def one(upper_a):
        ext_a, halo_a = (HALF + DEPTH, HALF) if upper_a else (0, 0)
        lam_ref[ext_a : ext_a + HALF] = side_ref[0:HALF]
        lam_ref[EXT + DEPTH + halo_a : EXT + DEPTH + halo_a + HALF] = side_ref[HALF : 2 * HALF]
        speed_ext[ext_a : ext_a + HALF] = side_ref[2 * HALF : 3 * HALF]
        q3_ref[ext_a : ext_a + HALF, inner, :] = side_ref[3 * HALF : 4 * HALF]
        upper = not upper_a
        ext_b, halo_b = (HALF + DEPTH, HALF) if upper else (0, 0)

        def store(j, row, lam, base, speed):
            lam_ref[ext_b + j, rows(row), :] = lam
            lam_ref[EXT + DEPTH + halo_b + j, rows(row), :] = base
            speed_ext[ext_b + j, rows(row), :] = speed
            q3_ref[ext_b + j, padded(row), :] = lam * speed

        side = (now_side, next_side, speed_side)
        adjoint_side(got_b, upper, now_ref, speed_ref, inject_ref, side, buf, weights, store)
        for p in range(DEPTH):
            for row in range(0, NX, CHUNK):
                lam = part_ref[p, rows(row), :]
                if p in side_planes(upper):
                    lam = lam + side_terms(buf, upper, p, row)
                lam_ref[p + HALF, rows(row), :] = lam
                q3_ref[p + HALF, padded(row), :] = lam * speed_ref[p, rows(row), :]

    by_parity(par, one)

    def own_lam2(p, row, lap):
        lam = 2.0 * lam_ref[p + HALF, rows(row), :] - now_ref[p, rows(row), :] + lap
        lam_ref[EXT + p, rows(row), :] = lam + inject_ref[p + HALF, 1, rows(row), :]

    sweep_own(q3_ref, HALF, weights, own_lam2)
    send_second(par, q3_ref, lam_ref.at[EXT : EXT + DEPTH], speed_ext, True, first_ref, second_ref)


def forward_pack_kernel(holder_ref, pieces_ref, order_ref, first_ref, second_ref):
    par = parity()
    per_plane = NX // 32
    for p in range(DEPTH):
        for j in range(per_plane):
            piece = pieces_ref[holder_ref[(DEPTH + p) * per_plane + j]]
            first_ref[HALF + p, 32 * j : 32 * j + 32, :] = piece
            second_ref[HALF + p, 32 * j : 32 * j + 32, :] = piece
    at = HALF * (1 - par)
    for p in range(HALF):
        for j in range(per_plane):
            first_ref[p, 32 * j : 32 * j + 32, :] = pieces_ref[holder_ref[(at + p) * per_plane + j]]
            second_ref[p, 32 * j : 32 * j + 32, :] = pieces_ref[holder_ref[(HALF - at + p) * per_plane + j]]


def source_place(depth_ref, row_ref):
    local = depth_ref[0] - (lax.axis_index("dom") * DEPTH - HALF)
    return local, row_ref[0] // NY, lax.rem(row_ref[0], NY)


def forward_own_kernel(mine_ref, order_ref, own_ref, part_ref, mark_ref):
    mark_ref[...] = jnp.zeros(mark_ref.shape, f32)
    zero_pads(own_ref)
    own_ref[:, PAD : PAD + NX, :] = mine_ref[HALF : HALF + DEPTH].astype(f32)

    def alone(p, row, lap):
        part_ref[p, rows(row), :] = lap

    sweep_own_alone(own_ref, band(), alone)


def forward_first_kernel(
    depth_ref, row_ref, wave_ref, mine_a, mine_b, own_ref, part_ref, got_a, got_b, speed_ext,
    first_ref, second_ref, u1_ref, u2_ref, base_ref, lap0_ref, lap1_ref,
    below, above, prev_own,
):
    par = parity()
    zero_pads(below)
    zero_pads(above)
    zero_pads(u1_ref)
    weights = band()
    inner = slice(PAD, PAD + NX)
    prev_own[pl.ds(HALF * (1 - par), HALF)] = mine_a[0:HALF].astype(f32)
    prev_own[pl.ds(HALF * par, HALF)] = mine_b[0:HALF].astype(f32)

    def halo(lower, upper):
        for ref, buf, is_upper in ((lower, below, False), (upper, above, True)):
            near_at, far_at = (HALF, 2 * HALF) if is_upper else (2 * HALF, HALF)
            fill_side(
                buf,
                is_upper,
                lambda j, ref=ref, at=near_at: ref[at + j].astype(f32),
                lambda j, ref=ref, at=far_at: ref[at + j].astype(f32),
                lambda p: own_ref[p, inner, :],
            )
            first, at = (HALF + DEPTH, HALF) if is_upper else (0, 0)

            def body(j, row, lap, ref=ref, buf=buf, first=first, at=at):
                now = buf[HALF + j, padded(row), :]
                value = 2.0 * now - ref[j, rows(row), :].astype(f32) + speed_ext[first + j, rows(row), :] * lap
                u1_ref[first + j, padded(row), :] = value
                base_ref[at + j, rows(row), :] = 2.0 * value - now

            group_laps(buf, HALF, weights, body)

    by_side(par, got_a, got_b, halo)
    for p in range(DEPTH):
        upper = p >= HALF
        for row in range(0, NX, CHUNK):
            lap = part_ref[p, rows(row), :] + side_terms(above if upper else below, upper, p, row)
            lap0_ref[p, rows(row), :] = lap
            value = 2.0 * own_ref[p, padded(row), :] - prev_own[p, rows(row), :]
            u1_ref[p + HALF, padded(row), :] = value + speed_ext[p + HALF, rows(row), :] * lap
    local, across, along_y = source_place(depth_ref, row_ref)
    outside = ((local >= 0) & (local < HALF)) | ((local >= HALF + DEPTH) & (local < EXT))

    @pl.when((local >= 0) & (local < EXT))
    def _():
        add_cell(u1_ref, local, across + PAD, along_y, wave_ref[0, 0])

    @pl.when(outside)
    def _():
        add_cell(base_ref, jnp.where(local < HALF, local, local - DEPTH), across, along_y, 2.0 * wave_ref[0, 0])

    def own_u2(p, row, lap):
        value = 2.0 * u1_ref[p + HALF, padded(row), :] - own_ref[p, padded(row), :]
        u2_ref[p, rows(row), :] = value + speed_ext[p + HALF, rows(row), :] * lap
        lap1_ref[p, rows(row), :] = lap

    sweep_own(u1_ref, HALF, weights, own_u2)

    @pl.when((local >= HALF) & (local < HALF + DEPTH))
    def _():
        add_cell(u2_ref, local - HALF, across, along_y, wave_ref[0, 1])

    send_second(par, u1_ref, u2_ref, speed_ext, False, first_ref, second_ref)


def middle_kernel(
    depth_ref, row_ref, wave_ref, inject_hbm, got_a, got_b, lam_ref, q3_ref, speed_ext, u1_ref, u2_own, base_ref, lap0_ref, lap1_ref,
    late_ref, u2_ref, grad_ref, lam2_halo, buf2, own_ref, part_ref,
    inject_ref, sems,
):
    par = parity()
    (copy,) = fetch((inject_hbm.at[HALF : HALF + DEPTH, 2],), (inject_ref,), sems)
    zero_pads(buf2)
    weights = band()
    inner = slice(PAD, PAD + NX)

    def alone(h, row, lap):
        lam2_halo[h, rows(row), :] = lam_ref[EXT + DEPTH + h, rows(row), :] + lap

    sweep_halo_alone(q3_ref, weights, alone)
    copy.wait()

    def halo(lower, upper):
        for ref, at, far_at in ((lower, 0, 0), (upper, HALF, WIDE - HALF)):
            ext_at = ext_of_halo(at)
            value = lam2_halo[at : at + HALF] + ref[0:HALF].astype(f32)
            lam2_halo[at : at + HALF] = value
            buf2[ext_at + HALF : ext_at + 2 * HALF, inner, :] = value * speed_ext[ext_at : ext_at + HALF]
            buf2[far_at : far_at + HALF, inner, :] = ref[HALF : 2 * HALF].astype(f32)

    by_side(par, got_a, got_b, halo)
    buf2[2 * HALF : 2 * HALF + DEPTH, inner, :] = lam_ref[EXT : EXT + DEPTH] * speed_ext[HALF : HALF + DEPTH]

    def own_lam1(p, row, lap):
        lam = 2.0 * lam_ref[EXT + p, rows(row), :] - lam_ref[p + HALF, rows(row), :] + lap
        lam = lam + inject_ref[p, rows(row), :]
        late_ref[p, rows(row), :] = lam
        grad_ref[p, rows(row), :] = (
            lam * lap0_ref[p, rows(row), :] + lam_ref[EXT + p, rows(row), :] * lap1_ref[p, rows(row), :]
        )

    sweep_own(buf2, 2 * HALF, weights, own_lam1)

    def halo_u2(h, row, lap):
        e = ext_of_halo(h)
        u2_ref[h, rows(row), :] = base_ref[h, rows(row), :] + speed_ext[e, rows(row), :] * lap

    sweep_halo_alone(u1_ref, weights, halo_u2)
    local, across, along_y = source_place(depth_ref, row_ref)

    @pl.when(((local >= 0) & (local < HALF)) | ((local >= HALF + DEPTH) & (local < EXT)))
    def _():
        add_cell(u2_ref, jnp.where(local < HALF, local, local - DEPTH), across, along_y, wave_ref[0, 1])

    zero_pads(own_ref)
    own_ref[:, inner, :] = u2_own[...]

    def u2_alone(p, row, lap):
        part_ref[p, rows(row), :] = lap

    sweep_own_alone(own_ref, weights, u2_alone)


def adjoint_last_kernel(
    inject_hbm, late_ref, lam_ref, lam2_halo, buf2, speed_ext, order_ref, early_ref, buf1, inject_ref, sems
):
    (copy,) = fetch((inject_hbm.at[:, 2:4],), (inject_ref,), sems)
    zero_pads(buf1)
    weights = band()
    buf1[HALF : HALF + DEPTH, PAD : PAD + NX, :] = late_ref[...] * speed_ext[HALF : HALF + DEPTH]
    copy.wait()

    def halo_lam1(h, row, lap):
        e = ext_of_halo(h)
        lam = 2.0 * lam2_halo[h, rows(row), :] - lam_ref[e, rows(row), :] + lap
        lam = lam + inject_ref[e, 0, rows(row), :]
        buf1[e, padded(row), :] = lam * speed_ext[e, rows(row), :]

    sweep_halo(buf2, weights, halo_lam1)

    def own_lam0(p, row, lap):
        lam = 2.0 * late_ref[p, rows(row), :] - lam_ref[EXT + p, rows(row), :] + lap
        early_ref[p, rows(row), :] = lam + inject_ref[p + HALF, 1, rows(row), :]

    sweep_own(buf1, HALF, weights, own_lam0)


def forward_second_kernel(
    depth_ref, row_ref, wave_ref, got_a, got_b, u1_ref, own_ref, part_ref, u2_halo_ref, speed_ext, lam_ref, lam4_ref,
    grad_ref, keep_ref, send_ref, below, above, buf3, total,
):
    par = parity()
    zero_pads(below)
    zero_pads(above)
    zero_pads(buf3)
    weights = band()
    inner = slice(PAD, PAD + NX)

    def halo(lower, upper):
        for ref, buf, is_upper in ((lower, below, False), (upper, above, True)):
            first, at = (HALF + DEPTH, HALF) if is_upper else (0, 0)
            fill_side(
                buf,
                is_upper,
                lambda j, ref=ref, at=at: u2_halo_ref[at + j] + ref[j].astype(f32),
                lambda j, ref=ref: ref[HALF + j].astype(f32),
                lambda p: own_ref[p, inner, :],
            )

            def body(j, row, lap, buf=buf, first=first):
                value = 2.0 * buf[HALF + j, padded(row), :] - u1_ref[first + j, padded(row), :]
                buf3[first + j, padded(row), :] = value + speed_ext[first + j, rows(row), :] * lap

            group_laps(buf, HALF, weights, body)

    by_side(par, got_a, got_b, halo)
    for p in range(DEPTH):
        upper = p >= HALF
        e = p + HALF
        for row in range(0, NX, CHUNK):
            lap = part_ref[p, rows(row), :] + side_terms(above if upper else below, upper, p, row)
            value = 2.0 * own_ref[p, padded(row), :] - u1_ref[e, padded(row), :]
            buf3[e, padded(row), :] = value + speed_ext[e, rows(row), :] * lap
            total[p, rows(row), :] = grad_ref[p, rows(row), :] + lap * lam_ref[e, rows(row), :]
    local, across, along_y = source_place(depth_ref, row_ref)

    @pl.when((local >= 0) & (local < EXT))
    def _():
        add_cell(buf3, local, across + PAD, along_y, wave_ref[0, 2])

    def to_gradient(p, row, lap):
        value = total[p, rows(row), :] + lap * lam4_ref[p, rows(row), :]
        total[p, rows(row), :] = grad_scale * value

    sweep_own(buf3, HALF, weights, to_gradient)
    shot = lax.axis_index("shot")
    pair, core = shot // 2, lax.rem(shot, 2)
    for n, half in enumerate((pair, 1 - pair)):
        keep_at = pl.multiple_of((half * 2 + core) * 32, 32)
        send_at = pl.multiple_of((half * 2 + 1 - core) * 32, 32)
        keep_ref[n] = total[:, pl.ds(keep_at, 32), :]
        send_ref[n] = total[:, pl.ds(send_at, 32), :]


def per_device(
    parked, parked_slot, holder_list, speed_sq, adjoint_next, adjoint_now,
    wavelet, src_depth, src_row, rec_depth, rec_row, residuals,
):
    peers = lax.axis_size("dom")
    even = [(i, i ^ 1) for i in range(peers)]
    odd = [(i, ((i + 1) ^ 1) - 1) for i in range(1, peers - 1)]

    def swap(a, b):
        far = lax.ppermute(b, "dom", odd)
        return lax.ppermute(a, "dom", even), far

    lam4, lam5 = adjoint_now[0], adjoint_next[0]
    ext = ((EXT, NX, NY), f32)
    slab = ((DEPTH, NX, NY), f32)
    wide = ((EXT, ROWS, NY), f32)

    def planes(count):
        return ((count, NX, NY), bf16)

    mark = ((8, NY), f32)
    (outgoing,) = call(
        gather_kernel, "gather", [HB] * 2, [((64, 32, NY), bf16)],
        [
            pltpu.VMEM((4, 64 * 8, NY), f32), pltpu.VMEM((1, 64), jnp.int32), pltpu.VMEM((64, 4096), bf16),
            pltpu.VMEM((4, 64, 8, NY), bf16), pltpu.SemaphoreType.DMA((5,)), pltpu.SemaphoreType.DMA((4,)),
        ],
        in_hbm(parked_slot[0], parked[0]), out=HB,
    )
    incoming = lax.all_to_all(outgoing, "dom", split_axis=0, concat_axis=0, tiled=True)
    send_a, send_b = call(
        adjoint_pack_kernel, "adjoint_pack", [HB] * 3, [planes(19)] * 2,
        [pltpu.VMEM(*slab)] * 3 + [pltpu.SemaphoreType.DMA((3,))], in_hbm(lam4, lam5, speed_sq),
    )
    got_a, got_b = swap(send_a, send_b)
    count = rec_depth.shape[0]
    steps = residuals.shape[1]
    inject, order = call(
        inject_kernel, "inject", [VM] * 3, [((EXT, steps, NX, NY), f32), mark],
        [
            pltpu.VMEM((2, steps * NY, count), bf16), pltpu.VMEM((EXT, steps, NX, NY), f32),
            pltpu.SemaphoreType.DMA((EXT // 2 + 1,)),
        ],
        (rec_depth.reshape(1, count), rec_row.reshape(1, count), residuals[0]), us=4, out=HB,
    )
    fields = pltpu.VMEM((EXT, 2, NX, NY), f32)
    trio = ((3 * HALF, ROWS, NY), f32)
    four = pltpu.VMEM((HALF, NX, NY), f32)
    own_wide = ((DEPTH, ROWS, NY), f32)
    mine_a, mine_b = call(
        forward_pack_kernel, "forward_pack", [SM, VM, HB], [planes(12)] * 2, [],
        (holder_list.reshape(64), incoming) + in_hbm(order),
    )
    side, part, order = call(
        adjoint_side_kernel, "adjoint_side", [VM] * 3 + [HB, VM], [((4 * HALF, NX, NY), f32), slab, mark],
        [buffer(DEPTH), pltpu.VMEM(*trio), four, four, four, fields, pltpu.SemaphoreType.DMA((1,))],
        (lam4, lam5, speed_sq) + in_hbm(inject) + (got_a,),
    )
    own0, lap0_part, order = call(
        forward_own_kernel, "forward_own", [VM, VM], [own_wide, slab, mark], [], (mine_a, order),
    )
    send_a, send_b, lam23, speed_ext, q3 = call(
        adjoint_first_kernel, "adjoint_first", [VM] * 2 + [HB] + [VM] * 4,
        [planes(8)] * 2 + [((EXT + 2 * DEPTH, NX, NY), f32), ext, wide],
        [pltpu.VMEM(*trio), four, four, four, fields, pltpu.SemaphoreType.DMA((1,))],
        (lam4, speed_sq) + in_hbm(inject) + (side, part, got_b, order),
    )
    back_a, back_b = swap(send_a, send_b)

    got_a, got_b = swap(mine_a, mine_b)
    send_a, send_b, u1, u2, base_u, lap0, lap1 = call(
        forward_first_kernel, "forward_first", [SM] * 3 + [VM] * 7,
        [planes(8)] * 2 + [wide, slab, slab, slab, slab],
        [pltpu.VMEM(*trio), pltpu.VMEM(*trio), pltpu.VMEM(*slab)],
        (src_depth, src_row, wavelet, mine_a, mine_b, own0, lap0_part, got_a, got_b, speed_ext),
    )
    got_a, got_b = swap(send_a, send_b)
    late, u2_halo, grad, lam2_halo, q2, own2, lap2_part = call(
        middle_kernel, "middle", [SM] * 3 + [HB] + [VM] * 10,
        [slab] * 4 + [((WIDE, ROWS, NY), f32), own_wide, slab],
        [pltpu.VMEM(*slab), pltpu.SemaphoreType.DMA((1,))],
        (src_depth, src_row, wavelet) + in_hbm(inject)
        + (back_a, back_b, lam23, q3, speed_ext, u1, u2, base_u, lap0, lap1),
    )
    quarter = ((2, DEPTH, NX // 4, NY), f32)
    keep, send = call(
        forward_second_kernel, "forward_second", [SM] * 3 + [VM] * 10, [quarter] * 2,
        [pltpu.VMEM(*trio), pltpu.VMEM(*trio), buffer(EXT), pltpu.VMEM(*slab)],
        (src_depth, src_row, wavelet, got_a, got_b, u1, own2, lap2_part, u2_halo, speed_ext, lam23, lam4, grad),
    )
    got = lax.ppermute(send, "shot", [(0, 1), (1, 0), (2, 3), (3, 2)])
    part = keep[1] + got[1]
    other = lax.ppermute(part, "shot", [(0, 2), (2, 0), (1, 3), (3, 1)])
    (early,) = call(
        adjoint_last_kernel, "adjoint_last", [HB] + [VM] * 6, [slab],
        [buffer(EXT), fields, pltpu.SemaphoreType.DMA((1,))],
        in_hbm(inject) + (late, lam23, lam2_halo, q2, speed_ext, part),
    )
    gradient = keep[0] + got[0] + other
    return (gradient, late[None], early[None])


def solution(mesh):
    in_specs = (
        P("shot", "dom", None),
        P("shot", "dom", None),
        P("shot", "dom", None),
        P("dom", None, None),
        P("shot", "dom", None, None),
        P("shot", "dom", None, None),
        P("shot", None),
        P("shot"),
        P("shot"),
        P(),
        P(),
        P("shot", None, None),
    )
    out_specs = (P("dom", "shot", None), P("shot", "dom", None, None), P("shot", "dom", None, None))
    return jax.shard_map(
        per_device, mesh=mesh, in_specs=in_specs, out_specs=out_specs, check_vma=False
    )
```

```python
import functools

import jax
import jax.numpy as jnp
from jax import lax
from jax.experimental import pallas as pl
from jax.experimental.pallas import tpu as pltpu
from jax.sharding import PartitionSpec as P

stencil_coef = (-205.0 / 72.0, 8.0 / 5.0, -1.0 / 5.0, 8.0 / 315.0, -1.0 / 560.0)
grad_scale = 0.0625

DEPTH = 8
HALF = 4
EXT = DEPTH + 2 * HALF
WIDE = DEPTH + 4 * HALF
NX = 128
NY = 128
PAD = 8
ROWS = NX + 2 * PAD
CHUNK = 32
GROUP = 4
bf16 = jnp.bfloat16
f32 = jnp.float32

VM = pl.BlockSpec(memory_space=pltpu.VMEM)
SM = pl.BlockSpec(memory_space=pltpu.SMEM)
HB = pl.BlockSpec(memory_space=pltpu.HBM)


def in_hbm(*arrays):
    return tuple(pltpu.with_memory_space_constraint(a, pltpu.HBM) for a in arrays)


def fetch(sources, targets, sems):
    copies = [pltpu.make_async_copy(src, dst, sems.at[n]) for n, (src, dst) in enumerate(zip(sources, targets))]
    for copy in copies:
        copy.start()
    return copies


def call(kernel, name, ins, outs, scratch, args, us=2, limit=20 << 20, out=VM):
    return pl.pallas_call(
        kernel,
        name=name,
        out_shape=[pltpu.HBM(*o) if out is HB else jax.ShapeDtypeStruct(*o) for o in outs],
        in_specs=ins,
        out_specs=[out] * len(outs),
        scratch_shapes=scratch,
        compiler_params=pltpu.CompilerParams(vmem_limit_bytes=limit),
        cost_estimate=pl.CostEstimate(flops=us * 10**9, bytes_accessed=us * 3_600_000, transcendentals=0),
    )(*args)


def buffer(planes):
    return pltpu.VMEM((planes, ROWS, NY), f32)


def zero_pads(buf):
    zeros = jnp.zeros((buf.shape[0], PAD, NY), f32)
    buf[:, 0:PAD, :] = zeros
    buf[:, PAD + NX : ROWS, :] = zeros


def band():
    apart = jnp.abs(
        lax.broadcasted_iota(jnp.int32, (NY, NY), 0) - lax.broadcasted_iota(jnp.int32, (NY, NY), 1)
    )
    weights = jnp.zeros((NY, NY), f32)
    for k in range(1, HALF + 1):
        weights = jnp.where(apart == k, 5.0 * stencil_coef[k], weights)
    head = weights.astype(bf16)
    rest = (weights - head.astype(f32)).astype(bf16)
    both = jnp.concatenate([head, rest], axis=1)
    return jnp.concatenate([both, both], axis=0), head


def along(plane, weights):
    both, head = weights
    first = plane.astype(bf16)
    left = plane - first.astype(f32)
    second = left.astype(bf16)
    third = (left - second.astype(f32)).astype(bf16)
    pair = jnp.dot(jnp.concatenate([first, second], axis=1), both, preferred_element_type=f32)
    return 0.2 * (pair[:, :NY] + pair[:, NY:] + jnp.dot(third, head, preferred_element_type=f32))


def rows(row):
    return slice(row, row + CHUNK)


def padded(row):
    return slice(PAD + row, PAD + row + CHUNK)


def group_laps(buf, first, weights, body):
    static = isinstance(first, int)
    parts = [along(buf[first + j, PAD : PAD + NX, :], weights) for j in range(GROUP)]
    for j in range(GROUP):
        at = first + j
        for row in range(0, NX, CHUNK):
            base = PAD + row
            lap = (3.0 * stencil_coef[0]) * buf[at, padded(row), :] + parts[j][row : row + CHUNK]
            for k in range(1, HALF + 1):
                near = buf[at, base + k : base + k + CHUNK, :] + buf[at, base - k : base - k + CHUNK, :]
                for q in (at + k, at - k):
                    if not static or 0 <= q < buf.shape[0]:
                        near = near + buf[q, padded(row), :]
                lap = lap + stencil_coef[k] * near
            body(j, row, lap)


def sweep_own(buf, shift, weights, body):
    @pl.loop(0, DEPTH // GROUP)
    def _(g):
        group_laps(buf, g * GROUP + shift, weights, lambda j, row, lap: body(g * GROUP + j, row, lap))


def sweep_halo(buf, weights, body):
    @pl.loop(0, 2)
    def _(g):
        group_laps(
            buf, HALF + g * (HALF + DEPTH), weights, lambda j, row, lap: body(g * GROUP + j, row, lap)
        )


def sweep_halo_alone(buf, weights, body):
    for g in range(2):
        group_laps(
            buf, g * (HALF + DEPTH), weights, lambda j, row, lap, g=g: body(g * GROUP + j, row, lap)
        )


def sweep_own_alone(buf, weights, body):
    for g in range(DEPTH // GROUP):
        group_laps(buf, g * GROUP, weights, lambda j, row, lap, g=g: body(g * GROUP + j, row, lap))


def fill_side(buf, upper, near, far, own):
    inner = slice(PAD, PAD + NX)
    for j in range(HALF):
        buf[HALF + j, inner, :] = near(j)
        buf[2 * HALF + j if upper else j, inner, :] = far(j)
        buf[j if upper else 2 * HALF + j, inner, :] = own(HALF + j if upper else j)


def side_terms(buf, upper, p, row):
    total = None
    for k in range(1, HALF + 1):
        q = p - HALF + k if upper else 2 * HALF + p - k
        if HALF <= q < 2 * HALF:
            term = stencil_coef[k] * buf[q, padded(row), :]
            total = term if total is None else total + term
    return total


def side_planes(upper):
    return range(HALF, DEPTH) if upper else range(HALF)


def ext_of_halo(h):
    return h + DEPTH * (h // HALF) if isinstance(h, int) else jnp.where(h < HALF, h, h + DEPTH)


def add_cell(ref, plane, row, column, amount):
    lane = lax.broadcasted_iota(jnp.int32, (1, NY), 1)
    old = ref[plane, pl.ds(row, 1), :]
    ref[plane, pl.ds(row, 1), :] = old + jnp.where(lane == column, amount, 0.0)


def parity():
    return lax.rem(lax.axis_index("dom"), 2)


def by_side(par, first, second, body):
    @pl.when(par == 0)
    def _():
        body(second, first)

    @pl.when(par == 1)
    def _():
        body(first, second)


def gather_kernel(slot_hbm, parked_hbm, out_hbm, held, slot_ref, parked_ref, staged, sems, out_sems):
    count, parts = parked_ref.shape[0], 4
    width, lines = parked_ref.shape[1] // parts, 32 // parts
    columns = [pl.ds(width * n, width) for n in range(parts)]
    slots, *copies = fetch(
        [slot_hbm] + [parked_hbm.at[:, c] for c in columns], [slot_ref] + [parked_ref.at[:, c] for c in columns], sems
    )
    slots.wait()
    row = lax.broadcasted_iota(jnp.int32, (count, count), 0)
    pick = jnp.where(row == slot_ref[...], 1.0, 0.0).astype(bf16)
    stores = []
    for n in range(parts):
        copies[n].wait()
        for line in range(lines):
            at = n * width + line * NY
            held[n, pl.ds(line, count, stride=lines), :] = lax.dot_general(
                pick, parked_ref[:, at : at + NY], (((0,), (0,)), ((), ())), preferred_element_type=f32
            )
        staged[n] = held[n].reshape(count, lines, NY).astype(bf16)
        stores.append(pltpu.make_async_copy(staged.at[n], out_hbm.at[:, pl.ds(n * lines, lines)], out_sems.at[n]))
        stores[-1].start()
    for store in stores:
        store.wait()


def adjoint_pack_kernel(now_hbm, next_hbm, speed_hbm, first_ref, second_ref, now_ref, next_ref, speed_ref, sems):
    fields = (now_ref, next_ref, speed_ref)
    for copy in fetch((now_hbm, next_hbm, speed_hbm), fields, sems):
        copy.wait()
    par = parity()
    for out_ref, near in ((first_ref, HALF * (1 - par)), (second_ref, HALF * par)):
        far = HALF - near
        close = near + 3 * (near // HALF)
        for n, ref in enumerate(fields):
            out_ref[pl.ds(HALF * n, HALF)] = ref[pl.ds(near, HALF)].astype(bf16)
            value = ref[pl.ds(close, 1)]
            out_ref[pl.ds(4 * HALF + n, 1)] = (value - value.astype(bf16).astype(f32)).astype(bf16)
        out_ref[pl.ds(3 * HALF, HALF)] = (now_ref[pl.ds(far, HALF)] * speed_ref[pl.ds(far, HALF)]).astype(bf16)


def inject_kernel(depth_ref, row_ref, amount_ref, out_hbm, mark_hbm, table, fields, sems):
    top = lax.axis_index("dom") * DEPTH - HALF
    count = depth_ref.shape[1]
    steps = amount_ref.shape[0]
    local = depth_ref[...] - top
    place = row_ref[...]
    key = jnp.where((local >= 0) & (local < EXT), local * NX + place // NY, -1)
    hit = lax.broadcasted_iota(jnp.int32, (NY, count), 0) == lax.rem(place, NY)
    for k in range(steps):
        amount = amount_ref[k : k + 1, :]
        head = amount.astype(bf16).astype(f32)
        table[0, k * NY : (k + 1) * NY, :] = jnp.where(hit, head, 0.0).astype(bf16)
        table[1, k * NY : (k + 1) * NY, :] = jnp.where(hit, amount - head, 0.0).astype(bf16)
    planes = 2
    cell = lax.broadcasted_iota(jnp.int32, (planes * NX, count), 0)

    def store(g):
        at = pl.ds(g * planes, planes)
        return pltpu.make_async_copy(fields.at[at], out_hbm.at[at], sems.at[g])

    @pl.loop(0, EXT // planes)
    def _(g):
        pick = jnp.where(cell + g * (planes * NX) == key, 1.0, 0.0).astype(bf16)
        field = lax.dot_general(
            pick, table[0], (((1,), (1,)), ((), ())), preferred_element_type=f32
        ) + lax.dot_general(pick, table[1], (((1,), (1,)), ((), ())), preferred_element_type=f32)
        for k in range(steps):
            for j in range(planes):
                fields[g * planes + j, k] = field[j * NX : (j + 1) * NX, k * NY : (k + 1) * NY]
        store(g).start()

    mark = pltpu.make_async_copy(fields.at[0, 0, 0:8], mark_hbm, sems.at[EXT // planes])
    mark.start()
    for g in range(EXT // planes):
        store(g).wait()
    mark.wait()


def send_second(par, buf, far_ref, speed_ext, scale_far, first_ref, second_ref):
    def emit(lower, upper):
        for p in range(DEPTH):
            near_ref, other_ref = (upper, lower) if p >= HALF else (lower, upper)
            for row in range(0, NX, CHUNK):
                total = None
                for k in range(1, HALF + 1):
                    q = p - k if p >= HALF else p + k
                    if (p >= HALF) == (q >= HALF):
                        continue
                    term = stencil_coef[k] * buf[q + HALF, padded(row), :]
                    total = term if total is None else total + term
                fresh = far_ref[p, rows(row), :]
                if scale_far:
                    fresh = fresh * speed_ext[p + HALF, rows(row), :]
                else:
                    total = total * speed_ext[p + HALF, rows(row), :]
                near_ref[p % HALF, rows(row), :] = total.astype(bf16)
                other_ref[HALF + p % HALF, rows(row), :] = fresh.astype(bf16)

    by_side(par, first_ref, second_ref, emit)


def adjoint_side(ref, upper, now_ref, speed_ref, inject_ref, side, buf, weights, store):
    now, after, speed = side
    close = 0 if upper else HALF - 1
    for n, held in enumerate(side):
        held[...] = ref[HALF * n : HALF * n + HALF].astype(f32)
        held[close] = held[close] + ref[4 * HALF + n].astype(f32)
    fill_side(
        buf,
        upper,
        lambda j: now[j] * speed[j],
        lambda j: ref[3 * HALF + j].astype(f32),
        lambda p: now_ref[p] * speed_ref[p],
    )
    first = HALF + DEPTH if upper else 0

    def body(j, row, lap):
        here = now[j, rows(row), :]
        lam = 2.0 * here - after[j, rows(row), :] + lap + inject_ref[first + j, 0, rows(row), :]
        base = 2.0 * lam - here + inject_ref[first + j, 1, rows(row), :]
        store(j, row, lam, base, speed[j, rows(row), :])

    group_laps(buf, HALF, weights, body)


def adjoint_side_kernel(
    now_ref, next_ref, speed_ref, inject_hbm, got_a, out_ref, part_ref, inject_ref, mark_ref,
    own, buf, now_side, next_side, speed_side, sems,
):
    par = parity()
    (copy,) = fetch((inject_hbm.at[:, 0:2],), (inject_ref,), sems)
    mark_ref[...] = jnp.zeros(mark_ref.shape, f32)
    zero_pads(own)
    zero_pads(buf)
    weights = band()
    own[:, PAD : PAD + NX, :] = now_ref[...] * speed_ref[...]

    def alone(p, row, lap):
        part_ref[p, rows(row), :] = 2.0 * now_ref[p, rows(row), :] - next_ref[p, rows(row), :] + lap

    sweep_own_alone(own, weights, alone)
    copy.wait()
    part_ref[...] = part_ref[...] + inject_ref[HALF : HALF + DEPTH, 0]

    def store(j, row, lam, base, speed):
        for n, value in enumerate((lam, base, speed, lam * speed)):
            out_ref[n * HALF + j, rows(row), :] = value

    def one(upper):
        side = (now_side, next_side, speed_side)
        adjoint_side(got_a, upper, now_ref, speed_ref, inject_ref, side, buf, weights, store)
        for p in side_planes(upper):
            for row in range(0, NX, CHUNK):
                part_ref[p, rows(row), :] = part_ref[p, rows(row), :] + side_terms(buf, upper, p, row)

    by_parity(par, one)


def by_parity(par, one):
    @pl.when(par == 0)
    def _():
        one(True)

    @pl.when(par == 1)
    def _():
        one(False)


def adjoint_first_kernel(
    now_ref, speed_ref, inject_ref, side_ref, part_ref, got_b, order_ref,
    first_ref, second_ref, lam_ref, speed_ext, q3_ref,
    buf, now_side, next_side, speed_side,
):
    par = parity()
    zero_pads(buf)
    zero_pads(q3_ref)
    weights = band()
    own = slice(HALF, HALF + DEPTH)
    inner = slice(PAD, PAD + NX)
    speed_ext[own] = speed_ref[...]

    def one(upper_a):
        ext_a, halo_a = (HALF + DEPTH, HALF) if upper_a else (0, 0)
        lam_ref[ext_a : ext_a + HALF] = side_ref[0:HALF]
        lam_ref[EXT + DEPTH + halo_a : EXT + DEPTH + halo_a + HALF] = side_ref[HALF : 2 * HALF]
        speed_ext[ext_a : ext_a + HALF] = side_ref[2 * HALF : 3 * HALF]
        q3_ref[ext_a : ext_a + HALF, inner, :] = side_ref[3 * HALF : 4 * HALF]
        upper = not upper_a
        ext_b, halo_b = (HALF + DEPTH, HALF) if upper else (0, 0)

        def store(j, row, lam, base, speed):
            lam_ref[ext_b + j, rows(row), :] = lam
            lam_ref[EXT + DEPTH + halo_b + j, rows(row), :] = base
            speed_ext[ext_b + j, rows(row), :] = speed
            q3_ref[ext_b + j, padded(row), :] = lam * speed

        side = (now_side, next_side, speed_side)
        adjoint_side(got_b, upper, now_ref, speed_ref, inject_ref, side, buf, weights, store)
        for p in range(DEPTH):
            for row in range(0, NX, CHUNK):
                lam = part_ref[p, rows(row), :]
                if p in side_planes(upper):
                    lam = lam + side_terms(buf, upper, p, row)
                lam_ref[p + HALF, rows(row), :] = lam
                q3_ref[p + HALF, padded(row), :] = lam * speed_ref[p, rows(row), :]

    by_parity(par, one)

    def own_lam2(p, row, lap):
        lam = 2.0 * lam_ref[p + HALF, rows(row), :] - now_ref[p, rows(row), :] + lap
        lam_ref[EXT + p, rows(row), :] = lam + inject_ref[p + HALF, 1, rows(row), :]

    sweep_own(q3_ref, HALF, weights, own_lam2)
    send_second(par, q3_ref, lam_ref.at[EXT : EXT + DEPTH], speed_ext, True, first_ref, second_ref)


def forward_pack_kernel(holder_ref, pieces_ref, order_ref, first_ref, second_ref):
    par = parity()
    per_plane = NX // 32
    for p in range(DEPTH):
        for j in range(per_plane):
            piece = pieces_ref[holder_ref[(DEPTH + p) * per_plane + j]]
            first_ref[HALF + p, 32 * j : 32 * j + 32, :] = piece
            second_ref[HALF + p, 32 * j : 32 * j + 32, :] = piece
    at = HALF * (1 - par)
    for p in range(HALF):
        for j in range(per_plane):
            first_ref[p, 32 * j : 32 * j + 32, :] = pieces_ref[holder_ref[(at + p) * per_plane + j]]
            second_ref[p, 32 * j : 32 * j + 32, :] = pieces_ref[holder_ref[(HALF - at + p) * per_plane + j]]


def source_place(depth_ref, row_ref):
    local = depth_ref[0] - (lax.axis_index("dom") * DEPTH - HALF)
    return local, row_ref[0] // NY, lax.rem(row_ref[0], NY)


def forward_own_kernel(mine_ref, order_ref, own_ref, part_ref, mark_ref):
    mark_ref[...] = jnp.zeros(mark_ref.shape, f32)
    zero_pads(own_ref)
    own_ref[:, PAD : PAD + NX, :] = mine_ref[HALF : HALF + DEPTH].astype(f32)

    def alone(p, row, lap):
        part_ref[p, rows(row), :] = lap

    sweep_own_alone(own_ref, band(), alone)


def forward_first_kernel(
    depth_ref, row_ref, wave_ref, mine_a, mine_b, own_ref, part_ref, got_a, got_b, speed_ext,
    first_ref, second_ref, u1_ref, u2_ref, base_ref, lap0_ref, lap1_ref,
    below, above, prev_own,
):
    par = parity()
    zero_pads(below)
    zero_pads(above)
    zero_pads(u1_ref)
    weights = band()
    inner = slice(PAD, PAD + NX)
    prev_own[pl.ds(HALF * (1 - par), HALF)] = mine_a[0:HALF].astype(f32)
    prev_own[pl.ds(HALF * par, HALF)] = mine_b[0:HALF].astype(f32)

    def halo(lower, upper):
        for ref, buf, is_upper in ((lower, below, False), (upper, above, True)):
            near_at, far_at = (HALF, 2 * HALF) if is_upper else (2 * HALF, HALF)
            fill_side(
                buf,
                is_upper,
                lambda j, ref=ref, at=near_at: ref[at + j].astype(f32),
                lambda j, ref=ref, at=far_at: ref[at + j].astype(f32),
                lambda p: own_ref[p, inner, :],
            )
            first, at = (HALF + DEPTH, HALF) if is_upper else (0, 0)

            def body(j, row, lap, ref=ref, buf=buf, first=first, at=at):
                now = buf[HALF + j, padded(row), :]
                value = 2.0 * now - ref[j, rows(row), :].astype(f32) + speed_ext[first + j, rows(row), :] * lap
                u1_ref[first + j, padded(row), :] = value
                base_ref[at + j, rows(row), :] = 2.0 * value - now

            group_laps(buf, HALF, weights, body)

    by_side(par, got_a, got_b, halo)
    for p in range(DEPTH):
        upper = p >= HALF
        for row in range(0, NX, CHUNK):
            lap = part_ref[p, rows(row), :] + side_terms(above if upper else below, upper, p, row)
            lap0_ref[p, rows(row), :] = lap
            value = 2.0 * own_ref[p, padded(row), :] - prev_own[p, rows(row), :]
            u1_ref[p + HALF, padded(row), :] = value + speed_ext[p + HALF, rows(row), :] * lap
    local, across, along_y = source_place(depth_ref, row_ref)
    outside = ((local >= 0) & (local < HALF)) | ((local >= HALF + DEPTH) & (local < EXT))

    @pl.when((local >= 0) & (local < EXT))
    def _():
        add_cell(u1_ref, local, across + PAD, along_y, wave_ref[0, 0])

    @pl.when(outside)
    def _():
        add_cell(base_ref, jnp.where(local < HALF, local, local - DEPTH), across, along_y, 2.0 * wave_ref[0, 0])

    def own_u2(p, row, lap):
        value = 2.0 * u1_ref[p + HALF, padded(row), :] - own_ref[p, padded(row), :]
        u2_ref[p, rows(row), :] = value + speed_ext[p + HALF, rows(row), :] * lap
        lap1_ref[p, rows(row), :] = lap

    sweep_own(u1_ref, HALF, weights, own_u2)

    @pl.when((local >= HALF) & (local < HALF + DEPTH))
    def _():
        add_cell(u2_ref, local - HALF, across, along_y, wave_ref[0, 1])

    send_second(par, u1_ref, u2_ref, speed_ext, False, first_ref, second_ref)


def middle_kernel(
    depth_ref, row_ref, wave_ref, inject_hbm, got_b, got_a, lam_ref, q3_ref, speed_ext, u1_ref, u2_own, base_ref, lap0_ref, lap1_ref,
    late_ref, u2_ref, grad_ref, lam2_halo, buf2, own_ref, part_ref,
    inject_ref, sems,
):
    par = parity()
    (copy,) = fetch((inject_hbm.at[HALF : HALF + DEPTH, 2],), (inject_ref,), sems)
    zero_pads(buf2)
    weights = band()
    inner = slice(PAD, PAD + NX)

    def alone(h, row, lap):
        lam2_halo[h, rows(row), :] = lam_ref[EXT + DEPTH + h, rows(row), :] + lap

    sweep_halo_alone(q3_ref, weights, alone)
    copy.wait()

    def halo(lower, upper):
        for ref, at, far_at in ((lower, 0, 0), (upper, HALF, WIDE - HALF)):
            ext_at = ext_of_halo(at)
            value = lam2_halo[at : at + HALF] + ref[0:HALF].astype(f32)
            lam2_halo[at : at + HALF] = value
            buf2[ext_at + HALF : ext_at + 2 * HALF, inner, :] = value * speed_ext[ext_at : ext_at + HALF]
            buf2[far_at : far_at + HALF, inner, :] = ref[HALF : 2 * HALF].astype(f32)

    by_side(par, got_a, got_b, halo)
    buf2[2 * HALF : 2 * HALF + DEPTH, inner, :] = lam_ref[EXT : EXT + DEPTH] * speed_ext[HALF : HALF + DEPTH]

    def own_lam1(p, row, lap):
        lam = 2.0 * lam_ref[EXT + p, rows(row), :] - lam_ref[p + HALF, rows(row), :] + lap
        lam = lam + inject_ref[p, rows(row), :]
        late_ref[p, rows(row), :] = lam
        grad_ref[p, rows(row), :] = (
            lam * lap0_ref[p, rows(row), :] + lam_ref[EXT + p, rows(row), :] * lap1_ref[p, rows(row), :]
        )

    sweep_own(buf2, 2 * HALF, weights, own_lam1)

    def halo_u2(h, row, lap):
        e = ext_of_halo(h)
        u2_ref[h, rows(row), :] = base_ref[h, rows(row), :] + speed_ext[e, rows(row), :] * lap

    sweep_halo_alone(u1_ref, weights, halo_u2)
    local, across, along_y = source_place(depth_ref, row_ref)

    @pl.when(((local >= 0) & (local < HALF)) | ((local >= HALF + DEPTH) & (local < EXT)))
    def _():
        add_cell(u2_ref, jnp.where(local < HALF, local, local - DEPTH), across, along_y, wave_ref[0, 1])

    zero_pads(own_ref)
    own_ref[:, inner, :] = u2_own[...]

    def u2_alone(p, row, lap):
        part_ref[p, rows(row), :] = lap

    sweep_own_alone(own_ref, weights, u2_alone)


def adjoint_last_kernel(
    inject_hbm, late_ref, lam_ref, lam2_halo, buf2, speed_ext, order_ref, early_ref, buf1, inject_ref, sems
):
    (copy,) = fetch((inject_hbm.at[:, 2:4],), (inject_ref,), sems)
    zero_pads(buf1)
    weights = band()
    buf1[HALF : HALF + DEPTH, PAD : PAD + NX, :] = late_ref[...] * speed_ext[HALF : HALF + DEPTH]
    copy.wait()

    def halo_lam1(h, row, lap):
        e = ext_of_halo(h)
        lam = 2.0 * lam2_halo[h, rows(row), :] - lam_ref[e, rows(row), :] + lap
        lam = lam + inject_ref[e, 0, rows(row), :]
        buf1[e, padded(row), :] = lam * speed_ext[e, rows(row), :]

    sweep_halo(buf2, weights, halo_lam1)

    def own_lam0(p, row, lap):
        lam = 2.0 * late_ref[p, rows(row), :] - lam_ref[EXT + p, rows(row), :] + lap
        early_ref[p, rows(row), :] = lam + inject_ref[p + HALF, 1, rows(row), :]

    sweep_own(buf1, HALF, weights, own_lam0)


def forward_second_kernel(
    depth_ref, row_ref, wave_ref, got_b, got_a, u1_ref, own_ref, part_ref, u2_halo_ref, speed_ext, lam_ref, lam4_ref,
    grad_ref, keep_ref, send_ref, below, above, buf3, total,
):
    par = parity()
    zero_pads(below)
    zero_pads(above)
    zero_pads(buf3)
    weights = band()
    inner = slice(PAD, PAD + NX)

    def halo(lower, upper):
        for ref, buf, is_upper in ((lower, below, False), (upper, above, True)):
            first, at = (HALF + DEPTH, HALF) if is_upper else (0, 0)
            fill_side(
                buf,
                is_upper,
                lambda j, ref=ref, at=at: u2_halo_ref[at + j] + ref[j].astype(f32),
                lambda j, ref=ref: ref[HALF + j].astype(f32),
                lambda p: own_ref[p, inner, :],
            )

            def body(j, row, lap, buf=buf, first=first):
                value = 2.0 * buf[HALF + j, padded(row), :] - u1_ref[first + j, padded(row), :]
                buf3[first + j, padded(row), :] = value + speed_ext[first + j, rows(row), :] * lap

            group_laps(buf, HALF, weights, body)

    by_side(par, got_a, got_b, halo)
    for p in range(DEPTH):
        upper = p >= HALF
        e = p + HALF
        for row in range(0, NX, CHUNK):
            lap = part_ref[p, rows(row), :] + side_terms(above if upper else below, upper, p, row)
            value = 2.0 * own_ref[p, padded(row), :] - u1_ref[e, padded(row), :]
            buf3[e, padded(row), :] = value + speed_ext[e, rows(row), :] * lap
            total[p, rows(row), :] = grad_ref[p, rows(row), :] + lap * lam_ref[e, rows(row), :]
    local, across, along_y = source_place(depth_ref, row_ref)

    @pl.when((local >= 0) & (local < EXT))
    def _():
        add_cell(buf3, local, across + PAD, along_y, wave_ref[0, 2])

    def to_gradient(p, row, lap):
        value = total[p, rows(row), :] + lap * lam4_ref[p, rows(row), :]
        total[p, rows(row), :] = grad_scale * value

    sweep_own(buf3, HALF, weights, to_gradient)
    shot = lax.axis_index("shot")
    pair, core = shot // 2, lax.rem(shot, 2)
    for n, half in enumerate((pair, 1 - pair)):
        keep_at = pl.multiple_of((half * 2 + core) * 32, 32)
        send_at = pl.multiple_of((half * 2 + 1 - core) * 32, 32)
        keep_ref[n] = total[:, pl.ds(keep_at, 32), :]
        send_ref[n] = total[:, pl.ds(send_at, 32), :]


def per_device(
    parked, parked_slot, holder_list, speed_sq, adjoint_next, adjoint_now,
    wavelet, src_depth, src_row, rec_depth, rec_row, residuals,
):
    peers = lax.axis_size("dom")
    even = [(i, i ^ 1) for i in range(peers)]
    odd = [(i, ((i + 1) ^ 1) - 1) for i in range(1, peers - 1)]

    def swap(a, b):
        far = lax.ppermute(b, "dom", odd)
        return lax.ppermute(a, "dom", even), far

    lam4, lam5 = adjoint_now[0], adjoint_next[0]
    ext = ((EXT, NX, NY), f32)
    slab = ((DEPTH, NX, NY), f32)
    wide = ((EXT, ROWS, NY), f32)

    def planes(count):
        return ((count, NX, NY), bf16)

    mark = ((8, NY), f32)
    (outgoing,) = call(
        gather_kernel, "gather", [HB] * 2, [((64, 32, NY), bf16)],
        [
            pltpu.VMEM((4, 64 * 8, NY), f32), pltpu.VMEM((1, 64), jnp.int32), pltpu.VMEM((64, 4096), bf16),
            pltpu.VMEM((4, 64, 8, NY), bf16), pltpu.SemaphoreType.DMA((5,)), pltpu.SemaphoreType.DMA((4,)),
        ],
        in_hbm(parked_slot[0], parked[0]), out=HB,
    )
    incoming = lax.all_to_all(outgoing, "dom", split_axis=0, concat_axis=0, tiled=True)
    send_a, send_b = call(
        adjoint_pack_kernel, "adjoint_pack", [HB] * 3, [planes(19)] * 2,
        [pltpu.VMEM(*slab)] * 3 + [pltpu.SemaphoreType.DMA((3,))], in_hbm(lam4, lam5, speed_sq),
    )
    got_a, got_b = swap(send_a, send_b)
    count = rec_depth.shape[0]
    steps = residuals.shape[1]
    inject, order = call(
        inject_kernel, "inject", [VM] * 3, [((EXT, steps, NX, NY), f32), mark],
        [
            pltpu.VMEM((2, steps * NY, count), bf16), pltpu.VMEM((EXT, steps, NX, NY), f32),
            pltpu.SemaphoreType.DMA((EXT // 2 + 1,)),
        ],
        (rec_depth.reshape(1, count), rec_row.reshape(1, count), residuals[0]), us=4, out=HB,
    )
    fields = pltpu.VMEM((EXT, 2, NX, NY), f32)
    trio = ((3 * HALF, ROWS, NY), f32)
    four = pltpu.VMEM((HALF, NX, NY), f32)
    own_wide = ((DEPTH, ROWS, NY), f32)
    mine_a, mine_b = call(
        forward_pack_kernel, "forward_pack", [SM, VM, HB], [planes(12)] * 2, [],
        (holder_list.reshape(64), incoming) + in_hbm(order),
    )
    side, part, inject01, order = call(
        adjoint_side_kernel, "adjoint_side", [VM] * 3 + [HB, VM], [((4 * HALF, NX, NY), f32), slab, ((EXT, 2, NX, NY), f32), mark],
        [buffer(DEPTH), pltpu.VMEM(*trio), four, four, four, pltpu.SemaphoreType.DMA((1,))],
        (lam4, lam5, speed_sq) + in_hbm(inject) + (got_a,),
    )
    own0, lap0_part, order = call(
        forward_own_kernel, "forward_own", [VM, VM], [own_wide, slab, mark], [], (mine_a, order),
    )
    send_a, send_b, lam23, speed_ext, q3 = call(
        adjoint_first_kernel, "adjoint_first", [VM] * 7,
        [planes(8)] * 2 + [((EXT + 2 * DEPTH, NX, NY), f32), ext, wide],
        [pltpu.VMEM(*trio), four, four, four],
        (lam4, speed_sq, inject01, side, part, got_b, order),
    )
    back_a, back_b = swap(send_a, send_b)

    got_a, got_b = swap(mine_a, mine_b)
    send_a, send_b, u1, u2, base_u, lap0, lap1 = call(
        forward_first_kernel, "forward_first", [SM] * 3 + [VM] * 7,
        [planes(8)] * 2 + [wide, slab, slab, slab, slab],
        [pltpu.VMEM(*trio), pltpu.VMEM(*trio), pltpu.VMEM(*slab)],
        (src_depth, src_row, wavelet, mine_a, mine_b, own0, lap0_part, got_a, got_b, speed_ext),
    )
    got_a, got_b = swap(send_a, send_b)
    late, u2_halo, grad, lam2_halo, q2, own2, lap2_part = call(
        middle_kernel, "middle", [SM] * 3 + [HB] + [VM] * 10,
        [slab] * 4 + [((WIDE, ROWS, NY), f32), own_wide, slab],
        [pltpu.VMEM(*slab), pltpu.SemaphoreType.DMA((1,))],
        (src_depth, src_row, wavelet) + in_hbm(inject)
        + (back_b, back_a, lam23, q3, speed_ext, u1, u2, base_u, lap0, lap1),
    )
    quarter = ((2, DEPTH, NX // 4, NY), f32)
    keep, send = call(
        forward_second_kernel, "forward_second", [SM] * 3 + [VM] * 10, [quarter] * 2,
        [pltpu.VMEM(*trio), pltpu.VMEM(*trio), buffer(EXT), pltpu.VMEM(*slab)],
        (src_depth, src_row, wavelet, got_b, got_a, u1, own2, lap2_part, u2_halo, speed_ext, lam23, lam4, grad),
    )
    got = lax.ppermute(send, "shot", [(0, 1), (1, 0), (2, 3), (3, 2)])
    part = keep[1] + got[1]
    other = lax.ppermute(part, "shot", [(0, 2), (2, 0), (1, 3), (3, 1)])
    (early,) = call(
        adjoint_last_kernel, "adjoint_last", [HB] + [VM] * 6, [slab],
        [buffer(EXT), fields, pltpu.SemaphoreType.DMA((1,))],
        in_hbm(inject) + (late, lam23, lam2_halo, q2, speed_ext, part),
    )
    gradient = keep[0] + got[0] + other
    return (gradient, late[None], early[None])


def solution(mesh):
    in_specs = (
        P("shot", "dom", None),
        P("shot", "dom", None),
        P("shot", "dom", None),
        P("dom", None, None),
        P("shot", "dom", None, None),
        P("shot", "dom", None, None),
        P("shot", None),
        P("shot"),
        P("shot"),
        P(),
        P(),
        P("shot", None, None),
    )
    out_specs = (P("dom", "shot", None), P("shot", "dom", None, None), P("shot", "dom", None, None))
    return jax.shard_map(
        per_device, mesh=mesh, in_specs=in_specs, out_specs=out_specs, check_vma=False
    )
```

```python
import functools

import jax
import jax.numpy as jnp
from jax import lax
from jax.experimental import pallas as pl
from jax.experimental.pallas import tpu as pltpu
from jax.sharding import PartitionSpec as P

stencil_coef = (-205.0 / 72.0, 8.0 / 5.0, -1.0 / 5.0, 8.0 / 315.0, -1.0 / 560.0)
grad_scale = 0.0625

DEPTH = 8
HALF = 4
EXT = DEPTH + 2 * HALF
WIDE = DEPTH + 4 * HALF
NX = 128
NY = 128
PAD = 8
ROWS = NX + 2 * PAD
CHUNK = 32
GROUP = 4
bf16 = jnp.bfloat16
f32 = jnp.float32

VM = pl.BlockSpec(memory_space=pltpu.VMEM)
SM = pl.BlockSpec(memory_space=pltpu.SMEM)
HB = pl.BlockSpec(memory_space=pltpu.HBM)


def in_hbm(*arrays):
    return tuple(pltpu.with_memory_space_constraint(a, pltpu.HBM) for a in arrays)


def fetch(sources, targets, sems):
    copies = [pltpu.make_async_copy(src, dst, sems.at[n]) for n, (src, dst) in enumerate(zip(sources, targets))]
    for copy in copies:
        copy.start()
    return copies


def call(kernel, name, ins, outs, scratch, args, us=2, limit=20 << 20, out=VM):
    return pl.pallas_call(
        kernel,
        name=name,
        out_shape=[pltpu.HBM(*o) if out is HB else jax.ShapeDtypeStruct(*o) for o in outs],
        in_specs=ins,
        out_specs=[out] * len(outs),
        scratch_shapes=scratch,
        compiler_params=pltpu.CompilerParams(vmem_limit_bytes=limit),
        cost_estimate=pl.CostEstimate(flops=us * 10**9, bytes_accessed=us * 3_600_000, transcendentals=0),
    )(*args)


def buffer(planes):
    return pltpu.VMEM((planes, ROWS, NY), f32)


def zero_pads(buf):
    zeros = jnp.zeros((buf.shape[0], PAD, NY), f32)
    buf[:, 0:PAD, :] = zeros
    buf[:, PAD + NX : ROWS, :] = zeros


def band():
    apart = jnp.abs(
        lax.broadcasted_iota(jnp.int32, (NY, NY), 0) - lax.broadcasted_iota(jnp.int32, (NY, NY), 1)
    )
    weights = jnp.zeros((NY, NY), f32)
    for k in range(1, HALF + 1):
        weights = jnp.where(apart == k, 5.0 * stencil_coef[k], weights)
    head = weights.astype(bf16)
    rest = (weights - head.astype(f32)).astype(bf16)
    both = jnp.concatenate([head, rest], axis=1)
    return jnp.concatenate([both, both], axis=0), head


def along(plane, weights):
    both, head = weights
    first = plane.astype(bf16)
    left = plane - first.astype(f32)
    second = left.astype(bf16)
    third = (left - second.astype(f32)).astype(bf16)
    pair = jnp.dot(jnp.concatenate([first, second], axis=1), both, preferred_element_type=f32)
    return 0.2 * (pair[:, :NY] + pair[:, NY:] + jnp.dot(third, head, preferred_element_type=f32))


def rows(row):
    return slice(row, row + CHUNK)


def padded(row):
    return slice(PAD + row, PAD + row + CHUNK)


def group_laps(buf, first, weights, body):
    static = isinstance(first, int)
    parts = [along(buf[first + j, PAD : PAD + NX, :], weights) for j in range(GROUP)]
    for j in range(GROUP):
        at = first + j
        for row in range(0, NX, CHUNK):
            base = PAD + row
            lap = (3.0 * stencil_coef[0]) * buf[at, padded(row), :] + parts[j][row : row + CHUNK]
            for k in range(1, HALF + 1):
                near = buf[at, base + k : base + k + CHUNK, :] + buf[at, base - k : base - k + CHUNK, :]
                for q in (at + k, at - k):
                    if not static or 0 <= q < buf.shape[0]:
                        near = near + buf[q, padded(row), :]
                lap = lap + stencil_coef[k] * near
            body(j, row, lap)


def sweep_own(buf, shift, weights, body):
    @pl.loop(0, DEPTH // GROUP)
    def _(g):
        group_laps(buf, g * GROUP + shift, weights, lambda j, row, lap: body(g * GROUP + j, row, lap))


def sweep_halo(buf, weights, body):
    @pl.loop(0, 2)
    def _(g):
        group_laps(
            buf, HALF + g * (HALF + DEPTH), weights, lambda j, row, lap: body(g * GROUP + j, row, lap)
        )


def sweep_halo_alone(buf, weights, body):
    for g in range(2):
        group_laps(
            buf, g * (HALF + DEPTH), weights, lambda j, row, lap, g=g: body(g * GROUP + j, row, lap)
        )


def sweep_own_alone(buf, weights, body):
    for g in range(DEPTH // GROUP):
        group_laps(buf, g * GROUP, weights, lambda j, row, lap, g=g: body(g * GROUP + j, row, lap))


def fill_side(buf, upper, near, far, own):
    inner = slice(PAD, PAD + NX)
    for j in range(HALF):
        buf[HALF + j, inner, :] = near(j)
        buf[2 * HALF + j if upper else j, inner, :] = far(j)
        buf[j if upper else 2 * HALF + j, inner, :] = own(HALF + j if upper else j)


def side_terms(buf, upper, p, row):
    total = None
    for k in range(1, HALF + 1):
        q = p - HALF + k if upper else 2 * HALF + p - k
        if HALF <= q < 2 * HALF:
            term = stencil_coef[k] * buf[q, padded(row), :]
            total = term if total is None else total + term
    return total


def side_planes(upper):
    return range(HALF, DEPTH) if upper else range(HALF)


def ext_of_halo(h):
    return h + DEPTH * (h // HALF) if isinstance(h, int) else jnp.where(h < HALF, h, h + DEPTH)


def add_cell(ref, plane, row, column, amount):
    lane = lax.broadcasted_iota(jnp.int32, (1, NY), 1)
    old = ref[plane, pl.ds(row, 1), :]
    ref[plane, pl.ds(row, 1), :] = old + jnp.where(lane == column, amount, 0.0)


def parity():
    return lax.rem(lax.axis_index("dom"), 2)


def by_side(par, first, second, body):
    @pl.when(par == 0)
    def _():
        body(second, first)

    @pl.when(par == 1)
    def _():
        body(first, second)


def gather_kernel(slot_hbm, parked_hbm, out_hbm, held, slot_ref, parked_ref, staged, sems, out_sems):
    count, parts = parked_ref.shape[0], 4
    width, lines = parked_ref.shape[1] // parts, 32 // parts
    columns = [pl.ds(width * n, width) for n in range(parts)]
    slots, *copies = fetch(
        [slot_hbm] + [parked_hbm.at[:, c] for c in columns], [slot_ref] + [parked_ref.at[:, c] for c in columns], sems
    )
    slots.wait()
    row = lax.broadcasted_iota(jnp.int32, (count, count), 0)
    pick = jnp.where(row == slot_ref[...], 1.0, 0.0).astype(bf16)
    stores = []
    for n in range(parts):
        copies[n].wait()
        for line in range(lines):
            at = n * width + line * NY
            held[n, pl.ds(line, count, stride=lines), :] = lax.dot_general(
                pick, parked_ref[:, at : at + NY], (((0,), (0,)), ((), ())), preferred_element_type=f32
            )
        staged[n] = held[n].reshape(count, lines, NY).astype(bf16)
        stores.append(pltpu.make_async_copy(staged.at[n], out_hbm.at[:, pl.ds(n * lines, lines)], out_sems.at[n]))
        stores[-1].start()
    for store in stores:
        store.wait()


def adjoint_pack_kernel(now_hbm, next_hbm, speed_hbm, first_ref, second_ref, now_ref, next_ref, speed_ref, sems):
    fields = (now_ref, next_ref, speed_ref)
    for copy in fetch((now_hbm, next_hbm, speed_hbm), fields, sems):
        copy.wait()
    par = parity()
    for out_ref, near in ((first_ref, HALF * (1 - par)), (second_ref, HALF * par)):
        far = HALF - near
        close = near + 3 * (near // HALF)
        for n, ref in enumerate(fields):
            out_ref[pl.ds(HALF * n, HALF)] = ref[pl.ds(near, HALF)].astype(bf16)
            value = ref[pl.ds(close, 1)]
            out_ref[pl.ds(4 * HALF + n, 1)] = (value - value.astype(bf16).astype(f32)).astype(bf16)
        out_ref[pl.ds(3 * HALF, HALF)] = (now_ref[pl.ds(far, HALF)] * speed_ref[pl.ds(far, HALF)]).astype(bf16)


def inject_kernel(depth_ref, row_ref, amount_ref, out_hbm, mark_hbm, table, fields, sems):
    top = lax.axis_index("dom") * DEPTH - HALF
    count = depth_ref.shape[1]
    steps = amount_ref.shape[0]
    local = depth_ref[...] - top
    place = row_ref[...]
    key = jnp.where((local >= 0) & (local < EXT), local * NX + place // NY, -1)
    hit = lax.broadcasted_iota(jnp.int32, (NY, count), 0) == lax.rem(place, NY)
    for k in range(steps):
        amount = amount_ref[k : k + 1, :]
        head = amount.astype(bf16).astype(f32)
        table[0, k * NY : (k + 1) * NY, :] = jnp.where(hit, head, 0.0).astype(bf16)
        table[1, k * NY : (k + 1) * NY, :] = jnp.where(hit, amount - head, 0.0).astype(bf16)
    planes = 2
    cell = lax.broadcasted_iota(jnp.int32, (planes * NX, count), 0)

    def store(g):
        at = pl.ds(g * planes, planes)
        return pltpu.make_async_copy(fields.at[at], out_hbm.at[at], sems.at[g])

    @pl.loop(0, EXT // planes)
    def _(g):
        pick = jnp.where(cell + g * (planes * NX) == key, 1.0, 0.0).astype(bf16)
        field = lax.dot_general(
            pick, table[0], (((1,), (1,)), ((), ())), preferred_element_type=f32
        ) + lax.dot_general(pick, table[1], (((1,), (1,)), ((), ())), preferred_element_type=f32)
        for k in range(steps):
            for j in range(planes):
                fields[g * planes + j, k] = field[j * NX : (j + 1) * NX, k * NY : (k + 1) * NY]
        store(g).start()

    mark = pltpu.make_async_copy(fields.at[0, 0, 0:8], mark_hbm, sems.at[EXT // planes])
    mark.start()
    for g in range(EXT // planes):
        store(g).wait()
    mark.wait()


def send_second(par, buf, far_ref, speed_ext, scale_far, first_ref, second_ref):
    def emit(lower, upper):
        for p in range(DEPTH):
            near_ref, other_ref = (upper, lower) if p >= HALF else (lower, upper)
            for row in range(0, NX, CHUNK):
                total = None
                for k in range(1, HALF + 1):
                    q = p - k if p >= HALF else p + k
                    if (p >= HALF) == (q >= HALF):
                        continue
                    term = stencil_coef[k] * buf[q + HALF, padded(row), :]
                    total = term if total is None else total + term
                fresh = far_ref[p, rows(row), :]
                if scale_far:
                    fresh = fresh * speed_ext[p + HALF, rows(row), :]
                else:
                    total = total * speed_ext[p + HALF, rows(row), :]
                near_ref[p % HALF, rows(row), :] = total.astype(bf16)
                other_ref[HALF + p % HALF, rows(row), :] = fresh.astype(bf16)

    by_side(par, first_ref, second_ref, emit)


def adjoint_side(ref, upper, now_ref, speed_ref, inject_ref, side, buf, weights, store):
    now, after, speed = side
    close = 0 if upper else HALF - 1
    for n, held in enumerate(side):
        held[...] = ref[HALF * n : HALF * n + HALF].astype(f32)
        held[close] = held[close] + ref[4 * HALF + n].astype(f32)
    fill_side(
        buf,
        upper,
        lambda j: now[j] * speed[j],
        lambda j: ref[3 * HALF + j].astype(f32),
        lambda p: now_ref[p] * speed_ref[p],
    )
    first = HALF + DEPTH if upper else 0

    def body(j, row, lap):
        here = now[j, rows(row), :]
        lam = 2.0 * here - after[j, rows(row), :] + lap + inject_ref[first + j, 0, rows(row), :]
        base = 2.0 * lam - here + inject_ref[first + j, 1, rows(row), :]
        store(j, row, lam, base, speed[j, rows(row), :])

    group_laps(buf, HALF, weights, body)


def adjoint_side_kernel(
    now_ref, next_ref, speed_ref, inject_hbm, got_a, out_ref, part_ref, inject_ref, mark_ref,
    own, buf, now_side, next_side, speed_side, sems,
):
    par = parity()
    (copy,) = fetch((inject_hbm.at[:, 0:3],), (inject_ref,), sems)
    mark_ref[...] = jnp.zeros(mark_ref.shape, f32)
    zero_pads(own)
    zero_pads(buf)
    weights = band()
    own[:, PAD : PAD + NX, :] = now_ref[...] * speed_ref[...]

    def alone(p, row, lap):
        part_ref[p, rows(row), :] = 2.0 * now_ref[p, rows(row), :] - next_ref[p, rows(row), :] + lap

    sweep_own_alone(own, weights, alone)
    copy.wait()
    part_ref[...] = part_ref[...] + inject_ref[HALF : HALF + DEPTH, 0]

    def store(j, row, lam, base, speed):
        for n, value in enumerate((lam, base, speed, lam * speed)):
            out_ref[n * HALF + j, rows(row), :] = value

    def one(upper):
        side = (now_side, next_side, speed_side)
        adjoint_side(got_a, upper, now_ref, speed_ref, inject_ref, side, buf, weights, store)
        for p in side_planes(upper):
            for row in range(0, NX, CHUNK):
                part_ref[p, rows(row), :] = part_ref[p, rows(row), :] + side_terms(buf, upper, p, row)

    by_parity(par, one)


def by_parity(par, one):
    @pl.when(par == 0)
    def _():
        one(True)

    @pl.when(par == 1)
    def _():
        one(False)


def adjoint_first_kernel(
    now_ref, speed_ref, inject_ref, side_ref, part_ref, got_b, order_ref,
    first_ref, second_ref, lam_ref, speed_ext, part1_ref,
    buf, q3_ref, q2_own, now_side, next_side, speed_side,
):
    par = parity()
    zero_pads(buf)
    zero_pads(q2_own)
    zero_pads(q3_ref)
    weights = band()
    own = slice(HALF, HALF + DEPTH)
    inner = slice(PAD, PAD + NX)
    speed_ext[own] = speed_ref[...]

    def one(upper_a):
        ext_a, halo_a = (HALF + DEPTH, HALF) if upper_a else (0, 0)
        lam_ref[ext_a : ext_a + HALF] = side_ref[0:HALF]
        lam_ref[EXT + DEPTH + halo_a : EXT + DEPTH + halo_a + HALF] = side_ref[HALF : 2 * HALF]
        speed_ext[ext_a : ext_a + HALF] = side_ref[2 * HALF : 3 * HALF]
        q3_ref[ext_a : ext_a + HALF, inner, :] = side_ref[3 * HALF : 4 * HALF]
        upper = not upper_a
        ext_b, halo_b = (HALF + DEPTH, HALF) if upper else (0, 0)

        def store(j, row, lam, base, speed):
            lam_ref[ext_b + j, rows(row), :] = lam
            lam_ref[EXT + DEPTH + halo_b + j, rows(row), :] = base
            speed_ext[ext_b + j, rows(row), :] = speed
            q3_ref[ext_b + j, padded(row), :] = lam * speed

        side = (now_side, next_side, speed_side)
        adjoint_side(got_b, upper, now_ref, speed_ref, inject_ref, side, buf, weights, store)
        for p in range(DEPTH):
            for row in range(0, NX, CHUNK):
                lam = part_ref[p, rows(row), :]
                if p in side_planes(upper):
                    lam = lam + side_terms(buf, upper, p, row)
                lam_ref[p + HALF, rows(row), :] = lam
                q3_ref[p + HALF, padded(row), :] = lam * speed_ref[p, rows(row), :]

    by_parity(par, one)

    def own_lam2(p, row, lap):
        lam = 2.0 * lam_ref[p + HALF, rows(row), :] - now_ref[p, rows(row), :] + lap
        lam = lam + inject_ref[p + HALF, 1, rows(row), :]
        lam_ref[EXT + p, rows(row), :] = lam
        q2_own[p, padded(row), :] = lam * speed_ref[p, rows(row), :]

    sweep_own(q3_ref, HALF, weights, own_lam2)

    def halo_lam2(h, row, lap):
        lam_ref[EXT + DEPTH + h, rows(row), :] = lam_ref[EXT + DEPTH + h, rows(row), :] + lap

    sweep_halo_alone(q3_ref, weights, halo_lam2)

    def own_lam1(p, row, lap):
        lam = 2.0 * lam_ref[EXT + p, rows(row), :] - lam_ref[p + HALF, rows(row), :] + lap
        part1_ref[p, rows(row), :] = lam + inject_ref[p + HALF, 2, rows(row), :]

    sweep_own_alone(q2_own, weights, own_lam1)
    send_second(par, q3_ref, lam_ref.at[EXT : EXT + DEPTH], speed_ext, True, first_ref, second_ref)


def forward_pack_kernel(holder_ref, pieces_ref, order_ref, first_ref, second_ref):
    par = parity()
    per_plane = NX // 32
    for p in range(DEPTH):
        for j in range(per_plane):
            piece = pieces_ref[holder_ref[(DEPTH + p) * per_plane + j]]
            first_ref[HALF + p, 32 * j : 32 * j + 32, :] = piece
            second_ref[HALF + p, 32 * j : 32 * j + 32, :] = piece
    at = HALF * (1 - par)
    for p in range(HALF):
        for j in range(per_plane):
            first_ref[p, 32 * j : 32 * j + 32, :] = pieces_ref[holder_ref[(at + p) * per_plane + j]]
            second_ref[p, 32 * j : 32 * j + 32, :] = pieces_ref[holder_ref[(HALF - at + p) * per_plane + j]]


def source_place(depth_ref, row_ref):
    local = depth_ref[0] - (lax.axis_index("dom") * DEPTH - HALF)
    return local, row_ref[0] // NY, lax.rem(row_ref[0], NY)


def forward_own_kernel(mine_ref, order_ref, own_ref, part_ref, mark_ref):
    mark_ref[...] = jnp.zeros(mark_ref.shape, f32)
    zero_pads(own_ref)
    own_ref[:, PAD : PAD + NX, :] = mine_ref[HALF : HALF + DEPTH].astype(f32)

    def alone(p, row, lap):
        part_ref[p, rows(row), :] = lap

    sweep_own_alone(own_ref, band(), alone)


def forward_first_kernel(
    depth_ref, row_ref, wave_ref, mine_a, mine_b, own_ref, part_ref, got_a, got_b, speed_ext, adjoint_a, adjoint_b,
    first_ref, second_ref, u1_ref, u2_ref, base_ref, lap0_ref, lap1_ref,
    below, above, prev_own,
):
    par = parity()
    zero_pads(below)
    zero_pads(above)
    zero_pads(u1_ref)
    weights = band()
    inner = slice(PAD, PAD + NX)
    prev_own[pl.ds(HALF * (1 - par), HALF)] = mine_a[0:HALF].astype(f32)
    prev_own[pl.ds(HALF * par, HALF)] = mine_b[0:HALF].astype(f32)

    def halo(lower, upper):
        for ref, buf, is_upper in ((lower, below, False), (upper, above, True)):
            near_at, far_at = (HALF, 2 * HALF) if is_upper else (2 * HALF, HALF)
            fill_side(
                buf,
                is_upper,
                lambda j, ref=ref, at=near_at: ref[at + j].astype(f32),
                lambda j, ref=ref, at=far_at: ref[at + j].astype(f32),
                lambda p: own_ref[p, inner, :],
            )
            first, at = (HALF + DEPTH, HALF) if is_upper else (0, 0)

            def body(j, row, lap, ref=ref, buf=buf, first=first, at=at):
                now = buf[HALF + j, padded(row), :]
                value = 2.0 * now - ref[j, rows(row), :].astype(f32) + speed_ext[first + j, rows(row), :] * lap
                u1_ref[first + j, padded(row), :] = value
                base_ref[at + j, rows(row), :] = 2.0 * value - now

            group_laps(buf, HALF, weights, body)

    by_side(par, got_a, got_b, halo)
    for p in range(DEPTH):
        upper = p >= HALF
        for row in range(0, NX, CHUNK):
            lap = part_ref[p, rows(row), :] + side_terms(above if upper else below, upper, p, row)
            lap0_ref[p, rows(row), :] = lap
            value = 2.0 * own_ref[p, padded(row), :] - prev_own[p, rows(row), :]
            u1_ref[p + HALF, padded(row), :] = value + speed_ext[p + HALF, rows(row), :] * lap
    local, across, along_y = source_place(depth_ref, row_ref)
    outside = ((local >= 0) & (local < HALF)) | ((local >= HALF + DEPTH) & (local < EXT))

    @pl.when((local >= 0) & (local < EXT))
    def _():
        add_cell(u1_ref, local, across + PAD, along_y, wave_ref[0, 0])

    @pl.when(outside)
    def _():
        add_cell(base_ref, jnp.where(local < HALF, local, local - DEPTH), across, along_y, 2.0 * wave_ref[0, 0])

    def own_u2(p, row, lap):
        value = 2.0 * u1_ref[p + HALF, padded(row), :] - own_ref[p, padded(row), :]
        u2_ref[p, rows(row), :] = value + speed_ext[p + HALF, rows(row), :] * lap
        lap1_ref[p, rows(row), :] = lap

    sweep_own(u1_ref, HALF, weights, own_u2)

    @pl.when((local >= HALF) & (local < HALF + DEPTH))
    def _():
        add_cell(u2_ref, local - HALF, across, along_y, wave_ref[0, 1])

    send_second(par, u1_ref, u2_ref, speed_ext, False, first_ref, second_ref)
    first_ref[2 * HALF : 4 * HALF] = adjoint_a[...]
    second_ref[2 * HALF : 4 * HALF] = adjoint_b[...]


def middle_kernel(
    depth_ref, row_ref, wave_ref, inject_hbm, speed_ext, u1_ref, u2_own, base_ref,
    u2_ref, own_ref, part_ref, inject_ref,
    sems,
):
    (copy,) = fetch((inject_hbm.at[:, 2:4],), (inject_ref,), sems)
    weights = band()

    def halo_u2(h, row, lap):
        e = ext_of_halo(h)
        u2_ref[h, rows(row), :] = base_ref[h, rows(row), :] + speed_ext[e, rows(row), :] * lap

    sweep_halo_alone(u1_ref, weights, halo_u2)
    local, across, along_y = source_place(depth_ref, row_ref)

    @pl.when(((local >= 0) & (local < HALF)) | ((local >= HALF + DEPTH) & (local < EXT)))
    def _():
        add_cell(u2_ref, jnp.where(local < HALF, local, local - DEPTH), across, along_y, wave_ref[0, 1])

    zero_pads(own_ref)
    own_ref[:, PAD : PAD + NX, :] = u2_own[...]

    def u2_alone(p, row, lap):
        part_ref[p, rows(row), :] = lap

    sweep_own_alone(own_ref, weights, u2_alone)
    copy.wait()


def adjoint_last_kernel(
    inject_ref, late_ref, lam_ref, lam2_halo, got_b, got_a, speed_ext, order_ref, early_ref, buf2, buf1
):
    par = parity()
    zero_pads(buf2)
    zero_pads(buf1)
    weights = band()
    inner = slice(PAD, PAD + NX)
    buf1[HALF : HALF + DEPTH, inner, :] = late_ref[...] * speed_ext[HALF : HALF + DEPTH]
    buf2[2 * HALF : 2 * HALF + DEPTH, inner, :] = lam_ref[EXT : EXT + DEPTH] * speed_ext[HALF : HALF + DEPTH]

    def halo(lower, upper):
        for ref, at, far_at in ((lower, 0, 0), (upper, HALF, WIDE - HALF)):
            ext_at = ext_of_halo(at)
            buf2[ext_at + HALF : ext_at + 2 * HALF, inner, :] = (
                lam2_halo[at : at + HALF] * speed_ext[ext_at : ext_at + HALF]
            )
            buf2[far_at : far_at + HALF, inner, :] = ref[3 * HALF : 4 * HALF].astype(f32)

    by_side(par, got_a, got_b, halo)

    def halo_lam1(h, row, lap):
        e = ext_of_halo(h)
        lam = 2.0 * lam2_halo[h, rows(row), :] - lam_ref[e, rows(row), :] + lap
        lam = lam + inject_ref[e, 0, rows(row), :]
        buf1[e, padded(row), :] = lam * speed_ext[e, rows(row), :]

    sweep_halo(buf2, weights, halo_lam1)

    def own_lam0(p, row, lap):
        lam = 2.0 * late_ref[p, rows(row), :] - lam_ref[EXT + p, rows(row), :] + lap
        early_ref[p, rows(row), :] = lam + inject_ref[p + HALF, 1, rows(row), :]

    sweep_own(buf1, HALF, weights, own_lam0)


def forward_second_kernel(
    depth_ref, row_ref, wave_ref, got_b, got_a, u1_ref, own_ref, part_ref, u2_halo_ref, speed_ext, lam_ref, lam4_ref,
    part1_ref, lap0_ref, lap1_ref,
    keep_ref, send_ref, late_ref, lam2_halo,
    below, above, buf3, total, q2_halo,
):
    par = parity()
    zero_pads(below)
    zero_pads(above)
    zero_pads(buf3)
    weights = band()
    inner = slice(PAD, PAD + NX)

    def halo(lower, upper):
        for ref, buf, is_upper in ((lower, below, False), (upper, above, True)):
            first, at = (HALF + DEPTH, HALF) if is_upper else (0, 0)
            fill_side(
                buf,
                is_upper,
                lambda j, ref=ref, at=at: u2_halo_ref[at + j] + ref[j].astype(f32),
                lambda j, ref=ref: ref[HALF + j].astype(f32),
                lambda p: own_ref[p, inner, :],
            )

            value = lam_ref[EXT + DEPTH + at : EXT + DEPTH + at + HALF] + ref[2 * HALF : 3 * HALF].astype(f32)
            lam2_halo[at : at + HALF] = value
            q2_halo[at : at + HALF] = value * speed_ext[first : first + HALF]

            def body(j, row, lap, buf=buf, first=first):
                value = 2.0 * buf[HALF + j, padded(row), :] - u1_ref[first + j, padded(row), :]
                buf3[first + j, padded(row), :] = value + speed_ext[first + j, rows(row), :] * lap

            group_laps(buf, HALF, weights, body)

    by_side(par, got_a, got_b, halo)
    for p in range(DEPTH):
        upper = p >= HALF
        e = p + HALF
        for row in range(0, NX, CHUNK):
            lap = part_ref[p, rows(row), :] + side_terms(above if upper else below, upper, p, row)
            value = 2.0 * own_ref[p, padded(row), :] - u1_ref[e, padded(row), :]
            buf3[e, padded(row), :] = value + speed_ext[e, rows(row), :] * lap
            lam1 = part1_ref[p, rows(row), :]
            for k in range(1, HALF + 1):
                q = p + k - HALF if upper else p - k + HALF
                if (q >= HALF) if upper else (q < HALF):
                    lam1 = lam1 + stencil_coef[k] * q2_halo[q, rows(row), :]
            late_ref[p, rows(row), :] = lam1
            total[p, rows(row), :] = (
                lam1 * lap0_ref[p, rows(row), :]
                + lam_ref[EXT + p, rows(row), :] * lap1_ref[p, rows(row), :]
                + lap * lam_ref[e, rows(row), :]
            )
    local, across, along_y = source_place(depth_ref, row_ref)

    @pl.when((local >= 0) & (local < EXT))
    def _():
        add_cell(buf3, local, across + PAD, along_y, wave_ref[0, 2])

    def to_gradient(p, row, lap):
        value = total[p, rows(row), :] + lap * lam4_ref[p, rows(row), :]
        total[p, rows(row), :] = grad_scale * value

    sweep_own(buf3, HALF, weights, to_gradient)
    shot = lax.axis_index("shot")
    pair, core = shot // 2, lax.rem(shot, 2)
    for n, half in enumerate((pair, 1 - pair)):
        keep_at = pl.multiple_of((half * 2 + core) * 32, 32)
        send_at = pl.multiple_of((half * 2 + 1 - core) * 32, 32)
        keep_ref[n] = total[:, pl.ds(keep_at, 32), :]
        send_ref[n] = total[:, pl.ds(send_at, 32), :]


def per_device(
    parked, parked_slot, holder_list, speed_sq, adjoint_next, adjoint_now,
    wavelet, src_depth, src_row, rec_depth, rec_row, residuals,
):
    peers = lax.axis_size("dom")
    even = [(i, i ^ 1) for i in range(peers)]
    odd = [(i, ((i + 1) ^ 1) - 1) for i in range(1, peers - 1)]

    def swap(a, b):
        far = lax.ppermute(b, "dom", odd)
        return lax.ppermute(a, "dom", even), far

    lam4, lam5 = adjoint_now[0], adjoint_next[0]
    ext = ((EXT, NX, NY), f32)
    slab = ((DEPTH, NX, NY), f32)
    wide = ((EXT, ROWS, NY), f32)

    def planes(count):
        return ((count, NX, NY), bf16)

    mark = ((8, NY), f32)
    (outgoing,) = call(
        gather_kernel, "gather", [HB] * 2, [((64, 32, NY), bf16)],
        [
            pltpu.VMEM((4, 64 * 8, NY), f32), pltpu.VMEM((1, 64), jnp.int32), pltpu.VMEM((64, 4096), bf16),
            pltpu.VMEM((4, 64, 8, NY), bf16), pltpu.SemaphoreType.DMA((5,)), pltpu.SemaphoreType.DMA((4,)),
        ],
        in_hbm(parked_slot[0], parked[0]), out=HB,
    )
    incoming = lax.all_to_all(outgoing, "dom", split_axis=0, concat_axis=0, tiled=True)
    send_a, send_b = call(
        adjoint_pack_kernel, "adjoint_pack", [HB] * 3, [planes(19)] * 2,
        [pltpu.VMEM(*slab)] * 3 + [pltpu.SemaphoreType.DMA((3,))], in_hbm(lam4, lam5, speed_sq),
    )
    got_a, got_b = swap(send_a, send_b)
    count = rec_depth.shape[0]
    steps = residuals.shape[1]
    inject, order = call(
        inject_kernel, "inject", [VM] * 3, [((EXT, steps, NX, NY), f32), mark],
        [
            pltpu.VMEM((2, steps * NY, count), bf16), pltpu.VMEM((EXT, steps, NX, NY), f32),
            pltpu.SemaphoreType.DMA((EXT // 2 + 1,)),
        ],
        (rec_depth.reshape(1, count), rec_row.reshape(1, count), residuals[0]), us=4, out=HB,
    )
    trio = ((3 * HALF, ROWS, NY), f32)
    four = pltpu.VMEM((HALF, NX, NY), f32)
    own_wide = ((DEPTH, ROWS, NY), f32)
    mine_a, mine_b = call(
        forward_pack_kernel, "forward_pack", [SM, VM, HB], [planes(12)] * 2, [],
        (holder_list.reshape(64), incoming) + in_hbm(order),
    )
    side, part, inject01, order = call(
        adjoint_side_kernel, "adjoint_side", [VM] * 3 + [HB, VM], [((4 * HALF, NX, NY), f32), slab, ((EXT, 3, NX, NY), f32), mark],
        [buffer(DEPTH), pltpu.VMEM(*trio), four, four, four, pltpu.SemaphoreType.DMA((1,))],
        (lam4, lam5, speed_sq) + in_hbm(inject) + (got_a,),
    )
    own0, lap0_part, order = call(
        forward_own_kernel, "forward_own", [VM, VM], [own_wide, slab, mark], [], (mine_a, order),
    )
    adjoint_a, adjoint_b, lam23, speed_ext, part1 = call(
        adjoint_first_kernel, "adjoint_first", [VM] * 7,
        [planes(8)] * 2 + [((EXT + 2 * DEPTH, NX, NY), f32), ext, slab],
        [pltpu.VMEM(*trio), buffer(EXT), buffer(DEPTH), four, four, four],
        (lam4, speed_sq, inject01, side, part, got_b, order),
    )
    got_a, got_b = swap(mine_a, mine_b)
    send_a, send_b, u1, u2, base_u, lap0, lap1 = call(
        forward_first_kernel, "forward_first", [SM] * 3 + [VM] * 9,
        [planes(16)] * 2 + [wide, slab, slab, slab, slab],
        [pltpu.VMEM(*trio), pltpu.VMEM(*trio), pltpu.VMEM(*slab)],
        (src_depth, src_row, wavelet, mine_a, mine_b, own0, lap0_part, got_a, got_b, speed_ext, adjoint_a, adjoint_b),
    )
    got_a, got_b = swap(send_a, send_b)
    u2_halo, own2, lap2_part, inject23 = call(
        middle_kernel, "middle", [SM] * 3 + [HB] + [VM] * 4, [slab, own_wide, slab, ((EXT, 2, NX, NY), f32)],
        [pltpu.SemaphoreType.DMA((1,))],
        (src_depth, src_row, wavelet) + in_hbm(inject) + (speed_ext, u1, u2, base_u),
    )
    quarter = ((2, DEPTH, NX // 4, NY), f32)
    keep, send, late, lam2_halo = call(
        forward_second_kernel, "forward_second", [SM] * 3 + [VM] * 12, [quarter] * 2 + [slab] * 2,
        [pltpu.VMEM(*trio), pltpu.VMEM(*trio), buffer(EXT), pltpu.VMEM(*slab), pltpu.VMEM(*slab)],
        (
            src_depth, src_row, wavelet, got_b, got_a, u1, own2, lap2_part, u2_halo, speed_ext, lam23, lam4,
            part1, lap0, lap1,
        ),
    )
    got = lax.ppermute(send, "shot", [(0, 1), (1, 0), (2, 3), (3, 2)])
    part = keep[1] + got[1]
    other = lax.ppermute(part, "shot", [(0, 2), (2, 0), (1, 3), (3, 1)])
    (early,) = call(
        adjoint_last_kernel, "adjoint_last", [VM] * 8, [slab],
        [buffer(WIDE), buffer(EXT)],
        (inject23, late, lam23, lam2_halo, got_b, got_a, speed_ext, part),
    )
    gradient = keep[0] + got[0] + other
    return (gradient, late[None], early[None])


def solution(mesh):
    in_specs = (
        P("shot", "dom", None),
        P("shot", "dom", None),
        P("shot", "dom", None),
        P("dom", None, None),
        P("shot", "dom", None, None),
        P("shot", "dom", None, None),
        P("shot", None),
        P("shot"),
        P("shot"),
        P(),
        P(),
        P("shot", None, None),
    )
    out_specs = (P("dom", "shot", None), P("shot", "dom", None, None), P("shot", "dom", None, None))
    return jax.shard_map(
        per_device, mesh=mesh, in_specs=in_specs, out_specs=out_specs, check_vma=False
    )
```

```python
import functools

import jax
import jax.numpy as jnp
from jax import lax
from jax.experimental import pallas as pl
from jax.experimental.pallas import tpu as pltpu
from jax.sharding import PartitionSpec as P

stencil_coef = (-205.0 / 72.0, 8.0 / 5.0, -1.0 / 5.0, 8.0 / 315.0, -1.0 / 560.0)
grad_scale = 0.0625

DEPTH = 8
HALF = 4
EXT = DEPTH + 2 * HALF
WIDE = DEPTH + 4 * HALF
NX = 128
NY = 128
PAD = 8
ROWS = NX + 2 * PAD
CHUNK = 32
GROUP = 4
bf16 = jnp.bfloat16
f32 = jnp.float32

VM = pl.BlockSpec(memory_space=pltpu.VMEM)
SM = pl.BlockSpec(memory_space=pltpu.SMEM)
HB = pl.BlockSpec(memory_space=pltpu.HBM)


def in_hbm(*arrays):
    return tuple(pltpu.with_memory_space_constraint(a, pltpu.HBM) for a in arrays)


def fetch(sources, targets, sems):
    copies = [pltpu.make_async_copy(src, dst, sems.at[n]) for n, (src, dst) in enumerate(zip(sources, targets))]
    for copy in copies:
        copy.start()
    return copies


def call(kernel, name, ins, outs, scratch, args, us=2, limit=20 << 20, out=VM):
    return pl.pallas_call(
        kernel,
        name=name,
        out_shape=[pltpu.HBM(*o) if out is HB else jax.ShapeDtypeStruct(*o) for o in outs],
        in_specs=ins,
        out_specs=[out] * len(outs),
        scratch_shapes=scratch,
        compiler_params=pltpu.CompilerParams(vmem_limit_bytes=limit),
        cost_estimate=pl.CostEstimate(flops=us * 10**9, bytes_accessed=us * 3_600_000, transcendentals=0),
    )(*args)


def buffer(planes):
    return pltpu.VMEM((planes, ROWS, NY), f32)


def zero_pads(buf):
    zeros = jnp.zeros((buf.shape[0], PAD, NY), f32)
    buf[:, 0:PAD, :] = zeros
    buf[:, PAD + NX : ROWS, :] = zeros


def band():
    apart = jnp.abs(
        lax.broadcasted_iota(jnp.int32, (NY, NY), 0) - lax.broadcasted_iota(jnp.int32, (NY, NY), 1)
    )
    weights = jnp.zeros((NY, NY), f32)
    for k in range(1, HALF + 1):
        weights = jnp.where(apart == k, 5.0 * stencil_coef[k], weights)
    head = weights.astype(bf16)
    rest = (weights - head.astype(f32)).astype(bf16)
    both = jnp.concatenate([head, rest], axis=1)
    return jnp.concatenate([both, both], axis=0), head


def along(plane, weights):
    both, head = weights
    first = plane.astype(bf16)
    left = plane - first.astype(f32)
    second = left.astype(bf16)
    third = (left - second.astype(f32)).astype(bf16)
    pair = jnp.dot(jnp.concatenate([first, second], axis=1), both, preferred_element_type=f32)
    return 0.2 * (pair[:, :NY] + pair[:, NY:] + jnp.dot(third, head, preferred_element_type=f32))


def rows(row):
    return slice(row, row + CHUNK)


def padded(row):
    return slice(PAD + row, PAD + row + CHUNK)


def group_laps(buf, first, weights, body):
    static = isinstance(first, int)
    parts = [along(buf[first + j, PAD : PAD + NX, :], weights) for j in range(GROUP)]
    for j in range(GROUP):
        at = first + j
        for row in range(0, NX, CHUNK):
            base = PAD + row
            lap = (3.0 * stencil_coef[0]) * buf[at, padded(row), :] + parts[j][row : row + CHUNK]
            for k in range(1, HALF + 1):
                near = buf[at, base + k : base + k + CHUNK, :] + buf[at, base - k : base - k + CHUNK, :]
                for q in (at + k, at - k):
                    if not static or 0 <= q < buf.shape[0]:
                        near = near + buf[q, padded(row), :]
                lap = lap + stencil_coef[k] * near
            body(j, row, lap)


def sweep_own(buf, shift, weights, body):
    @pl.loop(0, DEPTH // GROUP)
    def _(g):
        group_laps(buf, g * GROUP + shift, weights, lambda j, row, lap: body(g * GROUP + j, row, lap))


def sweep_halo(buf, weights, body):
    @pl.loop(0, 2)
    def _(g):
        group_laps(
            buf, HALF + g * (HALF + DEPTH), weights, lambda j, row, lap: body(g * GROUP + j, row, lap)
        )


def sweep_halo_alone(buf, weights, body):
    for g in range(2):
        group_laps(
            buf, g * (HALF + DEPTH), weights, lambda j, row, lap, g=g: body(g * GROUP + j, row, lap)
        )


def sweep_own_alone(buf, weights, body):
    for g in range(DEPTH // GROUP):
        group_laps(buf, g * GROUP, weights, lambda j, row, lap, g=g: body(g * GROUP + j, row, lap))


def fill_side(buf, upper, near, far, own):
    inner = slice(PAD, PAD + NX)
    for j in range(HALF):
        buf[HALF + j, inner, :] = near(j)
        buf[2 * HALF + j if upper else j, inner, :] = far(j)
        buf[j if upper else 2 * HALF + j, inner, :] = own(HALF + j if upper else j)


def side_terms(buf, upper, p, row):
    total = None
    for k in range(1, HALF + 1):
        q = p - HALF + k if upper else 2 * HALF + p - k
        if HALF <= q < 2 * HALF:
            term = stencil_coef[k] * buf[q, padded(row), :]
            total = term if total is None else total + term
    return total


def side_planes(upper):
    return range(HALF, DEPTH) if upper else range(HALF)


def ext_of_halo(h):
    return h + DEPTH * (h // HALF) if isinstance(h, int) else jnp.where(h < HALF, h, h + DEPTH)


def add_cell(ref, plane, row, column, amount):
    lane = lax.broadcasted_iota(jnp.int32, (1, NY), 1)
    old = ref[plane, pl.ds(row, 1), :]
    ref[plane, pl.ds(row, 1), :] = old + jnp.where(lane == column, amount, 0.0)


def parity():
    return lax.rem(lax.axis_index("dom"), 2)


def by_side(par, first, second, body):
    @pl.when(par == 0)
    def _():
        body(second, first)

    @pl.when(par == 1)
    def _():
        body(first, second)


def gather_kernel(slot_hbm, parked_hbm, out_hbm, held, slot_ref, parked_ref, staged, sems, out_sems):
    count, parts = parked_ref.shape[0], 4
    width, lines = parked_ref.shape[1] // parts, 32 // parts
    columns = [pl.ds(width * n, width) for n in range(parts)]
    slots, *copies = fetch(
        [slot_hbm] + [parked_hbm.at[:, c] for c in columns], [slot_ref] + [parked_ref.at[:, c] for c in columns], sems
    )
    slots.wait()
    row = lax.broadcasted_iota(jnp.int32, (count, count), 0)
    pick = jnp.where(row == slot_ref[...], 1.0, 0.0).astype(bf16)
    stores = []
    for n in range(parts):
        copies[n].wait()
        for line in range(lines):
            at = n * width + line * NY
            held[n, pl.ds(line, count, stride=lines), :] = lax.dot_general(
                pick, parked_ref[:, at : at + NY], (((0,), (0,)), ((), ())), preferred_element_type=f32
            )
        staged[n] = held[n].reshape(count, lines, NY).astype(bf16)
        stores.append(pltpu.make_async_copy(staged.at[n], out_hbm.at[:, pl.ds(n * lines, lines)], out_sems.at[n]))
        stores[-1].start()
    for store in stores:
        store.wait()


def adjoint_pack_kernel(now_ref, next_ref, speed_ref, first_ref, second_ref):
    fields = (now_ref, next_ref, speed_ref)
    par = parity()
    for out_ref, near in ((first_ref, HALF * (1 - par)), (second_ref, HALF * par)):
        far = HALF - near
        close = near + 3 * (near // HALF)
        for n, ref in enumerate(fields):
            out_ref[pl.ds(HALF * n, HALF)] = ref[pl.ds(near, HALF)].astype(bf16)
            value = ref[pl.ds(close, 1)]
            out_ref[pl.ds(4 * HALF + n, 1)] = (value - value.astype(bf16).astype(f32)).astype(bf16)
        out_ref[pl.ds(3 * HALF, HALF)] = (now_ref[pl.ds(far, HALF)] * speed_ref[pl.ds(far, HALF)]).astype(bf16)


def inject_kernel(depth_ref, row_ref, amount_ref, out_hbm, mark_hbm, table, fields, sems):
    top = lax.axis_index("dom") * DEPTH - HALF
    count = depth_ref.shape[1]
    steps = amount_ref.shape[0]
    local = depth_ref[...] - top
    place = row_ref[...]
    key = jnp.where((local >= 0) & (local < EXT), local * NX + place // NY, -1)
    hit = lax.broadcasted_iota(jnp.int32, (NY, count), 0) == lax.rem(place, NY)
    for k in range(steps):
        amount = amount_ref[k : k + 1, :]
        head = amount.astype(bf16).astype(f32)
        table[0, k * NY : (k + 1) * NY, :] = jnp.where(hit, head, 0.0).astype(bf16)
        table[1, k * NY : (k + 1) * NY, :] = jnp.where(hit, amount - head, 0.0).astype(bf16)
    planes = 2
    cell = lax.broadcasted_iota(jnp.int32, (planes * NX, count), 0)

    def store(g):
        at = pl.ds(g * planes, planes)
        return pltpu.make_async_copy(fields.at[at], out_hbm.at[at], sems.at[g])

    @pl.loop(0, EXT // planes)
    def _(g):
        pick = jnp.where(cell + g * (planes * NX) == key, 1.0, 0.0).astype(bf16)
        field = lax.dot_general(
            pick, table[0], (((1,), (1,)), ((), ())), preferred_element_type=f32
        ) + lax.dot_general(pick, table[1], (((1,), (1,)), ((), ())), preferred_element_type=f32)
        for k in range(steps):
            for j in range(planes):
                fields[g * planes + j, k] = field[j * NX : (j + 1) * NX, k * NY : (k + 1) * NY]
        store(g).start()

    mark = pltpu.make_async_copy(fields.at[0, 0, 0:8], mark_hbm, sems.at[EXT // planes])
    mark.start()
    for g in range(EXT // planes):
        store(g).wait()
    mark.wait()


def send_second(par, buf, far_ref, speed_ext, scale_far, first_ref, second_ref):
    def emit(lower, upper):
        for p in range(DEPTH):
            near_ref, other_ref = (upper, lower) if p >= HALF else (lower, upper)
            for row in range(0, NX, CHUNK):
                total = None
                for k in range(1, HALF + 1):
                    q = p - k if p >= HALF else p + k
                    if (p >= HALF) == (q >= HALF):
                        continue
                    term = stencil_coef[k] * buf[q + HALF, padded(row), :]
                    total = term if total is None else total + term
                fresh = far_ref[p, rows(row), :]
                if scale_far:
                    fresh = fresh * speed_ext[p + HALF, rows(row), :]
                else:
                    total = total * speed_ext[p + HALF, rows(row), :]
                near_ref[p % HALF, rows(row), :] = total.astype(bf16)
                other_ref[HALF + p % HALF, rows(row), :] = fresh.astype(bf16)

    by_side(par, first_ref, second_ref, emit)


def adjoint_side(ref, upper, now_ref, speed_ref, inject_ref, side, buf, weights, store):
    now, after, speed = side
    close = 0 if upper else HALF - 1
    for n, held in enumerate(side):
        held[...] = ref[HALF * n : HALF * n + HALF].astype(f32)
        held[close] = held[close] + ref[4 * HALF + n].astype(f32)
    fill_side(
        buf,
        upper,
        lambda j: now[j] * speed[j],
        lambda j: ref[3 * HALF + j].astype(f32),
        lambda p: now_ref[p] * speed_ref[p],
    )
    first = HALF + DEPTH if upper else 0

    def body(j, row, lap):
        here = now[j, rows(row), :]
        lam = 2.0 * here - after[j, rows(row), :] + lap + inject_ref[first + j, 0, rows(row), :]
        base = 2.0 * lam - here + inject_ref[first + j, 1, rows(row), :]
        store(j, row, lam, base, speed[j, rows(row), :])

    group_laps(buf, HALF, weights, body)


def adjoint_side_kernel(
    now_ref, next_ref, speed_ref, inject_hbm, got_a, out_ref, part_ref, inject_ref, mark_ref,
    own, buf, now_side, next_side, speed_side, sems,
):
    par = parity()
    (copy,) = fetch((inject_hbm.at[:, 0:2],), (inject_ref,), sems)
    mark_ref[...] = jnp.zeros(mark_ref.shape, f32)
    zero_pads(own)
    zero_pads(buf)
    weights = band()
    own[:, PAD : PAD + NX, :] = now_ref[...] * speed_ref[...]

    def alone(p, row, lap):
        part_ref[p, rows(row), :] = 2.0 * now_ref[p, rows(row), :] - next_ref[p, rows(row), :] + lap

    sweep_own_alone(own, weights, alone)
    copy.wait()
    part_ref[...] = part_ref[...] + inject_ref[HALF : HALF + DEPTH, 0]

    def store(j, row, lam, base, speed):
        for n, value in enumerate((lam, base, speed, lam * speed)):
            out_ref[n * HALF + j, rows(row), :] = value

    def one(upper):
        side = (now_side, next_side, speed_side)
        adjoint_side(got_a, upper, now_ref, speed_ref, inject_ref, side, buf, weights, store)
        for p in side_planes(upper):
            for row in range(0, NX, CHUNK):
                part_ref[p, rows(row), :] = part_ref[p, rows(row), :] + side_terms(buf, upper, p, row)

    by_parity(par, one)


def by_parity(par, one):
    @pl.when(par == 0)
    def _():
        one(True)

    @pl.when(par == 1)
    def _():
        one(False)


def adjoint_first_kernel(
    now_ref, speed_ref, inject_ref, side_ref, part_ref, got_b, order_ref,
    first_ref, second_ref, lam_ref, speed_ext, q3_ref,
    buf, now_side, next_side, speed_side,
):
    par = parity()
    zero_pads(buf)
    zero_pads(q3_ref)
    weights = band()
    own = slice(HALF, HALF + DEPTH)
    inner = slice(PAD, PAD + NX)
    speed_ext[own] = speed_ref[...]

    def one(upper_a):
        ext_a, halo_a = (HALF + DEPTH, HALF) if upper_a else (0, 0)
        lam_ref[ext_a : ext_a + HALF] = side_ref[0:HALF]
        lam_ref[EXT + DEPTH + halo_a : EXT + DEPTH + halo_a + HALF] = side_ref[HALF : 2 * HALF]
        speed_ext[ext_a : ext_a + HALF] = side_ref[2 * HALF : 3 * HALF]
        q3_ref[ext_a : ext_a + HALF, inner, :] = side_ref[3 * HALF : 4 * HALF]
        upper = not upper_a
        ext_b, halo_b = (HALF + DEPTH, HALF) if upper else (0, 0)

        def store(j, row, lam, base, speed):
            lam_ref[ext_b + j, rows(row), :] = lam
            lam_ref[EXT + DEPTH + halo_b + j, rows(row), :] = base
            speed_ext[ext_b + j, rows(row), :] = speed
            q3_ref[ext_b + j, padded(row), :] = lam * speed

        side = (now_side, next_side, speed_side)
        adjoint_side(got_b, upper, now_ref, speed_ref, inject_ref, side, buf, weights, store)
        for p in range(DEPTH):
            for row in range(0, NX, CHUNK):
                lam = part_ref[p, rows(row), :]
                if p in side_planes(upper):
                    lam = lam + side_terms(buf, upper, p, row)
                lam_ref[p + HALF, rows(row), :] = lam
                q3_ref[p + HALF, padded(row), :] = lam * speed_ref[p, rows(row), :]

    by_parity(par, one)

    def own_lam2(p, row, lap):
        lam = 2.0 * lam_ref[p + HALF, rows(row), :] - now_ref[p, rows(row), :] + lap
        lam_ref[EXT + p, rows(row), :] = lam + inject_ref[p + HALF, 1, rows(row), :]

    sweep_own(q3_ref, HALF, weights, own_lam2)
    send_second(par, q3_ref, lam_ref.at[EXT : EXT + DEPTH], speed_ext, True, first_ref, second_ref)


def forward_pack_kernel(holder_ref, pieces_ref, order_ref, first_ref, second_ref):
    par = parity()
    per_plane = NX // 32
    for p in range(DEPTH):
        for j in range(per_plane):
            piece = pieces_ref[holder_ref[(DEPTH + p) * per_plane + j]]
            first_ref[HALF + p, 32 * j : 32 * j + 32, :] = piece
            second_ref[HALF + p, 32 * j : 32 * j + 32, :] = piece
    at = HALF * (1 - par)
    for p in range(HALF):
        for j in range(per_plane):
            first_ref[p, 32 * j : 32 * j + 32, :] = pieces_ref[holder_ref[(at + p) * per_plane + j]]
            second_ref[p, 32 * j : 32 * j + 32, :] = pieces_ref[holder_ref[(HALF - at + p) * per_plane + j]]


def source_place(depth_ref, row_ref):
    local = depth_ref[0] - (lax.axis_index("dom") * DEPTH - HALF)
    return local, row_ref[0] // NY, lax.rem(row_ref[0], NY)


def forward_own_kernel(mine_ref, order_ref, own_ref, part_ref, mark_ref):
    mark_ref[...] = jnp.zeros(mark_ref.shape, f32)
    zero_pads(own_ref)
    own_ref[:, PAD : PAD + NX, :] = mine_ref[HALF : HALF + DEPTH].astype(f32)

    def alone(p, row, lap):
        part_ref[p, rows(row), :] = lap

    sweep_own_alone(own_ref, band(), alone)


def forward_first_kernel(
    depth_ref, row_ref, wave_ref, mine_a, mine_b, own_ref, part_ref, got_a, got_b, speed_ext,
    first_ref, second_ref, u1_ref, u2_ref, base_ref, lap0_ref, lap1_ref,
    below, above, prev_own,
):
    par = parity()
    zero_pads(below)
    zero_pads(above)
    zero_pads(u1_ref)
    weights = band()
    inner = slice(PAD, PAD + NX)
    prev_own[pl.ds(HALF * (1 - par), HALF)] = mine_a[0:HALF].astype(f32)
    prev_own[pl.ds(HALF * par, HALF)] = mine_b[0:HALF].astype(f32)

    def halo(lower, upper):
        for ref, buf, is_upper in ((lower, below, False), (upper, above, True)):
            near_at, far_at = (HALF, 2 * HALF) if is_upper else (2 * HALF, HALF)
            fill_side(
                buf,
                is_upper,
                lambda j, ref=ref, at=near_at: ref[at + j].astype(f32),
                lambda j, ref=ref, at=far_at: ref[at + j].astype(f32),
                lambda p: own_ref[p, inner, :],
            )
            first, at = (HALF + DEPTH, HALF) if is_upper else (0, 0)

            def body(j, row, lap, ref=ref, buf=buf, first=first, at=at):
                now = buf[HALF + j, padded(row), :]
                value = 2.0 * now - ref[j, rows(row), :].astype(f32) + speed_ext[first + j, rows(row), :] * lap
                u1_ref[first + j, padded(row), :] = value
                base_ref[at + j, rows(row), :] = 2.0 * value - now

            group_laps(buf, HALF, weights, body)

    by_side(par, got_a, got_b, halo)
    for p in range(DEPTH):
        upper = p >= HALF
        for row in range(0, NX, CHUNK):
            lap = part_ref[p, rows(row), :] + side_terms(above if upper else below, upper, p, row)
            lap0_ref[p, rows(row), :] = lap
            value = 2.0 * own_ref[p, padded(row), :] - prev_own[p, rows(row), :]
            u1_ref[p + HALF, padded(row), :] = value + speed_ext[p + HALF, rows(row), :] * lap
    local, across, along_y = source_place(depth_ref, row_ref)
    outside = ((local >= 0) & (local < HALF)) | ((local >= HALF + DEPTH) & (local < EXT))

    @pl.when((local >= 0) & (local < EXT))
    def _():
        add_cell(u1_ref, local, across + PAD, along_y, wave_ref[0, 0])

    @pl.when(outside)
    def _():
        add_cell(base_ref, jnp.where(local < HALF, local, local - DEPTH), across, along_y, 2.0 * wave_ref[0, 0])

    def own_u2(p, row, lap):
        value = 2.0 * u1_ref[p + HALF, padded(row), :] - own_ref[p, padded(row), :]
        u2_ref[p, rows(row), :] = value + speed_ext[p + HALF, rows(row), :] * lap
        lap1_ref[p, rows(row), :] = lap

    sweep_own(u1_ref, HALF, weights, own_u2)

    @pl.when((local >= HALF) & (local < HALF + DEPTH))
    def _():
        add_cell(u2_ref, local - HALF, across, along_y, wave_ref[0, 1])

    send_second(par, u1_ref, u2_ref, speed_ext, False, first_ref, second_ref)


def middle_kernel(
    depth_ref, row_ref, wave_ref, inject_hbm, got_b, got_a, lam_ref, q3_ref, speed_ext, u1_ref, u2_own, base_ref, lap0_ref, lap1_ref,
    late_ref, u2_ref, grad_ref, lam2_halo, buf2, own_ref, part_ref,
    inject_ref, sems,
):
    par = parity()
    (copy,) = fetch((inject_hbm.at[HALF : HALF + DEPTH, 2],), (inject_ref,), sems)
    zero_pads(buf2)
    weights = band()
    inner = slice(PAD, PAD + NX)

    def alone(h, row, lap):
        lam2_halo[h, rows(row), :] = lam_ref[EXT + DEPTH + h, rows(row), :] + lap

    sweep_halo_alone(q3_ref, weights, alone)
    copy.wait()

    def halo(lower, upper):
        for ref, at, far_at in ((lower, 0, 0), (upper, HALF, WIDE - HALF)):
            ext_at = ext_of_halo(at)
            value = lam2_halo[at : at + HALF] + ref[0:HALF].astype(f32)
            lam2_halo[at : at + HALF] = value
            buf2[ext_at + HALF : ext_at + 2 * HALF, inner, :] = value * speed_ext[ext_at : ext_at + HALF]
            buf2[far_at : far_at + HALF, inner, :] = ref[HALF : 2 * HALF].astype(f32)

    by_side(par, got_a, got_b, halo)
    buf2[2 * HALF : 2 * HALF + DEPTH, inner, :] = lam_ref[EXT : EXT + DEPTH] * speed_ext[HALF : HALF + DEPTH]

    def own_lam1(p, row, lap):
        lam = 2.0 * lam_ref[EXT + p, rows(row), :] - lam_ref[p + HALF, rows(row), :] + lap
        lam = lam + inject_ref[p, rows(row), :]
        late_ref[p, rows(row), :] = lam
        grad_ref[p, rows(row), :] = (
            lam * lap0_ref[p, rows(row), :] + lam_ref[EXT + p, rows(row), :] * lap1_ref[p, rows(row), :]
        )

    sweep_own(buf2, 2 * HALF, weights, own_lam1)

    def halo_u2(h, row, lap):
        e = ext_of_halo(h)
        u2_ref[h, rows(row), :] = base_ref[h, rows(row), :] + speed_ext[e, rows(row), :] * lap

    sweep_halo_alone(u1_ref, weights, halo_u2)
    local, across, along_y = source_place(depth_ref, row_ref)

    @pl.when(((local >= 0) & (local < HALF)) | ((local >= HALF + DEPTH) & (local < EXT)))
    def _():
        add_cell(u2_ref, jnp.where(local < HALF, local, local - DEPTH), across, along_y, wave_ref[0, 1])

    zero_pads(own_ref)
    own_ref[:, inner, :] = u2_own[...]

    def u2_alone(p, row, lap):
        part_ref[p, rows(row), :] = lap

    sweep_own_alone(own_ref, weights, u2_alone)


def adjoint_last_kernel(
    inject_hbm, late_ref, lam_ref, lam2_halo, buf2, speed_ext, order_ref, early_ref, buf1, inject_ref, sems
):
    (copy,) = fetch((inject_hbm.at[:, 2:4],), (inject_ref,), sems)
    zero_pads(buf1)
    weights = band()
    buf1[HALF : HALF + DEPTH, PAD : PAD + NX, :] = late_ref[...] * speed_ext[HALF : HALF + DEPTH]
    copy.wait()

    def halo_lam1(h, row, lap):
        e = ext_of_halo(h)
        lam = 2.0 * lam2_halo[h, rows(row), :] - lam_ref[e, rows(row), :] + lap
        lam = lam + inject_ref[e, 0, rows(row), :]
        buf1[e, padded(row), :] = lam * speed_ext[e, rows(row), :]

    sweep_halo(buf2, weights, halo_lam1)

    def own_lam0(p, row, lap):
        lam = 2.0 * late_ref[p, rows(row), :] - lam_ref[EXT + p, rows(row), :] + lap
        early_ref[p, rows(row), :] = lam + inject_ref[p + HALF, 1, rows(row), :]

    sweep_own(buf1, HALF, weights, own_lam0)


def forward_second_kernel(
    depth_ref, row_ref, wave_ref, got_b, got_a, u1_ref, own_ref, part_ref, u2_halo_ref, speed_ext, lam_ref, lam4_ref,
    grad_ref, keep_ref, send_ref, below, above, buf3, total,
):
    par = parity()
    zero_pads(below)
    zero_pads(above)
    zero_pads(buf3)
    weights = band()
    inner = slice(PAD, PAD + NX)

    def halo(lower, upper):
        for ref, buf, is_upper in ((lower, below, False), (upper, above, True)):
            first, at = (HALF + DEPTH, HALF) if is_upper else (0, 0)
            fill_side(
                buf,
                is_upper,
                lambda j, ref=ref, at=at: u2_halo_ref[at + j] + ref[j].astype(f32),
                lambda j, ref=ref: ref[HALF + j].astype(f32),
                lambda p: own_ref[p, inner, :],
            )

            def body(j, row, lap, buf=buf, first=first):
                value = 2.0 * buf[HALF + j, padded(row), :] - u1_ref[first + j, padded(row), :]
                buf3[first + j, padded(row), :] = value + speed_ext[first + j, rows(row), :] * lap

            group_laps(buf, HALF, weights, body)

    by_side(par, got_a, got_b, halo)
    for p in range(DEPTH):
        upper = p >= HALF
        e = p + HALF
        for row in range(0, NX, CHUNK):
            lap = part_ref[p, rows(row), :] + side_terms(above if upper else below, upper, p, row)
            value = 2.0 * own_ref[p, padded(row), :] - u1_ref[e, padded(row), :]
            buf3[e, padded(row), :] = value + speed_ext[e, rows(row), :] * lap
            total[p, rows(row), :] = grad_ref[p, rows(row), :] + lap * lam_ref[e, rows(row), :]
    local, across, along_y = source_place(depth_ref, row_ref)

    @pl.when((local >= 0) & (local < EXT))
    def _():
        add_cell(buf3, local, across + PAD, along_y, wave_ref[0, 2])

    def to_gradient(p, row, lap):
        value = total[p, rows(row), :] + lap * lam4_ref[p, rows(row), :]
        total[p, rows(row), :] = grad_scale * value

    sweep_own(buf3, HALF, weights, to_gradient)
    shot = lax.axis_index("shot")
    pair, core = shot // 2, lax.rem(shot, 2)
    for n, half in enumerate((pair, 1 - pair)):
        keep_at = pl.multiple_of((half * 2 + core) * 32, 32)
        send_at = pl.multiple_of((half * 2 + 1 - core) * 32, 32)
        keep_ref[n] = total[:, pl.ds(keep_at, 32), :]
        send_ref[n] = total[:, pl.ds(send_at, 32), :]


def per_device(
    parked, parked_slot, holder_list, speed_sq, adjoint_next, adjoint_now,
    wavelet, src_depth, src_row, rec_depth, rec_row, residuals,
):
    peers = lax.axis_size("dom")
    even = [(i, i ^ 1) for i in range(peers)]
    odd = [(i, ((i + 1) ^ 1) - 1) for i in range(1, peers - 1)]

    def swap(a, b):
        far = lax.ppermute(b, "dom", odd)
        return lax.ppermute(a, "dom", even), far

    lam4, lam5 = adjoint_now[0], adjoint_next[0]
    ext = ((EXT, NX, NY), f32)
    slab = ((DEPTH, NX, NY), f32)
    wide = ((EXT, ROWS, NY), f32)

    def planes(count):
        return ((count, NX, NY), bf16)

    mark = ((8, NY), f32)
    (outgoing,) = call(
        gather_kernel, "gather", [HB] * 2, [((64, 32, NY), bf16)],
        [
            pltpu.VMEM((4, 64 * 8, NY), f32), pltpu.VMEM((1, 64), jnp.int32), pltpu.VMEM((64, 4096), bf16),
            pltpu.VMEM((4, 64, 8, NY), bf16), pltpu.SemaphoreType.DMA((5,)), pltpu.SemaphoreType.DMA((4,)),
        ],
        in_hbm(parked_slot[0], parked[0]), out=HB,
    )
    incoming = lax.all_to_all(outgoing, "dom", split_axis=0, concat_axis=0, tiled=True)
    send_a, send_b = call(
        adjoint_pack_kernel, "adjoint_pack", [VM] * 3, [planes(19)] * 2, [], (lam4, lam5, speed_sq),
    )
    got_a, got_b = swap(send_a, send_b)
    count = rec_depth.shape[0]
    steps = residuals.shape[1]
    inject, order = call(
        inject_kernel, "inject", [VM] * 3, [((EXT, steps, NX, NY), f32), mark],
        [
            pltpu.VMEM((2, steps * NY, count), bf16), pltpu.VMEM((EXT, steps, NX, NY), f32),
            pltpu.SemaphoreType.DMA((EXT // 2 + 1,)),
        ],
        (rec_depth.reshape(1, count), rec_row.reshape(1, count), residuals[0]), us=4, out=HB,
    )
    fields = pltpu.VMEM((EXT, 2, NX, NY), f32)
    trio = ((3 * HALF, ROWS, NY), f32)
    four = pltpu.VMEM((HALF, NX, NY), f32)
    own_wide = ((DEPTH, ROWS, NY), f32)
    mine_a, mine_b = call(
        forward_pack_kernel, "forward_pack", [SM, VM, HB], [planes(12)] * 2, [],
        (holder_list.reshape(64), incoming) + in_hbm(order),
    )
    side, part, inject01, order = call(
        adjoint_side_kernel, "adjoint_side", [VM] * 3 + [HB, VM], [((4 * HALF, NX, NY), f32), slab, ((EXT, 2, NX, NY), f32), mark],
        [buffer(DEPTH), pltpu.VMEM(*trio), four, four, four, pltpu.SemaphoreType.DMA((1,))],
        (lam4, lam5, speed_sq) + in_hbm(inject) + (got_a,),
    )
    own0, lap0_part, order = call(
        forward_own_kernel, "forward_own", [VM, VM], [own_wide, slab, mark], [], (mine_a, order),
    )
    send_a, send_b, lam23, speed_ext, q3 = call(
        adjoint_first_kernel, "adjoint_first", [VM] * 7,
        [planes(8)] * 2 + [((EXT + 2 * DEPTH, NX, NY), f32), ext, wide],
        [pltpu.VMEM(*trio), four, four, four],
        (lam4, speed_sq, inject01, side, part, got_b, order),
    )
    back_a, back_b = swap(send_a, send_b)

    got_a, got_b = swap(mine_a, mine_b)
    send_a, send_b, u1, u2, base_u, lap0, lap1 = call(
        forward_first_kernel, "forward_first", [SM] * 3 + [VM] * 7,
        [planes(8)] * 2 + [wide, slab, slab, slab, slab],
        [pltpu.VMEM(*trio), pltpu.VMEM(*trio), pltpu.VMEM(*slab)],
        (src_depth, src_row, wavelet, mine_a, mine_b, own0, lap0_part, got_a, got_b, speed_ext),
    )
    got_a, got_b = swap(send_a, send_b)
    late, u2_halo, grad, lam2_halo, q2, own2, lap2_part = call(
        middle_kernel, "middle", [SM] * 3 + [HB] + [VM] * 10,
        [slab] * 4 + [((WIDE, ROWS, NY), f32), own_wide, slab],
        [pltpu.VMEM(*slab), pltpu.SemaphoreType.DMA((1,))],
        (src_depth, src_row, wavelet) + in_hbm(inject)
        + (back_b, back_a, lam23, q3, speed_ext, u1, u2, base_u, lap0, lap1),
    )
    quarter = ((2, DEPTH, NX // 4, NY), f32)
    keep, send = call(
        forward_second_kernel, "forward_second", [SM] * 3 + [VM] * 10, [quarter] * 2,
        [pltpu.VMEM(*trio), pltpu.VMEM(*trio), buffer(EXT), pltpu.VMEM(*slab)],
        (src_depth, src_row, wavelet, got_b, got_a, u1, own2, lap2_part, u2_halo, speed_ext, lam23, lam4, grad),
    )
    got = lax.ppermute(send, "shot", [(0, 1), (1, 0), (2, 3), (3, 2)])
    part = keep[1] + got[1]
    other = lax.ppermute(part, "shot", [(0, 2), (2, 0), (1, 3), (3, 1)])
    (early,) = call(
        adjoint_last_kernel, "adjoint_last", [HB] + [VM] * 6, [slab],
        [buffer(EXT), fields, pltpu.SemaphoreType.DMA((1,))],
        in_hbm(inject) + (late, lam23, lam2_halo, q2, speed_ext, part),
    )
    gradient = keep[0] + got[0] + other
    return (gradient, late[None], early[None])


def solution(mesh):
    in_specs = (
        P("shot", "dom", None),
        P("shot", "dom", None),
        P("shot", "dom", None),
        P("dom", None, None),
        P("shot", "dom", None, None),
        P("shot", "dom", None, None),
        P("shot", None),
        P("shot"),
        P("shot"),
        P(),
        P(),
        P("shot", None, None),
    )
    out_specs = (P("dom", "shot", None), P("shot", "dom", None, None), P("shot", "dom", None, None))
    return jax.shard_map(
        per_device, mesh=mesh, in_specs=in_specs, out_specs=out_specs, check_vma=False
    )
```
